32 devices in a mesh: dp: 8 (over y, x, core), head: 4 (over z).
Axes of the slice: x: 2, y: 2, z: 4, core: 2. Of those that a mesh axis runs over, the one named last changes fastest.
Arguments:
- layer_entries: bfloat16 [8192, 1024], P(('dp', 'head')), may hold values from -6 to 6
- triple_projection_matrix: bfloat16 [1024, 3072], P('dp', 'head'), may hold values from -0.1875 to 0.1875
- attention_exit_matrix: bfloat16 [1024, 1024], P('dp', 'head'), may hold values from -1.5 to 1.5
- expand_matrix: bfloat16 [1024, 4096], P('dp', 'head'), may hold values from -0.1875 to 0.1875
- contract_matrix: bfloat16 [4096, 1024], P('dp', 'head'), may hold values from -0.09375 to 0.09375
- nested_projector: bfloat16 [1024, 288], P('dp', 'head'), may hold values from -0.1875 to 0.1875
- offset_model_width: bfloat16 [5, 1024], P(None, ('dp', 'head')), may hold values from -3 to 3
- offset_expanded: bfloat16 [4096], P(('dp', 'head')), may hold values from -3 to 3
- standardize_factor: bfloat16 [2, 1024], P(None, ('dp', 'head')), may hold values from 0.5 to 1.5
- standardize_offset: bfloat16 [2, 1024], P(None, ('dp', 'head')), may hold values from -3 to 3
- logarithmic_warmth: float32 [1], replicated, may hold values from -3.9 to -3
- passage_lengths_each: int32 [24], P('dp'), may hold values from 50 to 256, as said below
- question_lengths: int32 [64], P('dp'), may hold values from 8 to 32, as said below
- relevant_passage: int32 [64], P('dp'), may hold values from 0 to 2
Outputs:
- outputs: bfloat16 [8192, 1024], P(('dp', 'head'))
- loss: float32 [1], replicated
- grad_tokens: float32 [8192, 1024], P(('dp', 'head'))
- grad_w_qkv: float32 [1024, 3072], P('dp', 'head')
- grad_w_out: float32 [1024, 1024], P('dp', 'head')
- grad_w_up: float32 [1024, 4096], P('dp', 'head')
- grad_w_down: float32 [4096, 1024], P('dp', 'head')
- grad_w_heads: float32 [1024, 288], P('dp', 'head')
- grad_bias_d: float32 [5, 1024], P(None, ('dp', 'head'))
- grad_bias_up: float32 [4096], P(('dp', 'head'))
- grad_norm_gain: float32 [2, 1024], P(None, ('dp', 'head'))
- grad_norm_shift: float32 [2, 1024], P(None, ('dp', 'head'))
- grad_log_temp: float32 [1], replicated
The draws below stay inside these ranges and needn't reach their ends.
Inputs may be any that keep to these rules, and one draw needn't show every extreme that they name: `passage_lengths_each`: tokens of each document; in every draw some document has exactly 256. `question_lengths`: real tokens of each query; in every draw some query has exactly 32.
All inputs are finite; a program needn't handle non-finite values.
Results may differ from the reference program's by a relative error of at most 0.024.
Values may be sent and summed in bfloat16 or wider, within the bound.
No kernel may reach another device: no remote copies, remote signals or barrier semaphores. Data moves between devices by JAX's collectives and lax.ppermute only.
A program may use at most 128 MiB of HBM per device.

```python
import jax
import jax.numpy as jnp
from jax import lax

D = 1024
HEADS = 16
HEAD_DIM = 64
FF = 4096
EMB = 128
EMB_MID = 96
EMB_SMALL = 64
QLEN = 32
QMIN = 8
MIN_DOC = 50
TOK_DEV = 256
QRY_GROUP = 8
ROW_BLOCK = 256
HEAD_COLS = 288
TOKENS = 8192
DOCS = 24
QUERIES = 64
N_DP = 8
N_HEAD = 4


def draw_passage_lengths_each(key, part):
    leading_key = jax.random.fold_in(key, 11)
    second_key = jax.random.fold_in(key, 12)
    lengths = jax.random.randint(leading_key, (DOCS,), MIN_DOC, TOK_DEV + 1, dtype=jnp.int32)
    longest = jax.random.randint(second_key, (), 0, DOCS, dtype=jnp.int32)
    return jnp.where(jnp.arange(DOCS, dtype=jnp.int32) == longest, TOK_DEV, lengths)


def draw_question_lengths(key, part):
    leading_key = jax.random.fold_in(key, 21)
    second_key = jax.random.fold_in(key, 22)
    lengths = jax.random.randint(leading_key, (QUERIES,), QMIN, QLEN + 1, dtype=jnp.int32)
    longest = jax.random.randint(second_key, (), 0, QUERIES, dtype=jnp.int32)
    return jnp.where(jnp.arange(QUERIES, dtype=jnp.int32) == longest, QLEN, lengths)


def with_ends(entries, own_key, smallest, largest):
    place = [jax.random.randint(jax.random.fold_in(own_key, axis), (), 0, length) for axis, length in enumerate(entries.shape)]
    widest = entries.shape.index(max(entries.shape))
    beside = place[:widest] + [(place[widest] + 1) % entries.shape[widest]] + place[widest + 1:]
    return entries.at[tuple(place)].set(smallest).at[tuple(beside)].set(largest)


def levels(stream_key, extent, split, smallest, top_value):
    def one(dim, parts):
        heights = jax.random.uniform(jax.random.fold_in(jax.random.fold_in(stream_key, 6), dim), (parts,), jnp.float32, smallest / len(split), top_value / len(split))
        return jnp.repeat(jnp.exp(heights), extent[dim] // parts).reshape((-1,) + (1,) * (len(extent) - dim - 1))

    factor_of = one(*split[0])
    for cut in split[1:]:
        factor_of = factor_of * one(*cut)
    return factor_of


def bell_draw(rng, shape, width, most, pieces=(), kind=jnp.bfloat16):
    level = levels(rng, shape, pieces, -0.22, 0.18) if pieces else 1.0
    array = jax.random.normal(rng, shape, jnp.float32) * width * level
    return jnp.minimum(jnp.maximum(array, -most), most).astype(kind)


def setup_inputs(seed: int = 0) -> dict:
    seeds = jax.random.split(jax.random.key(seed), 15)
    return {
        "layer_entries": bell_draw(seeds[0], (TOKENS, D), 1.0, 6.0, ((0, 32),)),
        "triple_projection_matrix": bell_draw(seeds[1], (D, 3 * D), D ** -0.5, 0.1875, ((0, 8), (1, 4))),
        "attention_exit_matrix": bell_draw(seeds[2], (D, D), (D // 64) ** -0.5, 1.5, ((0, 8), (1, 4))),
        "expand_matrix": bell_draw(seeds[3], (D, FF), D ** -0.5, 0.1875, ((0, 8), (1, 4))),
        "contract_matrix": bell_draw(seeds[4], (FF, D), FF ** -0.5, 0.09375, ((0, 8), (1, 4))),
        "nested_projector": bell_draw(seeds[5], (D, HEAD_COLS), D ** -0.5, 0.1875, ((0, 8), (1, 4))),
        "offset_model_width": bell_draw(seeds[6], (5, D), 0.5, 3.0, ((1, 32),)),
        "offset_expanded": bell_draw(seeds[7], (FF,), 0.5, 3.0, ((0, 32),)),
        "standardize_factor": jnp.clip(1.0 + 0.1 * jax.random.normal(seeds[8], (2, D), jnp.float32), 0.5, 1.5).astype(jnp.bfloat16),
        "standardize_offset": bell_draw(seeds[9], (2, D), 0.5, 3.0, ((1, 32),)),
        "logarithmic_warmth": jnp.clip(jax.random.uniform(seeds[10], (1,), jnp.float32, -3.9, -3.0), -3.9, -3.0),
        "passage_lengths_each": draw_passage_lengths_each(jax.random.fold_in(seeds[14], 71), 0),
        "question_lengths": draw_question_lengths(jax.random.fold_in(seeds[14], 71), 0),
        "relevant_passage": with_ends(jax.random.randint(seeds[13], (QUERIES,), 0, N_HEAD - 1), jax.random.fold_in(seeds[13], 1), 0, (N_HEAD - 1) - 1).astype(jnp.int32),
    }


EPS_NORM = 1e-05
EPS_UNIT = 1e-06
SHARPNESS = 0.05
ROPE_BASE = 10000.0
MASKED = -1000000000.0
SQRT_HALF = 0.7071067811865476

@jax.custom_vjp
def low(v):
    return lax.optimization_barrier(v.astype(jnp.bfloat16)).astype(jnp.float32)

@jax.custom_vjp
def low_back(v):
    return v

def low_keep(v):
    return (low(v), None)

def low_pass(kept, grad):
    return (grad,)

def back_keep(v):
    return (v, None)

def back_low(kept, grad):
    return (low(grad),)
low.defvjp(low_keep, low_pass)
low_back.defvjp(back_keep, back_low)

def exact_dot(left, right):
    return jnp.dot(left, right, precision=lax.Precision.HIGHEST, preferred_element_type=jnp.float32)

def exact_sum(formula, left, right):
    return jnp.einsum(formula, left, right, precision=lax.Precision.HIGHEST, preferred_element_type=jnp.float32)

def rope_tables(positions):
    halfway = HEAD_DIM // 2
    powers = jnp.arange(halfway, dtype=jnp.float32) * (2.0 / HEAD_DIM)
    angles = positions.astype(jnp.float32)[:, None] * (ROPE_BASE ** (-powers))[None, :]
    return (jnp.cos(angles)[:, None, :], jnp.sin(angles)[:, None, :])

def rotate(vectors, cosines, sines):
    halfway = vectors.shape[-1] // 2
    first_half = vectors[..., :halfway]
    second_half = vectors[..., halfway:]
    return jnp.concatenate([first_half * cosines - second_half * sines, second_half * cosines + first_half * sines], axis=-1)

def layer_norm(values, gain, shift):
    centred = values - lax.optimization_barrier(jnp.mean(values, axis=-1, keepdims=True))
    variance = lax.optimization_barrier(jnp.mean(centred * centred, axis=-1, keepdims=True))
    return centred * lax.rsqrt(variance + EPS_NORM) * gain + shift

def encode_block(block_rows, weights, segment, position, valid):
    wqkv, wout, wup, wdown, biases, bias_mid, gains, shifts = weights
    row_count = block_rows.shape[0]
    bias_qkv = jnp.concatenate([biases[0], biases[1], biases[2]])
    qkv = low_back(exact_dot(block_rows, wqkv) + bias_qkv).reshape(row_count, 3, HEADS, HEAD_DIM)
    cosines, sines = rope_tables(position)
    queries = low(rotate(qkv[:, 0], cosines, sines))
    keys = low(rotate(qkv[:, 1], cosines, sines))
    values = low(qkv[:, 2])
    block_count = row_count // ROW_BLOCK

    def attend(arguments_given):
        query_block, segment_block = arguments_given
        pairing_ratings = low_back(exact_sum('rhd,thd->hrt', query_block, keys) * HEAD_DIM ** (-0.5))
        allowed = (segment_block[:, None] == segment[None, :]) & valid[None, :]
        pairing_ratings = jnp.where(allowed[None], pairing_ratings, MASKED)
        top_score = lax.optimization_barrier(jnp.max(pairing_ratings, axis=-1, keepdims=True))
        raised = jnp.exp(pairing_ratings - top_score)
        probs = raised / lax.optimization_barrier(jnp.sum(raised, axis=-1, keepdims=True))
        return exact_sum('hrt,thd->rhd', low(probs), values)
    attended = lax.map(jax.checkpoint(attend), (queries.reshape(block_count, ROW_BLOCK, HEADS, HEAD_DIM), segment.reshape(block_count, ROW_BLOCK)))
    attended = low(low_back(attended.reshape(row_count, D)))
    branch = low_back(exact_dot(attended, wout) + biases[3])
    normed = layer_norm(block_rows + branch, gains[0], shifts[0])
    pre_act = low_back(exact_dot(low(normed), wup) + bias_mid)
    hidden = 0.5 * pre_act * (1.0 + jax.scipy.special.erf(pre_act * SQRT_HALF))
    branch_two = low_back(exact_dot(low(hidden), wdown) + biases[4])
    return layer_norm(normed + branch_two, gains[1], shifts[1])

def unit_rows(mapped_vectors):
    return low(mapped_vectors * lax.rsqrt(lax.optimization_barrier(jnp.sum(mapped_vectors * mapped_vectors, axis=-1, keepdims=True)) + EPS_UNIT))

def cohort_objective(arguments_given, projector_matrix, logarithmic_warmth):
    group_rows, query_lens, doc_lens, targets = arguments_given
    rounded = low(group_rows)
    query_rows = rounded[0]
    doc_rows = rounded[1:].reshape(-1, D)
    docs_group = doc_lens.shape[0]
    row_ids = jnp.arange(TOK_DEV, dtype=jnp.int32)
    query_valid = (row_ids % QLEN < jnp.repeat(query_lens, QLEN)).astype(jnp.float32)
    doc_valid = (row_ids[None, :] < doc_lens[:, None]).reshape(1, -1)
    smoothing_warmth = jnp.exp(logarithmic_warmth[0])
    onehot = (targets[:, None] == jnp.arange(docs_group, dtype=jnp.int32)[None, :]).astype(jnp.float32)
    query_ids = jnp.arange(QRY_GROUP, dtype=jnp.int32)
    starts = (0, 0, EMB, EMB + EMB_MID)
    widths = (EMB, EMB, EMB_MID, EMB_SMALL)
    total_loss = jnp.zeros((), jnp.float32)
    for member in range(4):
        window = projector_matrix[:, starts[member]:starts[member] + widths[member]]
        query_unit = unit_rows(low_back(exact_dot(query_rows, window)))
        doc_unit = unit_rows(low_back(exact_dot(doc_rows, window)))
        similar = low_back(exact_sum('te,se->ts', query_unit, doc_unit)) / SHARPNESS
        similar = jnp.where(doc_valid, similar, MASKED).reshape(TOK_DEV, docs_group, TOK_DEV)
        top_score = lax.optimization_barrier(jnp.max(similar, axis=-1))
        soft_max = SHARPNESS * (top_score + jnp.log(lax.optimization_barrier(jnp.sum(jnp.exp(similar - top_score[..., None]), axis=-1))))
        pairing_ratings = lax.optimization_barrier(jnp.sum((soft_max * query_valid[:, None]).reshape(QRY_GROUP, QLEN, docs_group), axis=1)) / query_lens[:, None].astype(jnp.float32)
        similarity_entries = pairing_ratings / smoothing_warmth
        top_logit = lax.optimization_barrier(jnp.max(similarity_entries, axis=-1))
        losses = top_logit + jnp.log(lax.optimization_barrier(jnp.sum(jnp.exp(similarity_entries - top_logit[:, None]), axis=-1))) - lax.optimization_barrier(jnp.sum(similarity_entries * onehot, axis=-1))
        if member < 2:
            chosen = (query_ids // (QRY_GROUP // 2) == member).astype(jnp.float32)
        else:
            chosen = jnp.ones((QRY_GROUP,), jnp.float32)
        total_loss = total_loss + jnp.sum(chosen * losses) / QRY_GROUP
    return total_loss

def reference(layer_entries, triple_projection_matrix, attention_exit_matrix, expand_matrix, contract_matrix, nested_projector, offset_model_width, offset_expanded, standardize_factor, standardize_offset, logarithmic_warmth, passage_lengths_each, question_lengths, relevant_passage):
    groups = N_DP
    docs_group = N_HEAD - 1
    block_total = groups * N_HEAD
    row_ids = jnp.arange(TOK_DEV, dtype=jnp.int32)
    query_lens = question_lengths.reshape(groups, QRY_GROUP)
    doc_lens = passage_lengths_each.reshape(groups, docs_group)
    targets = relevant_passage.reshape(groups, QRY_GROUP)
    query_valid = (row_ids % QLEN)[None, :] < jnp.repeat(query_lens, QLEN, axis=1)
    doc_valid = row_ids[None, None, :] < doc_lens[:, :, None]
    valid = jnp.concatenate([query_valid[:, None, :], doc_valid], axis=1).reshape(block_total, TOK_DEV)
    segment = jnp.concatenate([jnp.broadcast_to(row_ids // QLEN, (groups, 1, TOK_DEV)), jnp.zeros((groups, docs_group, TOK_DEV), jnp.int32)], axis=1).reshape(block_total, TOK_DEV)
    position = jnp.concatenate([jnp.broadcast_to(row_ids % QLEN, (groups, 1, TOK_DEV)), jnp.broadcast_to(row_ids, (groups, docs_group, TOK_DEV))], axis=1).reshape(block_total, TOK_DEV)
    real_numbers = tuple((element_entry.astype(jnp.float32) for element_entry in (layer_entries, triple_projection_matrix, attention_exit_matrix, expand_matrix, contract_matrix, nested_projector, offset_model_width, offset_expanded, standardize_factor, standardize_offset, logarithmic_warmth)))

    def forward(block_input, wqkv, wout, wup, wdown, wheads, biases, bias_mid, gains, shifts, temp_log):
        weights = (wqkv, wout, wup, wdown, biases, bias_mid, gains, shifts)

        def one_block(carry, arguments_given):
            rows_in, segment_in, position_in, valid_in = arguments_given
            return (carry, jax.checkpoint(encode_block)(rows_in, weights, segment_in, position_in, valid_in))
        carry_out, encoded = lax.scan(one_block, jnp.zeros((), jnp.float32), (block_input.reshape(block_total, TOK_DEV, D), segment, position, valid))

        def one_group(arguments_given):
            return cohort_objective(arguments_given, wheads, temp_log)
        losses = lax.map(jax.checkpoint(one_group), (encoded.reshape(groups, N_HEAD, TOK_DEV, D), query_lens, doc_lens, targets))
        return (jnp.sum(losses), encoded.reshape(TOKENS, D))
    loss, backward, encoded = jax.vjp(forward, *real_numbers, has_aux=True)
    grads = backward(jnp.ones_like(loss))
    return (encoded.astype(jnp.bfloat16), loss.reshape(1), grads[0], grads[1], grads[2], grads[3], grads[4], grads[5], grads[6], grads[7], grads[8], grads[9], grads[10])
```

```python
import jax
import jax.numpy as jnp
from jax import lax
from jax.sharding import PartitionSpec as P

D = 1024
HEADS = 16
HEAD_DIM = 64
FF = 4096
EMB = 128
EMB_MID = 96
EMB_SMALL = 64
QLEN = 32

EPS_NORM = 1e-05
EPS_UNIT = 1e-06
SHARPNESS = 0.05
ROPE_BASE = 10000.0
MASKED = -1000000000.0
SQRT_HALF = 0.7071067811865476
GAUSS_SCALE = 0.3989422804014327

BF = jnp.bfloat16
F32 = jnp.float32
STARTS = (0, EMB, EMB + EMB_MID)
WIDTHS = (EMB, EMB_MID, EMB_SMALL)
SLOTS = 3
QUADS = 4
GROUP = 128
HIDE = FF // 8


def mm(a, b):
    return jnp.dot(a, b, preferred_element_type=F32)


def mm_tn(a, b):
    return lax.dot_general(a, b, (((0,), (0,)), ((), ())), preferred_element_type=F32)


def mm_nt(a, b):
    return lax.dot_general(a, b, (((1,), (1,)), ((), ())), preferred_element_type=F32)


def norm_forward(values, gain, shift):
    centred = values - jnp.mean(values, axis=-1, keepdims=True)
    variance = jnp.mean(centred * centred, axis=-1, keepdims=True)
    inverse = lax.rsqrt(variance + EPS_NORM)
    scaled = centred * inverse
    return (scaled * gain + shift, scaled, inverse)


def norm_backward(grad_out, scaled, inverse, gain):
    grad_scaled = grad_out * gain
    grad_in = inverse * (
        grad_scaled
        - jnp.mean(grad_scaled, axis=-1, keepdims=True)
        - scaled * jnp.mean(grad_scaled * scaled, axis=-1, keepdims=True)
    )
    return (grad_in, jnp.sum(grad_out * scaled, axis=0), jnp.sum(grad_out, axis=0))


def rope_tables(positions):
    halfway = HEAD_DIM // 2
    powers = jnp.arange(halfway, dtype=F32) * (2.0 / HEAD_DIM)
    angles = positions.astype(F32)[:, None] * (ROPE_BASE ** (-powers))[None, :]
    return (jnp.cos(angles)[:, None, :], jnp.sin(angles)[:, None, :])


def rotate(vectors, cosines, sines):
    halfway = vectors.shape[-1] // 2
    first = vectors[..., :halfway]
    second = vectors[..., halfway:]
    return jnp.concatenate(
        [first * cosines - second * sines, second * cosines + first * sines], axis=-1
    )


def pad_windows(matrix):
    columns = [
        jnp.pad(matrix[:, s : s + w], ((0, 0), (0, EMB - w))) for s, w in zip(STARTS, WIDTHS)
    ]
    return jnp.concatenate(columns, axis=1)


def soft_maxsim(all_proj, place, doc_lens, query_lens, targets, temp_log):
    docs = doc_lens.shape[0]
    rows = all_proj.shape[0] // (docs + 1)
    queries = query_lens.shape[0]
    own_doc = jnp.maximum(place - 1, 0)
    row_ids = jnp.arange(rows, dtype=jnp.int32)
    doc_valid = (row_ids[None, :] < doc_lens[:, None]).reshape(1, -1)
    query_valid = (row_ids % QLEN < jnp.repeat(query_lens, QLEN)).astype(F32)
    lengths = query_lens.astype(F32)
    warmth = jnp.exp(temp_log[0])
    onehot = (targets[:, None] == jnp.arange(docs, dtype=jnp.int32)[None, :]).astype(F32)
    loss = jnp.zeros((), F32)
    grad_temp = jnp.zeros((), F32)
    grads = []
    for slot in range(SLOTS):
        mapped = all_proj[:, slot * EMB : (slot + 1) * EMB].astype(F32)
        inverse = lax.rsqrt(jnp.sum(mapped * mapped, axis=-1, keepdims=True) + EPS_UNIT)
        unit = mapped * inverse
        low = unit.astype(BF)
        query_unit, doc_unit = low[:rows], low[rows:]
        similar = jnp.where(doc_valid, mm_nt(query_unit, doc_unit) / SHARPNESS, MASKED)
        similar = similar.reshape(rows, docs, rows)
        top = jnp.max(similar, axis=-1)
        raised = jnp.exp(similar - top[..., None])
        total = jnp.sum(raised, axis=-1)
        soft = SHARPNESS * (top + jnp.log(total))
        ratings = (
            jnp.sum((soft * query_valid[:, None]).reshape(queries, QLEN, docs), axis=1)
            / lengths[:, None]
        )
        logits = ratings / warmth
        top_logit = jnp.max(logits, axis=-1)
        logit_exp = jnp.exp(logits - top_logit[:, None])
        logit_total = jnp.sum(logit_exp, axis=-1)
        losses = top_logit + jnp.log(logit_total) - jnp.sum(logits * onehot, axis=-1)
        loss = loss + jnp.sum(losses) / queries
        grad_logits = (logit_exp / logit_total[:, None] - onehot) / queries
        grad_temp = grad_temp - jnp.sum(grad_logits * logits)
        grad_soft = (
            jnp.repeat(grad_logits / warmth / lengths[:, None], QLEN, axis=0)
            * query_valid[:, None]
        )
        grad_similar = (
            (grad_soft[:, :, None] * (raised / total[..., None]))
            .reshape(rows, docs * rows)
            .astype(BF)
        )
        own_similar = lax.dynamic_slice(grad_similar, (0, own_doc * rows), (rows, rows))
        grad_unit = jnp.where(
            place == 0, mm(grad_similar, doc_unit), mm_tn(own_similar, query_unit)
        )
        own_unit = lax.dynamic_slice(unit, (place * rows, 0), (rows, EMB))
        own_inverse = lax.dynamic_slice(inverse, (place * rows, 0), (rows, 1))
        grads.append(
            own_inverse
            * (grad_unit - own_unit * jnp.sum(grad_unit * own_unit, axis=-1, keepdims=True))
        )
    return loss, grad_temp, jnp.concatenate(grads, axis=1).astype(BF)


def on_device(
    layer_entries,
    triple_projection_matrix,
    attention_exit_matrix,
    expand_matrix,
    contract_matrix,
    nested_projector,
    offset_model_width,
    offset_expanded,
    standardize_factor,
    standardize_offset,
    logarithmic_warmth,
    passage_lengths_each,
    question_lengths,
    relevant_passage,
):
    n_dp = lax.axis_size("dp")
    n_hd = lax.axis_size("head")
    n_all = n_dp * n_hd
    dp = lax.axis_index("dp")
    hd = lax.axis_index("head")
    low_span = n_dp // 8
    quad = dp // (2 * low_span)
    core = (dp // low_span) % 2
    pair_mask = low_span
    x_mask = 2 * low_span
    y_mask = 4 * low_span

    def swap(a, dp_mask=0, hd_mask=0):
        pairs = [
            (d * n_hd + h, (d ^ dp_mask) * n_hd + (h ^ hd_mask))
            for d in range(n_dp)
            for h in range(n_hd)
        ]
        return lax.ppermute(a, ("dp", "head"), pairs)

    def joined(bit, own, other):
        return jnp.where(
            bit == 0, jnp.concatenate([own, other], 0), jnp.concatenate([other, own], 0)
        )

    def gather_low(a):
        span = 1
        while span < low_span:
            a = joined((dp // span) % 2, a, swap(a, span))
            span *= 2
        return a

    def gather_head(a):
        span = 1
        while span < n_hd:
            a = joined((hd // span) % 2, a, swap(a, 0, span))
            span *= 2
        return a

    def scatter_low(a):
        span = low_span // 2
        while span >= 1:
            half = a.shape[0] // 2
            bit = (dp // span) % 2
            give = lax.dynamic_slice_in_dim(a, (1 - bit) * half, half, 0)
            keep = lax.dynamic_slice_in_dim(a, bit * half, half, 0)
            a = (keep.astype(F32) + swap(give, span).astype(F32)).astype(BF)
            span //= 2
        return a

    rows = layer_entries.shape[0]

    wup_low = gather_low(expand_matrix)
    wdown_low = gather_low(contract_matrix)
    up_rows = wup_low.shape[0]
    col_blocks = wup_low.shape[1] // 256
    packed_mlp = jnp.concatenate(
        [wup_low[:, i * 256 : (i + 1) * 256] for i in range(col_blocks)] + [wdown_low], axis=0
    )
    if low_span > 1:
        dp_groups = [
            [((q * 2 + k) * low_span + s) for q in range(QUADS) for k in range(2)]
            for s in range(low_span)
        ]
        mlp_all = lax.all_gather(
            lax.all_gather(packed_mlp, "head"), "dp", axis_index_groups=dp_groups
        )
        mlp_all = mlp_all.reshape((8, n_hd) + packed_mlp.shape)
    else:
        mlp_all = lax.all_gather(packed_mlp, ("dp", "head")).reshape(
            (8, n_hd) + packed_mlp.shape
        )
    heads_all = lax.all_gather(nested_projector, "head", axis=1, tiled=True)
    wide = offset_model_width.shape[1]
    vectors = jnp.concatenate(
        [
            offset_model_width,
            standardize_factor,
            standardize_offset,
            offset_expanded.reshape(FF // D, wide),
        ],
        axis=0,
    )
    vectors = lax.all_gather(lax.all_gather(vectors, "head"), "dp").reshape(n_all, 13, wide)

    partner_rows = swap(layer_entries, pair_mask)
    lens_own = jnp.concatenate([passage_lengths_each, question_lengths])
    lens_partner = swap(lens_own, pair_mask)
    both = jnp.concatenate([layer_entries, partner_rows], axis=0)

    wqkv_low = gather_low(triple_projection_matrix)
    k_rows = wqkv_low.shape[0]
    by_parity = wqkv_low.reshape(k_rows, -1, 2, GROUP)
    keep = lax.dynamic_index_in_dim(by_parity, core, 2, False).reshape(k_rows, -1)
    give = lax.dynamic_index_in_dim(by_parity, 1 - core, 2, False).reshape(k_rows, -1)
    wqkv_own = joined(core, keep, swap(give, pair_mask))
    wout_low = gather_low(attention_exit_matrix)
    halves = wout_low.shape[1] // GROUP
    wout_own = jnp.concatenate(
        [wout_low[:, i * GROUP : (i + 1) * GROUP] for i in range(halves)], axis=0
    )
    qkv_cols = wqkv_own.shape[1]
    out_shape = (wout_low.shape[0], halves)
    packed = jnp.concatenate([wqkv_own, wout_own], axis=1)
    shard = packed.shape
    packed = gather_head(packed[None])
    half = shard[0] // 2
    first, second = packed[:, :half], packed[:, half:]
    y_bit, x_bit = quad // 2, quad % 2
    first = joined(x_bit, first[None], swap(first, x_mask)[None])
    second = joined(y_bit, second[None], swap(second, y_mask)[None])
    first = joined(y_bit, first[None], swap(first, y_mask)[None])
    second = joined(x_bit, second[None], swap(second, x_mask)[None])
    second = jnp.swapaxes(second, 0, 1)
    packed = jnp.concatenate([first, second], axis=3).reshape((QUADS, n_hd) + shard)
    wqkv = packed[..., :qkv_cols].transpose(0, 2, 1, 3).reshape(D, n_hd * qkv_cols)
    wout = (
        packed[..., qkv_cols:]
        .reshape(QUADS, n_hd, halves, out_shape[0], GROUP)
        .transpose(0, 3, 1, 2, 4)
        .reshape(D // 2, D)
    )

    biases = vectors[:, :5].transpose(1, 0, 2).reshape(5, D).astype(F32)
    gains = vectors[:, 5:7].transpose(1, 0, 2).reshape(2, D).astype(F32)
    shifts = vectors[:, 7:9].transpose(1, 0, 2).reshape(2, D).astype(F32)
    bias_mid = vectors[:, 9:].reshape(FF).astype(F32)
    bias_qkv = biases[:3].reshape(-1, 2, GROUP)
    bias_qkv = lax.dynamic_index_in_dim(bias_qkv, core, 1, False).reshape(-1)
    bias_up = lax.dynamic_index_in_dim(
        bias_mid.reshape(-1, 2, HIDE), core, 1, False
    ).reshape(-1)

    row_ids = jnp.arange(rows, dtype=jnp.int32)
    is_query = hd == 0
    docs = passage_lengths_each.shape[0]

    def valid_of(lens):
        doc_here = lens[jnp.maximum(hd - 1, 0)]
        return jnp.where(is_query, row_ids % QLEN < jnp.repeat(lens[docs:], QLEN), row_ids < doc_here)

    valid = jnp.stack([valid_of(lens_own), valid_of(lens_partner)])
    segment = jnp.where(is_query, row_ids // QLEN, 0)
    position = jnp.where(is_query, row_ids % QLEN, row_ids)
    allowed = (segment[:, None] == segment[None, :])[None] & valid[:, None, :]
    cosines, sines = rope_tables(position)
    score_scale = HEAD_DIM ** (-0.5)
    heads_here = HEADS // 2

    qkv = (mm(both, wqkv) + bias_qkv).reshape(2, rows, 3, heads_here, HEAD_DIM)
    queries = rotate(qkv[:, :, 0], cosines, sines).astype(BF)
    keys = rotate(qkv[:, :, 1], cosines, sines).astype(BF)
    values = qkv[:, :, 2].astype(BF)
    scores = (
        jnp.einsum("brhd,bthd->bhrt", queries, keys, preferred_element_type=F32) * score_scale
    )
    scores = jnp.where(allowed[:, None], scores, MASKED)
    raised = jnp.exp(scores - jnp.max(scores, axis=-1, keepdims=True))
    probs = raised / jnp.sum(raised, axis=-1, keepdims=True)
    probs_low = probs.astype(BF)
    attended = (
        jnp.einsum("bhrt,bthd->brhd", probs_low, values, preferred_element_type=F32)
        .reshape(2 * rows, D // 2)
        .astype(BF)
    )
    part = mm(attended, wout)
    branch = part[:rows] + swap(part[rows:], pair_mask) + biases[3]
    normed, scaled_one, inverse_one = norm_forward(
        layer_entries.astype(F32) + branch, gains[0], shifts[0]
    )
    normed_own = normed.astype(BF)
    normed_low = jnp.concatenate([normed_own, swap(normed_own, pair_mask)], axis=0)

    order = [quad ^ r for r in range(QUADS)]
    up_all = mlp_all[:, :, : col_blocks * up_rows].reshape(8, n_hd, col_blocks, up_rows, 256)
    up_all = up_all.reshape(8, n_hd, -1, 2, HIDE // 256, up_rows, 256)
    up_all = lax.dynamic_index_in_dim(up_all, core, 3, False)
    wup = (
        up_all.transpose(1, 2, 0, 4, 3, 5)
        .reshape(QUADS, D, HIDE)
    )
    wup = jnp.concatenate(
        [lax.dynamic_index_in_dim(wup, order[r], 0, False) for r in range(QUADS)], axis=1
    )
    down_all = mlp_all[:, :, col_blocks * up_rows :].reshape(QUADS, 2, n_hd, HIDE, D // n_hd)
    down_all = lax.dynamic_index_in_dim(down_all, core, 1, False)
    wdown = jnp.concatenate(
        [lax.dynamic_index_in_dim(down_all, order[r], 0, False) for r in range(QUADS)], axis=1
    )
    wdown = wdown.transpose(1, 0, 2).reshape(QUADS * HIDE, D)
    bias_up_rel = jnp.concatenate(
        [lax.dynamic_slice(bias_up, (order[r] * HIDE,), (HIDE,)) for r in range(QUADS)]
    )
    pre_act = mm(normed_low, wup) + bias_up_rel
    gate = 0.5 * (1.0 + lax.erf(pre_act * SQRT_HALF))
    hidden = (pre_act * gate).astype(BF)
    part = mm(hidden, wdown)
    branch_two = part[:rows] + swap(part[rows:], pair_mask) + biases[4]
    final, scaled_two, inverse_two = norm_forward(normed + branch_two, gains[1], shifts[1])
    outputs = final.astype(BF)

    windows = pad_windows(lax.all_gather(heads_all, "dp", axis=0, tiled=True))
    own_proj = mm(outputs, windows).astype(BF)
    all_proj = lax.all_gather(own_proj, "head", axis=0, tiled=True)
    loss, grad_temp, grad_proj = soft_maxsim(
        all_proj, hd, passage_lengths_each, question_lengths, relevant_passage, logarithmic_warmth
    )

    grad_final = mm_nt(grad_proj, windows)
    grad_all = mm_tn(outputs, grad_proj)
    grad_heads = jnp.concatenate(
        [grad_all[:, i * EMB : i * EMB + w] for i, w in enumerate(WIDTHS)], axis=1
    )
    grad_two, gain_two, shift_two = norm_backward(grad_final, scaled_two, inverse_two, gains[1])
    branch_two_own = grad_two.astype(BF)
    branch_two_both = jnp.concatenate([branch_two_own, swap(branch_two_own, pair_mask)], axis=0)

    def in_order(a):
        width = a.shape[1] // QUADS
        return [lax.dynamic_slice(a, (0, order[r] * width), (a.shape[0], width)) for r in range(QUADS)]

    def blocks_of(a):
        width = a.shape[1] // QUADS
        return [a[:, r * width : (r + 1) * width] for r in range(QUADS)]

    def reduce_quads(lhs, rhs, first_mask, second_mask):
        away = {x_mask: 1, y_mask: 2}
        a, b = away[first_mask], away[second_mask]
        width = lhs[0].shape[1]
        send = mm_tn(jnp.concatenate([lhs[a], lhs[3]], axis=1), rhs).astype(BF)
        got = swap(send, first_mask).astype(F32)
        send = (mm_tn(lhs[b], rhs) + got[width:]).astype(BF)
        kept = mm_tn(lhs[0], rhs) + got[:width]
        return (kept + swap(send, second_mask).astype(F32)).astype(BF)

    def over_head(a):
        return lax.psum_scatter(a, "head", scatter_dimension=1, tiled=True)

    def finish_split(a, group):
        a = over_head(a)
        count = a.shape[0] // 2
        give = lax.dynamic_slice_in_dim(a, (1 - core) * count, count, 0)
        keep = lax.dynamic_slice_in_dim(a, core * count, count, 0)
        other = swap(give, pair_mask)
        keep = keep.reshape(count, -1, 1, group)
        other = other.reshape(count, -1, 1, group)
        whole = jnp.where(
            core == 0,
            jnp.concatenate([keep, other], axis=2),
            jnp.concatenate([other, keep], axis=2),
        ).reshape(count, -1)
        return scatter_low(whole).astype(F32)

    grad_w_heads = lax.psum_scatter(
        lax.psum_scatter(grad_heads, "dp", scatter_dimension=0, tiled=True),
        "head", scatter_dimension=1, tiled=True,
    )

    grad_w_down = scatter_low(
        over_head(reduce_quads(blocks_of(hidden), branch_two_both, x_mask, y_mask))
    ).astype(F32)
    slope = gate + pre_act * jnp.exp(-0.5 * pre_act * pre_act) * GAUSS_SCALE
    grad_pre_rel = (mm_nt(branch_two_both, wdown) * slope).astype(BF)
    bias_up_grad = jnp.sum(grad_pre_rel.astype(F32), axis=0)
    part = mm_nt(grad_pre_rel, wup)
    grad_pre = jnp.concatenate(
        [lax.dynamic_slice(grad_pre_rel, (0, order[r] * HIDE), (2 * rows, HIDE)) for r in range(QUADS)],
        axis=1,
    )
    grad_w_up = finish_split(
        reduce_quads(in_order(normed_low), grad_pre, y_mask, x_mask), HIDE
    )
    grad_normed = grad_two + part[:rows] + swap(part[rows:], pair_mask)
    grad_one, gain_one, shift_one = norm_backward(grad_normed, scaled_one, inverse_one, gains[0])
    branch_own = grad_one.astype(BF)
    branch_both = jnp.concatenate([branch_own, swap(branch_own, pair_mask)], axis=0)
    grad_w_out = scatter_low(
        over_head(reduce_quads(in_order(attended), branch_both, y_mask, x_mask))
    ).astype(F32)
    grad_attended = (
        mm_nt(branch_both, wout).astype(BF).reshape(2, rows, heads_here, HEAD_DIM)
    )
    grad_values = jnp.einsum("bhrt,brhd->bthd", probs_low, grad_attended, preferred_element_type=F32)
    grad_probs = jnp.einsum("brhd,bthd->bhrt", grad_attended, values, preferred_element_type=F32)
    grad_scores = (
        probs * (grad_probs - jnp.sum(probs * grad_probs, axis=-1, keepdims=True))
    ).astype(BF)
    grad_queries = (
        jnp.einsum("bhrt,bthd->brhd", grad_scores, keys, preferred_element_type=F32) * score_scale
    )
    grad_keys = (
        jnp.einsum("bhrt,brhd->bthd", grad_scores, queries, preferred_element_type=F32)
        * score_scale
    )
    grad_qkv = (
        jnp.stack(
            [rotate(grad_queries, cosines, -sines), rotate(grad_keys, cosines, -sines), grad_values],
            axis=2,
        )
        .reshape(2 * rows, 3 * D // 2)
        .astype(BF)
    )
    both_rel = in_order(both)
    split = 3 * D // 4
    kept = jnp.concatenate(
        [
            reduce_quads(both_rel, grad_qkv[:, :split], x_mask, y_mask),
            reduce_quads(both_rel, grad_qkv[:, split:], y_mask, x_mask),
        ],
        axis=1,
    )
    grad_w_qkv = finish_split(kept, GROUP)
    part = mm_nt(grad_qkv, wqkv)
    grad_tokens = grad_one + part[:rows] + swap(part[rows:], pair_mask)

    own_core = (jnp.arange(2) == core).astype(F32)
    qkv_bias = (
        jnp.sum(grad_qkv.astype(F32), axis=0).reshape(-1, 1, GROUP) * own_core[None, :, None]
    ).reshape(3, D)
    up_bias = jnp.zeros((QUADS, HIDE), F32)
    up_bias = jnp.stack(
        [lax.dynamic_slice(bias_up_grad, (order[r] * HIDE,), (HIDE,)) for r in range(QUADS)]
    )
    up_bias = (up_bias[:, None, :] * own_core[None, :, None]).reshape(FF)
    small = jnp.concatenate(
        [
            qkv_bias,
            jnp.sum(branch_own.astype(F32), axis=0)[None],
            jnp.sum(branch_two_own.astype(F32), axis=0)[None],
            jnp.stack([gain_one, gain_two, shift_one, shift_two]),
        ],
        axis=0,
    )
    once = (hd == 0).astype(F32)
    scalars = jnp.broadcast_to(jnp.stack([loss, grad_temp]) * once, (n_all, 2))
    small = jnp.concatenate(
        [
            small.reshape(9, n_all, wide).transpose(1, 0, 2).reshape(n_all, 9 * wide),
            up_bias.reshape(n_all, FF // n_all),
            scalars,
        ],
        axis=1,
    )
    summed = lax.psum_scatter(small.reshape(n_dp, -1), "dp", scatter_dimension=0, tiled=True)
    summed = lax.psum_scatter(summed.reshape(n_hd, -1), "head", scatter_dimension=0, tiled=True)
    summed = summed.reshape(-1)
    mat = summed[: 9 * wide].reshape(9, wide)
    end = 9 * wide + FF // n_all
    return (
        outputs,
        summed[end : end + 1],
        grad_tokens,
        grad_w_qkv,
        grad_w_out,
        grad_w_up,
        grad_w_down,
        grad_w_heads,
        mat[:5],
        summed[9 * wide : end],
        mat[5:7],
        mat[7:9],
        summed[end + 1 : end + 2],
    )


def solution(mesh):
    return jax.shard_map(
        on_device,
        mesh=mesh,
        in_specs=(
            P(("dp", "head"), None),
            P("dp", "head"),
            P("dp", "head"),
            P("dp", "head"),
            P("dp", "head"),
            P("dp", "head"),
            P(None, ("dp", "head")),
            P(("dp", "head")),
            P(None, ("dp", "head")),
            P(None, ("dp", "head")),
            P(),
            P("dp"),
            P("dp"),
            P("dp"),
        ),
        out_specs=(
            P(("dp", "head"), None),
            P(),
            P(("dp", "head"), None),
            P("dp", "head"),
            P("dp", "head"),
            P("dp", "head"),
            P("dp", "head"),
            P("dp", "head"),
            P(None, ("dp", "head")),
            P(("dp", "head")),
            P(None, ("dp", "head")),
            P(None, ("dp", "head")),
            P(),
        ),
        check_vma=False,
    )
```

```python
import jax
import jax.numpy as jnp
from jax import lax
from jax.experimental import pallas as pl
from jax.experimental.pallas import tpu as pltpu
from jax.sharding import PartitionSpec as P

D = 1024
HEADS = 16
HEAD_DIM = 64
FF = 4096
EMB = 128
EMB_MID = 96
EMB_SMALL = 64
QLEN = 32

EPS_NORM = 1e-05
EPS_UNIT = 1e-06
SHARPNESS = 0.05
ROPE_BASE = 10000.0
MASKED = -1000000000.0
SQRT_HALF = 0.7071067811865476
GAUSS_SCALE = 0.3989422804014327

BF = jnp.bfloat16
F32 = jnp.float32
STARTS = (0, EMB, EMB + EMB_MID)
WIDTHS = (EMB, EMB_MID, EMB_SMALL)
SLOTS = 3
QUADS = 4
GROUP = 128
HIDE = FF // 8


PAIRS = 4
VMEM_SPEC = pl.BlockSpec(memory_space=pltpu.VMEM)
SMEM_SPEC = pl.BlockSpec(memory_space=pltpu.SMEM)


def dot_nn(a, b):
    return lax.dot_general(a, b, (((1,), (0,)), ((), ())), preferred_element_type=F32)


def dot_tn(a, b):
    return lax.dot_general(a, b, (((0,), (0,)), ((), ())), preferred_element_type=F32)


def dot_nt(a, b):
    return lax.dot_general(a, b, (((1,), (1,)), ((), ())), preferred_element_type=F32)


def params(mib):
    return pltpu.CompilerParams(vmem_limit_bytes=58 << 20)


TIME_UNIT = 1150000000


def cost(micros):
    return pl.CostEstimate(flops=int(micros * TIME_UNIT), bytes_accessed=1, transcendentals=0)


def whole(a):
    zeros = (0,) * len(a.shape)
    return pl.BlockSpec(a.shape, lambda i: zeros, pipeline_mode=pl.Buffered(1))


def call(kernel, outs, args, n_smem, mib, estimate, name, scratch=()):
    return pl.pallas_call(
        kernel,
        out_shape=outs,
        grid=(1,),
        in_specs=[SMEM_SPEC] * n_smem + [whole(a) for a in args[n_smem:]],
        out_specs=[whole(a) for a in outs],
        scratch_shapes=list(scratch),
        compiler_params=params(mib),
        cost_estimate=estimate,
        name=name,
    )(*args)


def norm_parts(values):
    centred = values - jnp.mean(values, axis=-1, keepdims=True)
    variance = jnp.mean(centred * centred, axis=-1, keepdims=True)
    inverse = lax.rsqrt(variance + EPS_NORM)
    return centred * inverse, inverse


def norm_back(grad_out, scaled, inverse, gain):
    grad_scaled = grad_out * gain
    return inverse * (
        grad_scaled
        - jnp.mean(grad_scaled, axis=-1, keepdims=True)
        - scaled * jnp.mean(grad_scaled * scaled, axis=-1, keepdims=True)
    )


def pieces_of(a0, ax, ay, b0, by, bx):
    def piece(rq, rz):
        at = rz // 2
        if rz % 2 == 0:
            return [a0.at[at], ax.at[at], ay.at[0, at], ay.at[1, at]][rq]
        return [b0.at[at], bx.at[0, at], by.at[at], bx.at[1, at]][rq]

    return piece


def lanes_at(index, width=GROUP):
    return pl.ds(pl.multiple_of(index * width, width), width)


def turn(x, cos, sin_a, sin_b):
    return x * cos + pltpu.roll(x, 96, 1) * sin_a + pltpu.roll(x, 32, 1) * sin_b


def head_mask(h, shape):
    lane = lax.broadcasted_iota(jnp.int32, shape, 1)
    return (lane < HEAD_DIM) if h == 0 else (lane >= HEAD_DIM)


def softmax_rows(q, k, allowed):
    s = jnp.where(allowed, dot_nt(q, k), MASKED)
    raised = jnp.exp(s - jnp.max(s, axis=-1, keepdims=True))
    return raised * (1.0 / jnp.sum(raised, axis=-1, keepdims=True))


def attention_forward(
    place, x, a0, ax, ay, b0, by, bx, cos, sin_a, sin_b, mask, qkv, att, part, vec
):
    quad, hd, core = place[0], place[1], place[5]
    piece = pieces_of(a0, ax, ay, b0, by, bx)
    rows = cos.shape[0]
    for rq in range(4):
        for c in range(2):
            at = slice(c * GROUP, (c + 1) * GROUP)
            total = piece(rq, 0)[256:272, at].astype(F32)
            for rz in range(1, 4):
                total += piece(rq, rz)[256:272, at].astype(F32)
            vec[:, lanes_at(2 * (quad ^ rq) + c)] = total
    for rz in range(4):
        z = hd ^ rz
        acc = dot_nn(x[0], piece(0, rz)[0:256, 0:384])
        for rq in range(1, 4):
            acc += dot_nn(x[rq], piece(rq, rz)[0:256, 0:384])
        for j in range(3):
            i = 3 * z + j
            scale = jnp.where(i < PAIRS, HEAD_DIM**-0.5, 1.0).astype(F32)
            near = vec[0:8, lanes_at(2 * (i % 4) + core)]
            row = lax.broadcasted_iota(jnp.int32, near.shape, 0)
            bias = jnp.sum(jnp.where(row == i // 4, near, 0.0), axis=0, keepdims=True)
            for b in range(2):
                here = acc[b * rows : (b + 1) * rows, j * GROUP : (j + 1) * GROUP]
                here = here + bias
                turned = turn(here, cos[...], sin_a[...], sin_b[...])
                here = jnp.where(i < 2 * PAIRS, turned, here) * scale
                qkv[b * rows : (b + 1) * rows, lanes_at(i)] = here.astype(BF)

    def one(it, carry):
        b, r = it // PAIRS, it % PAIRS
        i = quad ^ r
        row = pl.ds(pl.multiple_of(b * rows, rows), rows)
        q = qkv[row, pl.ds(pl.multiple_of(i * GROUP, GROUP), GROUP)]
        k = qkv[row, pl.ds(pl.multiple_of((PAIRS + i) * GROUP, GROUP), GROUP)]
        v = qkv[row, pl.ds(pl.multiple_of((2 * PAIRS + i) * GROUP, GROUP), GROUP)]
        allowed = mask[b] > 0
        got = []
        for h in range(2):
            qh = jnp.where(head_mask(h, q.shape), q, jnp.zeros_like(q))
            probs = softmax_rows(qh, k, allowed)
            got.append(dot_nn(probs.astype(BF), v))
        att[r, row, :] = jnp.where(head_mask(0, q.shape), got[0], got[1]).astype(BF)
        return carry

    lax.fori_loop(0, 2 * PAIRS, one, 0)
    for rz in range(4):
        for half in range(2):
            sel = slice(half * GROUP, (half + 1) * GROUP)
            acc = dot_nn(att[0], piece(0, rz)[sel, 384:512])
            for rq in range(1, 4):
                acc += dot_nn(att[rq], piece(rq, rz)[sel, 384:512])
            part[:, lanes_at(2 * (hd ^ rz) + half)] = acc


def attention_backward(
    place, own, other, qkv, a0, ax, ay, b0, by, bx, cos, sin_a, sin_b, mask,
    grad_qkv, gx_own, gx_other, sums, ga,
):
    quad, hd = place[0], place[1]
    piece = pieces_of(a0, ax, ay, b0, by, bx)
    rows = cos.shape[0]
    for b, grad in ((0, own), (1, other)):
        for rq in range(4):
            acc = None
            for rz in range(4):
                for half in range(2):
                    w = piece(rq, rz)[half * GROUP : (half + 1) * GROUP, 384:512]
                    term = dot_nt(grad[:, lanes_at(2 * (hd ^ rz) + half)], w)
                    acc = term if acc is None else acc + term
            ga[rq, b * rows : (b + 1) * rows, :] = acc.astype(BF)

    def one(it, carry):
        b, r = it // PAIRS, it % PAIRS
        i = quad ^ r
        row = pl.ds(pl.multiple_of(b * rows, rows), rows)
        at_q = pl.ds(pl.multiple_of(i * GROUP, GROUP), GROUP)
        at_k = pl.ds(pl.multiple_of((PAIRS + i) * GROUP, GROUP), GROUP)
        at_v = pl.ds(pl.multiple_of((2 * PAIRS + i) * GROUP, GROUP), GROUP)
        q, k, v = qkv[row, at_q], qkv[row, at_k], qkv[row, at_v]
        grad_out = ga[r, row, :]
        allowed = mask[b] > 0
        zero = jnp.zeros_like(q)
        gq = gk = gv = None
        for h in range(2):
            sel = head_mask(h, q.shape)
            qh = jnp.where(sel, q, zero)
            kh = jnp.where(sel, k, zero)
            goh = jnp.where(sel, grad_out, zero)
            probs = softmax_rows(qh, k, allowed)
            gp = dot_nt(goh, v)
            gs = probs * (gp - jnp.sum(probs * gp, axis=-1, keepdims=True))
            gs = gs.astype(BF)
            tq, tk, tv = dot_nn(gs, kh), dot_tn(gs, qh), dot_tn(probs.astype(BF), goh)
            gq = tq if gq is None else gq + tq
            gk = tk if gk is None else gk + tk
            gv = tv if gv is None else gv + tv
        c, sa, sb = cos[...], -sin_a[...], -sin_b[...]
        grad_qkv[row, at_q] = turn(gq * (HEAD_DIM**-0.5), c, sa, sb).astype(BF)
        grad_qkv[row, at_k] = turn(gk, c, sa, sb).astype(BF)
        grad_qkv[row, at_v] = gv.astype(BF)
        return carry

    lax.fori_loop(0, 2 * PAIRS, one, 0)
    for rq in range(4):
        at = pl.ds(pl.multiple_of((quad ^ rq) * 256, 256), 256)
        acc = None
        for rz in range(4):
            cols = pl.ds(pl.multiple_of((hd ^ rz) * 384, GROUP), 384)
            term = dot_nt(grad_qkv[:, cols], piece(rq, rz)[0:256, 0:384])
            acc = term if acc is None else acc + term
        gx_own[:, at] = acc[:rows]
        gx_other[:, at] = acc[rows:]
    sums[...] = jnp.sum(grad_qkv[...].astype(F32), axis=0, keepdims=True)


def feed_forward(
    place, x, part, recv, vec, wup, wdown,
    scaled_out, inv_out, rel_out, hidden_out, slope_out, own_out, other_out, low,
):
    r = pl.program_id(0)
    rows = scaled_out.shape[0]

    @pl.when(r == 0)
    def _():
        for b in range(2):
            sel = slice(b * rows, (b + 1) * rows)
            swapped = slice((1 - b) * rows, (2 - b) * rows)
            h = x[sel, :].astype(F32) + part[sel, :] + recv[swapped, :] + vec[3:4, :]
            scaled, inverse = norm_parts(h)
            low[sel, :] = (scaled * vec[5:6, :] + vec[7:8, :]).astype(BF)
            if b == 0:
                scaled_out[...] = scaled
                inv_out[...] = inverse
        for q in range(QUADS):
            at = pl.ds(pl.multiple_of((place[0] ^ q) * 256, 256), 256)
            rel_out[q, :, :] = low[:, at]
        own_out[...] = jnp.zeros_like(own_out)
        other_out[...] = jnp.zeros_like(other_out)

    for cb in range(2):
        cols = slice(cb * 256, (cb + 1) * 256)
        w = wup[:, 0, cb * 128 : (cb + 1) * 128, :].reshape(D, 256)
        bias = [
            vec[9 + 2 * cb + k : 10 + 2 * cb + k, lanes_at(2 * (place[0] ^ r) + place[1])]
            for k in range(2)
        ]
        pre = dot_nn(low[...], w) + jnp.concatenate(bias, axis=1)
        gate = 0.5 * (1.0 + lax.erf(pre * SQRT_HALF))
        hidden_out[0, :, cols] = (pre * gate).astype(BF)
        slope_out[0, :, cols] = (
            gate + pre * jnp.exp(-0.5 * pre * pre) * GAUSS_SCALE
        ).astype(BF)
    for z in range(4):
        cols = slice(z * 256, (z + 1) * 256)
        acc = dot_nn(hidden_out[0], wdown[0, z])
        own_out[:, cols] += acc[:rows]
        other_out[:, cols] += acc[rows:]


def feed_forward_back(
    place, own, other, slope, wup, wdown, pre_out, own_out, other_out, sums, both
):
    r = pl.program_id(0)
    rows = own.shape[0]

    @pl.when(r == 0)
    def _():
        both[0:rows, :] = own[...]
        both[rows:, :] = other[...]
        own_out[...] = jnp.zeros_like(own_out)
        other_out[...] = jnp.zeros_like(other_out)

    acc = dot_nt(both[:, 0:256], wdown[0, 0])
    for z in range(1, 4):
        acc += dot_nt(both[:, z * 256 : (z + 1) * 256], wdown[0, z])
    grad = (acc * slope[0].astype(F32)).astype(BF)
    pre_out[...] = grad
    sums[...] = jnp.sum(grad.astype(F32), axis=0, keepdims=True)
    total = None
    for cb in range(2):
        w = wup[:, 0, cb * 128 : (cb + 1) * 128, :].reshape(D, 256)
        term = dot_nt(pre_out[:, cb * 256 : (cb + 1) * 256], w)
        total = term if total is None else total + term
    own_out[...] += total[:rows]
    other_out[...] += total[rows:]


def final_norm(scaled_one, part, recv, vec, windows, out, scaled_out, inv_out, proj):
    h = scaled_one[...] * vec[5:6, :] + vec[7:8, :] + part[...] + recv[...] + vec[4:5, :]
    scaled, inverse = norm_parts(h)
    scaled_out[...] = scaled
    inv_out[...] = inverse
    low = (scaled * vec[6:7, :] + vec[8:9, :]).astype(BF)
    out[...] = low
    proj[...] = dot_nn(low, windows[...]).astype(BF)


def soft_maxsim(
    place, temp, lanes, projs, windows, out, scaled, inverse_two, vec,
    grad_two, low_two, grad_heads, sums, scalars, gproj, units, shares, similar_low,
):
    hd = place[1]
    rows = out.shape[0]
    docs = projs.shape[0] - 1
    row = lax.broadcasted_iota(jnp.int32, (rows, GROUP), 0)
    lane = lax.broadcasted_iota(jnp.int32, (rows, GROUP), 1)
    member = (row // QLEN == lane).astype(F32)
    lens = lanes[0:1, :]
    len_row = jnp.sum(member * lens, axis=1, keepdims=True)
    valid = (row % QLEN).astype(F32) < len_row
    queries = rows // QLEN
    used = lax.broadcasted_iota(jnp.int32, (1, GROUP), 1) < queries
    weight = jnp.where(valid, member, 0.0) / jnp.where(used, lens, 1.0)
    warmth = jnp.exp(jnp.full((1, GROUP), temp[0], F32))
    key = lax.broadcasted_iota(jnp.int32, (rows, rows), 1)
    loss = jnp.zeros((1, GROUP), F32)
    grad_temp = jnp.zeros((1, GROUP), F32)
    for slot in range(SLOTS):
        cols = slice(slot * EMB, (slot + 1) * EMB)

        def unit_of(block):
            mapped = projs[block, :, cols].astype(F32)
            inverse = lax.rsqrt(jnp.sum(mapped * mapped, axis=-1, keepdims=True) + EPS_UNIT)
            return mapped * inverse, inverse

        for block in range(docs + 1):
            units[block * rows : (block + 1) * rows, :] = unit_of(block)[0].astype(BF)
        logits = []
        for d in range(docs):
            doc = slice((d + 1) * rows, (d + 2) * rows)
            similar = dot_nt(units[0:rows, :], units[doc, :]) * (1.0 / SHARPNESS)
            similar = jnp.where(key < place[2 + d], similar, MASKED)
            top = jnp.max(similar, axis=-1, keepdims=True)
            raised = jnp.exp(similar - top)
            total = jnp.sum(raised, axis=-1, keepdims=True)
            soft = SHARPNESS * (top + jnp.log(total))
            shares[:, d * rows : (d + 1) * rows] = raised * (1.0 / total)
            logits.append(jnp.sum(soft * weight, axis=0, keepdims=True) / warmth)
        top_logit = jnp.maximum(jnp.maximum(logits[0], logits[1]), logits[2])
        exps = [jnp.exp(x - top_logit) for x in logits]
        total = exps[0] + exps[1] + exps[2]
        hits = [(lanes[1:2, :] == float(d)).astype(F32) for d in range(docs)]
        picked = logits[0] * hits[0] + logits[1] * hits[1] + logits[2] * hits[2]
        loss += jnp.where(used, top_logit + jnp.log(total) - picked, 0.0) / queries
        for d in range(docs):
            grad = jnp.where(used, exps[d] / total - hits[d], 0.0) / queries
            grad_temp -= grad * logits[d]
            grad_soft = jnp.sum(weight * (grad / warmth), axis=1, keepdims=True)
            at = slice(d * rows, (d + 1) * rows)
            similar_low[:, at] = (grad_soft * shares[:, at]).astype(BF)

        own = jnp.maximum(hd - 1, 0)
        at = pl.ds(pl.multiple_of(own * rows, rows), rows)
        from_docs = dot_nn(similar_low[...], units[rows:, :])
        from_queries = dot_tn(similar_low[:, at], units[0:rows, :])
        grad = jnp.where(hd == 0, from_docs, from_queries)
        unit, inverse = unit_of(hd)
        gproj[:, cols] = (
            inverse * (grad - unit * jnp.sum(grad * unit, axis=-1, keepdims=True))
        ).astype(BF)

    scalars[0:1, :] = loss
    scalars[1:2, :] = grad_temp
    grad_final = dot_nt(gproj[...], windows[...])
    xhat = scaled[...]
    grad = norm_back(grad_final, xhat, inverse_two[...], vec[6:7, :])
    grad_two[...] = grad
    low_two[...] = grad.astype(BF)
    sums[0:1, :] = jnp.sum(grad_final * xhat, axis=0, keepdims=True)
    sums[1:2, :] = jnp.sum(grad_final, axis=0, keepdims=True)
    sums[2:3, :] = jnp.sum(low_two[...].astype(F32), axis=0, keepdims=True)
    grad_heads[...] = dot_tn(out[...], gproj[...])


def first_norm_back(grad_two, own, recv, scaled, inverse, vec, grad_one, low_one, sums):
    grad_out = grad_two[...] + own[...] + recv[...]
    xhat = scaled[...]
    grad = norm_back(grad_out, xhat, inverse[...], vec[5:6, :])
    grad_one[...] = grad
    low_one[...] = grad.astype(BF)
    sums[0:1, :] = jnp.sum(grad_out * xhat, axis=0, keepdims=True)
    sums[1:2, :] = jnp.sum(grad_out, axis=0, keepdims=True)
    sums[2:3, :] = jnp.sum(low_one[...].astype(F32), axis=0, keepdims=True)


def weight_grad(spot, lhs, rhs, blocks, places, adds, name, micros, kind=BF):
    tokens, width = lhs.shape[1:]
    whole_cols = places is None
    places = (None,) if whole_cols else places
    count = len(places)
    tile = rhs[0].shape[1] // (1 if whole_cols else 4)
    step = (blocks[1] - blocks[0]) if len(blocks) > 1 else 0
    parts = len(rhs)
    span = tokens // parts
    n_add = len(adds)

    def column(s, place):
        return 0 if place is None else s[2] ^ place

    def kernel(spot_ref, lhs_ref, *refs):
        out = refs[-1]
        for k in range(count):
            total = None
            for p in range(parts):
                term = dot_tn(lhs_ref[0, p * span : (p + 1) * span, :], refs[k * parts + p][...])
                total = term if total is None else total + term
            for add in refs[count * parts + k * n_add : count * parts + (k + 1) * n_add]:
                total += add[0].astype(F32)
            out[k] = total.astype(kind)

    specs = [pl.BlockSpec((1, tokens, width), lambda i, s: (blocks[0] + step * i, 0, 0))]
    for place in places:
        specs += [pl.BlockSpec((span, tile), lambda i, s, c=place: (0, column(s, c)))] * parts
    for place in places:
        for _, at, aligned in adds:
            if aligned:
                index = lambda i, s, at=at, c=place: (at, 0, column(s, c))
            else:
                index = lambda i, s, at=at: (at, 0, 0)
            specs.append(pl.BlockSpec((1, width, tile), index))
    return pl.pallas_call(
        kernel,
        out_shape=jax.ShapeDtypeStruct((len(blocks) * count, width, tile), kind),
        grid_spec=pltpu.PrefetchScalarGridSpec(
            num_scalar_prefetch=1,
            grid=(len(blocks),),
            in_specs=specs,
            out_specs=pl.BlockSpec((count, width, tile), lambda i, s: (i, 0, 0)),
        ),
        compiler_params=params(24),
        cost_estimate=cost(micros),
        name=name,
    )(spot, lhs, *(list(rhs) * count), *([a for a, _, _ in adds] * count))


def tail_grad(spot, x, grad_qkv, att, own, other, halves, blocks, places, adds, name, micros, kind=BF):
    tokens = x.shape[1]
    whole_cols = places is None
    places = (None,) if whole_cols else places
    count = len(places)
    heads = 4 if whole_cols else 1
    step = (blocks[1] - blocks[0]) if len(blocks) > 1 else 0
    n_half = len(halves)
    rows = tokens // 2
    n_add = len(adds)
    per = n_add // n_half
    lane_blocks = 1 if whole_cols else n_half

    def column(s, place):
        return 0 if place is None else s[2] ^ place

    def kernel(spot_ref, x_ref, att_ref, *refs):
        out = refs[-1]
        at_add = count * (1 + 2 * lane_blocks)
        for c in range(count):
            qkv_ref, *pair = refs[c * (1 + 2 * lane_blocks) : (c + 1) * (1 + 2 * lane_blocks)]
            for k, half in enumerate(halves):
                left_all = dot_tn(x_ref[0, :, half * GROUP : (half + 1) * GROUP], qkv_ref[...])
                for z in range(heads):
                    if whole_cols:
                        lanes = slice((2 * z + half) * GROUP, (2 * z + half + 1) * GROUP)
                        up, down = pair[0][:, lanes], pair[1][:, lanes]
                    else:
                        up, down = pair[2 * k][...], pair[2 * k + 1][...]
                    right = dot_tn(att_ref[0, 0:rows, :], up) + dot_tn(att_ref[0, rows:, :], down)
                    left = left_all[:, z * 384 : (z + 1) * 384]
                    first = at_add + c * n_add + k * per
                    lo = z * 512
                    for add in refs[first : first + per]:
                        left += add[0, 0, :, lo : lo + 384].astype(F32)
                        right += add[0, 0, :, lo + 384 : lo + 512].astype(F32)
                    out[c, k, :, lo : lo + 384] = left.astype(kind)
                    out[c, k, :, lo + 384 : lo + 512] = right.astype(kind)

    specs = [
        pl.BlockSpec((1, tokens, 256), lambda i, s: (blocks[0] + step * i, 0, 0)),
        pl.BlockSpec((1, tokens, GROUP), lambda i, s: (blocks[0] + step * i, 0, 0)),
    ]
    inputs = []
    for place in places:
        specs.append(pl.BlockSpec((tokens, 384 * heads), lambda i, s, c=place: (0, column(s, c))))
        inputs.append(grad_qkv)
        for half in halves[:lane_blocks]:
            if whole_cols:
                index = lambda i, s: (0, 0)
            else:
                index = lambda i, s, c=place, half=half: (0, 2 * column(s, c) + half)
            specs += [pl.BlockSpec((rows, D if whole_cols else GROUP), index)] * 2
            inputs += [own, other]
    for place in places:
        for a, at, k, aligned in adds:
            if aligned:
                index = lambda i, s, at=at, k=k, c=place: (at, k, 0, column(s, c))
            else:
                index = lambda i, s, at=at, k=k: (at, k, 0, 0)
            specs.append(pl.BlockSpec((1, 1, GROUP, 512 * heads), index))
            inputs.append(a)
    return pl.pallas_call(
        kernel,
        out_shape=jax.ShapeDtypeStruct((len(blocks) * count, n_half, GROUP, 512 * heads), kind),
        grid_spec=pltpu.PrefetchScalarGridSpec(
            num_scalar_prefetch=1,
            grid=(len(blocks),),
            in_specs=specs,
            out_specs=pl.BlockSpec(
                (count, n_half, GROUP, 512 * heads), lambda i, s: (i, 0, 0, 0)
            ),
        ),
        compiler_params=params(24),
        cost_estimate=cost(micros),
        name=name,
    )(spot, x, att, *inputs)


def pack_sums(spot, two, one, up, qkv, scalars, out):
    core, hd = spot[1], spot[2]
    out[...] = jnp.zeros_like(out)
    for i in range(3 * PAIRS):
        out[2 * (i % 4) + core, i // 4 : i // 4 + 1, :] = qkv[0:1, i * GROUP : (i + 1) * GROUP]
    for i in range(4 * QUADS):
        out[2 * (i // 4) + core, 9 + i % 4 : 10 + i % 4, :] = up[
            0:1, i * GROUP : (i + 1) * GROUP
        ]
    once = jnp.where(hd == 0, 1.0, 0.0).astype(F32)
    totals = [jnp.sum(scalars[k : k + 1, :], axis=1, keepdims=True) * once for k in range(2)]
    for t in range(2 * QUADS):
        at = slice(t * GROUP, (t + 1) * GROUP)
        out[t, 3:4, :] = one[2:3, at]
        out[t, 4:5, :] = two[2:3, at]
        out[t, 5:6, :] = one[0:1, at]
        out[t, 6:7, :] = two[0:1, at]
        out[t, 7:8, :] = one[1:2, at]
        out[t, 8:9, :] = two[1:2, at]
        for k in range(2):
            out[t, 13 + k : 14 + k, :] = jnp.broadcast_to(totals[k], (1, GROUP))


def make_windows(tiles, windows):
    lane = lax.broadcasted_iota(jnp.int32, (GROUP // 2, GROUP), 1)
    for dp in range(2 * QUADS):
        for half in range(2):
            first_row = dp * GROUP + half * (GROUP // 2)
            at = slice(first_row, first_row + GROUP // 2)
            t = [
                tiles[dp, z, :, half * GROUP : (half + 1) * GROUP].astype(F32) for z in range(4)
            ]
            second = pltpu.roll(t[1], 72, 1)
            first = jnp.where(lane < 72, t[0], second)
            middle = jnp.where(lane < 16, second, pltpu.roll(t[2], 16, 1))
            middle = jnp.where(lane < 88, middle, pltpu.roll(t[3], 88, 1))
            windows[at, 0:128] = first.astype(BF)
            windows[at, 128:256] = jnp.where(lane < 96, middle, 0.0).astype(BF)
            windows[at, 256:384] = jnp.where(lane < 64, pltpu.roll(t[3], 120, 1), 0.0).astype(BF)


def on_device(
    layer_entries,
    triple_projection_matrix,
    attention_exit_matrix,
    expand_matrix,
    contract_matrix,
    nested_projector,
    offset_model_width,
    offset_expanded,
    standardize_factor,
    standardize_offset,
    logarithmic_warmth,
    passage_lengths_each,
    question_lengths,
    relevant_passage,
):
    n_dp = lax.axis_size("dp")
    n_hd = lax.axis_size("head")
    n_all = n_dp * n_hd
    dp = lax.axis_index("dp")
    hd = lax.axis_index("head")
    low_span = n_dp // 8
    quad = dp // (2 * low_span)
    core = (dp // low_span) % 2
    pair_mask = low_span
    x_mask = 2 * low_span
    y_mask = 4 * low_span

    def swap(a, dp_mask=0, hd_mask=0):
        pairs = [
            (d * n_hd + h, (d ^ dp_mask) * n_hd + (h ^ hd_mask))
            for d in range(n_dp)
            for h in range(n_hd)
        ]
        return lax.ppermute(a, ("dp", "head"), pairs)

    def after(value, *others):
        return lax.optimization_barrier((value, *others))[0]

    def joined(bit, own, other):
        return jnp.where(
            bit == 0, jnp.concatenate([own, other], 0), jnp.concatenate([other, own], 0)
        )

    def gather_low(a):
        span = 1
        while span < low_span:
            a = joined((dp // span) % 2, a, swap(a, span))
            span *= 2
        return a

    def scatter_low(a):
        span = low_span // 2
        while span >= 1:
            half = a.shape[0] // 2
            bit = (dp // span) % 2
            give = lax.dynamic_slice_in_dim(a, (1 - bit) * half, half, 0)
            keep = lax.dynamic_slice_in_dim(a, bit * half, half, 0)
            a = (keep.astype(F32) + swap(give, span).astype(F32)).astype(BF)
            span //= 2
        return a

    rows = layer_entries.shape[0]
    docs = passage_lengths_each.shape[0]

    wup_low = gather_low(expand_matrix)
    col_blocks = wup_low.shape[1] // 256
    heads_low = gather_low(nested_projector)
    head_cols = heads_low.shape[1]
    heads_low = jnp.pad(heads_low, ((0, 0), (0, GROUP - head_cols)))
    packed_mlp = jnp.concatenate(
        [wup_low[:, i * 256 : (i + 1) * 256] for i in range(col_blocks)]
        + [
            gather_low(contract_matrix),
            jnp.concatenate([heads_low[: GROUP // 2], heads_low[GROUP // 2 :]], axis=1),
        ],
        axis=0,
    )
    if low_span > 1:
        dp_groups = [
            [((q * 2 + k) * low_span + s) for q in range(QUADS) for k in range(2)]
            for s in range(low_span)
        ]
        mlp_all = lax.all_gather(
            lax.all_gather(packed_mlp, "head"), "dp", axis_index_groups=dp_groups
        )
    else:
        mlp_all = lax.all_gather(packed_mlp, ("dp", "head"))
    mlp_all = mlp_all.reshape((8, n_hd) + packed_mlp.shape)

    partner_rows = swap(layer_entries, pair_mask)
    lens_own = jnp.concatenate([passage_lengths_each, question_lengths])
    lens_partner = swap(lens_own, pair_mask)
    both = jnp.concatenate([layer_entries, partner_rows], axis=0)
    order = [quad ^ r for r in range(QUADS)]
    both_rel = jnp.stack(
        [lax.dynamic_slice(both, (0, order[r] * 256), (2 * rows, 256)) for r in range(QUADS)]
    )

    wide = offset_model_width.shape[1]
    mine = (jnp.arange(n_hd) == hd).astype(BF)
    vectors = jnp.concatenate([offset_model_width, standardize_factor, standardize_offset], axis=0)
    n_vec = vectors.shape[0]
    vectors = gather_low(vectors[None]).transpose(1, 0, 2)
    vectors = (vectors[:, :, None, :] * mine[None, None, :, None]).reshape(n_vec, GROUP)
    middle = gather_low(offset_expanded[None])
    middle = (middle[:, None, :] * mine[None, :, None]).reshape(4, GROUP)
    vectors = jnp.concatenate([vectors, middle, jnp.zeros((16 - n_vec - 4, GROUP), BF)], axis=0)

    wqkv_low = gather_low(triple_projection_matrix)
    parts = wqkv_low.reshape(wqkv_low.shape[0], -1, 2, GROUP)
    keep, give = (
        lax.dynamic_index_in_dim(parts, k, 2, False).reshape(wqkv_low.shape[0], -1)
        for k in (core, 1 - core)
    )
    qkv_cols = keep.shape[1]
    k_rows = keep.shape[0]
    other = jnp.pad(vectors, ((0, 0), (0, qkv_cols - GROUP)))
    other = swap(jnp.concatenate([give, other], axis=0), pair_mask)
    wout_low = gather_low(attention_exit_matrix)
    wout_own = jnp.concatenate([wout_low[:, :GROUP], wout_low[:, GROUP:]], axis=0)
    vectors = jnp.where(
        core == 0,
        jnp.concatenate([vectors, other[k_rows:, :GROUP]], axis=1),
        jnp.concatenate([other[k_rows:, :GROUP], vectors], axis=1),
    )
    packed = jnp.concatenate(
        [
            jnp.concatenate([joined(core, keep, other[:k_rows]), wout_own], axis=1),
            jnp.pad(vectors, ((0, 0), (0, qkv_cols + GROUP - 2 * GROUP))),
        ],
        axis=0,
    )[None]

    a0 = jnp.concatenate([packed, swap(packed, 0, 2)], axis=0)
    b0 = swap(a0, 0, 1)
    ax = swap(a0, x_mask)
    by = swap(b0, y_mask)
    ay = swap(jnp.stack([a0, ax]), y_mask)
    bx = swap(jnp.stack([b0, by]), x_mask)
    attn_pieces = (a0, ax, ay, b0, by, bx)
    spot = jnp.stack([quad, core, hd]).astype(jnp.int32)

    row_ids = jnp.arange(rows, dtype=jnp.int32)
    is_query = hd == 0

    def valid_of(lens):
        doc_here = lens[jnp.maximum(hd - 1, 0)]
        return jnp.where(
            is_query, row_ids % QLEN < jnp.repeat(lens[docs:], QLEN), row_ids < doc_here
        )

    valid = jnp.stack([valid_of(lens_own), valid_of(lens_partner)])
    segment = jnp.where(is_query, row_ids // QLEN, 0)
    position = jnp.where(is_query, row_ids % QLEN, row_ids)
    mask = ((segment[:, None] == segment[None, :])[None] & valid[:, None, :]).astype(F32)
    halfway = HEAD_DIM // 2
    powers = jnp.arange(halfway, dtype=F32) * (2.0 / HEAD_DIM)
    angles = position.astype(F32)[:, None] * (ROPE_BASE ** (-powers))[None, :]
    cosine, sine = jnp.cos(angles), jnp.sin(angles)
    none = jnp.zeros_like(sine)
    cos = jnp.concatenate([cosine] * 4, axis=1)
    sin_a = jnp.concatenate([-sine, none] * 2, axis=1)
    sin_b = jnp.concatenate([none, sine] * 2, axis=1)
    place = jnp.concatenate(
        [
            jnp.stack([quad, hd]).astype(jnp.int32),
            passage_lengths_each,
            core.reshape(1).astype(jnp.int32),
        ]
    ).astype(jnp.int32)
    tokens = 2 * rows

    qkv, att, part, vec = call(
        attention_forward,
        [
            jax.ShapeDtypeStruct((tokens, 3 * D // 2), BF),
            jax.ShapeDtypeStruct((PAIRS, tokens, GROUP), BF),
            jax.ShapeDtypeStruct((tokens, D), F32),
            jax.ShapeDtypeStruct((16, D), F32),
        ],
        [place, both_rel, *attn_pieces, cos, sin_a, sin_b, mask],
        1, 40, cost(0.1), "attention_forward",
    )
    recv = swap(part, pair_mask)
    def up_map(r, s):
        return (0, s[0] ^ r, s[1], 0)

    def down_map(r, s):
        return (2 * (s[0] ^ r) + s[1], 0, 1, 0)

    def const2(r, s):
        return (0, 0)

    up_spec = pl.BlockSpec((8, 1, 256, 256), up_map)
    down_spec = pl.BlockSpec((1, 4, HIDE, 256), down_map)
    scaled_one, inv_one, low_rel, hidden, slope, out_own, out_other = pl.pallas_call(
        feed_forward,
        out_shape=[
            jax.ShapeDtypeStruct((rows, D), F32),
            jax.ShapeDtypeStruct((rows, 1), F32),
            jax.ShapeDtypeStruct((QUADS, tokens, 256), BF),
            jax.ShapeDtypeStruct((QUADS, tokens, HIDE), BF),
            jax.ShapeDtypeStruct((QUADS, tokens, HIDE), BF),
            jax.ShapeDtypeStruct((rows, D), F32),
            jax.ShapeDtypeStruct((rows, D), F32),
        ],
        grid_spec=pltpu.PrefetchScalarGridSpec(
            num_scalar_prefetch=1,
            grid=(QUADS,),
            in_specs=[
                pl.BlockSpec((tokens, D), const2),
                pl.BlockSpec((tokens, D), const2),
                pl.BlockSpec((tokens, D), const2),
                pl.BlockSpec((16, D), const2),
                up_spec,
                down_spec,
            ],
            out_specs=[
                pl.BlockSpec((rows, D), const2),
                pl.BlockSpec((rows, 1), const2),
                pl.BlockSpec((QUADS, tokens, 256), lambda r, s: (0, 0, 0)),
                pl.BlockSpec((1, tokens, HIDE), lambda r, s: (r, 0, 0)),
                pl.BlockSpec((1, tokens, HIDE), lambda r, s: (r, 0, 0)),
                pl.BlockSpec((rows, D), const2),
                pl.BlockSpec((rows, D), const2),
            ],
            scratch_shapes=[pltpu.VMEM((tokens, D), BF)],
        ),
        compiler_params=params(48),
        cost_estimate=cost(12),
        name="feed_forward",
    )(spot, both, part, recv, vec, mlp_all, mlp_all)
    windows = pl.pallas_call(
        make_windows,
        out_shape=jax.ShapeDtypeStruct((D, SLOTS * EMB), BF),
        grid=(1,),
        in_specs=[pl.BlockSpec((8, 4, GROUP // 2, 256), lambda i: (0, 0, 16, 0))],
        out_specs=pl.BlockSpec((D, SLOTS * EMB), lambda i: (0, 0)),
        compiler_params=params(16),
        cost_estimate=cost(1),
        name="make_windows",
    )(mlp_all)
    recv = swap(out_other, pair_mask)
    outputs, scaled_two, inv_two, own_proj = call(
        final_norm,
        [
            jax.ShapeDtypeStruct((rows, D), BF),
            jax.ShapeDtypeStruct((rows, D), F32),
            jax.ShapeDtypeStruct((rows, 1), F32),
            jax.ShapeDtypeStruct((rows, SLOTS * EMB), BF),
        ],
        [scaled_one, out_own, recv, vec, windows],
        0, 16, cost(2.6), "final_norm",
    )
    projs = lax.all_gather(own_proj, "head")
    lanes = jnp.stack(
        [
            jnp.pad(question_lengths.astype(F32), (0, GROUP - question_lengths.shape[0])),
            jnp.pad(relevant_passage.astype(F32), (0, GROUP - relevant_passage.shape[0])),
        ]
    )
    grad_two, low_two, grad_heads, sums_two, scalars = call(
        soft_maxsim,
        [
            jax.ShapeDtypeStruct((rows, D), F32),
            jax.ShapeDtypeStruct((rows, D), BF),
            jax.ShapeDtypeStruct((D, SLOTS * EMB), F32),
            jax.ShapeDtypeStruct((3, D), F32),
            jax.ShapeDtypeStruct((2, GROUP), F32),
        ],
        [place, logarithmic_warmth, lanes, projs, windows, outputs, scaled_two, inv_two, vec],
        2, 24, cost(4.3), "soft_maxsim", [
            pltpu.VMEM((rows, SLOTS * EMB), BF),
            pltpu.VMEM(((docs + 1) * rows, EMB), BF),
            pltpu.VMEM((rows, docs * rows), F32),
            pltpu.VMEM((rows, docs * rows), BF),
        ],
    )

    low_two_other = swap(low_two, pair_mask)

    def swap_head(a, mask):
        return swap(a, 0, mask)

    def finish_split(a, group):
        count = a.shape[0] // 2
        give = lax.dynamic_slice_in_dim(a, (1 - core) * count, count, 0)
        keep = lax.dynamic_slice_in_dim(a, core * count, count, 0)
        other = swap(give, pair_mask)
        keep = keep.reshape(count, -1, 1, group)
        other = other.reshape(count, -1, 1, group)
        whole = jnp.where(
            core == 0,
            jnp.concatenate([keep, other], axis=2),
            jnp.concatenate([other, keep], axis=2),
        ).reshape(count, -1)
        return scatter_low(whole).astype(F32)

    grad_w_heads = jnp.concatenate(
        [grad_heads[:, i * EMB : i * EMB + w] for i, w in enumerate(WIDTHS)], axis=1
    )
    low_two, grad_w_heads = lax.optimization_barrier((low_two, grad_w_heads))
    down_far = weight_grad(
        spot, hidden, (low_two, low_two_other), (1, 3), None, (), "down_far", 0.1
    )
    down_got = swap(down_far, x_mask)
    low_two_next = after(low_two, down_far)
    grad_pre, gn_own, gn_other, bias_up_grad = pl.pallas_call(
        feed_forward_back,
        out_shape=[
            jax.ShapeDtypeStruct((tokens, QUADS * HIDE), BF),
            jax.ShapeDtypeStruct((rows, D), F32),
            jax.ShapeDtypeStruct((rows, D), F32),
            jax.ShapeDtypeStruct((1, QUADS * HIDE), F32),
        ],
        grid_spec=pltpu.PrefetchScalarGridSpec(
            num_scalar_prefetch=1,
            grid=(QUADS,),
            in_specs=[
                pl.BlockSpec((rows, D), const2),
                pl.BlockSpec((rows, D), const2),
                pl.BlockSpec((1, tokens, HIDE), lambda r, s: (r, 0, 0)),
                up_spec,
                down_spec,
            ],
            out_specs=[
                pl.BlockSpec((tokens, HIDE), lambda r, s: (0, s[0] ^ r)),
                pl.BlockSpec((rows, D), const2),
                pl.BlockSpec((rows, D), const2),
                pl.BlockSpec((1, HIDE), lambda r, s: (0, s[0] ^ r)),
            ],
            scratch_shapes=[pltpu.VMEM((tokens, D), BF)],
        ),
        compiler_params=params(40),
        cost_estimate=cost(0.1),
        name="feed_forward_back",
    )(spot, low_two_next, low_two_other, slope, mlp_all, mlp_all)
    up_far = weight_grad(spot, low_rel, (grad_pre,), (2, 3), None, (), "up_far", 0.1)
    up_got = swap(up_far, y_mask)
    recv = swap(gn_other, pair_mask)
    grad_one, low_one, sums_one = call(
        first_norm_back,
        [
            jax.ShapeDtypeStruct((rows, D), F32),
            jax.ShapeDtypeStruct((rows, D), BF),
            jax.ShapeDtypeStruct((3, D), F32),
        ],
        [grad_two, after(gn_own, up_far), recv, scaled_one, inv_one, vec],
        0, 16, cost(0.1), "first_norm_back",
    )
    low_one_other = swap(low_one, pair_mask)
    grad_qkv, gx_own, gx_other, bias_qkv_grad = call(
        attention_backward,
        [
            jax.ShapeDtypeStruct((tokens, 3 * D // 2), BF),
            jax.ShapeDtypeStruct((rows, D), F32),
            jax.ShapeDtypeStruct((rows, D), F32),
            jax.ShapeDtypeStruct((1, 3 * D // 2), F32),
        ],
        [place, low_one, low_one_other, qkv, *attn_pieces, cos, sin_a, sin_b, mask],
        1, 40, cost(0.1), "attention_backward", [pltpu.VMEM((PAIRS, tokens, GROUP), BF)],
    )
    sums = pl.pallas_call(
        pack_sums,
        out_shape=jax.ShapeDtypeStruct((2 * QUADS, 16, GROUP), F32),
        in_specs=[SMEM_SPEC] + [VMEM_SPEC] * 5,
        out_specs=VMEM_SPEC,
        cost_estimate=cost(0.1),
        name="pack_sums",
    )(spot, sums_two, sums_one, bias_up_grad, bias_qkv_grad, scalars)

    def tail(after_this, halves, blocks, places, adds, name, micros, kind=BF):
        return tail_grad(
            spot, both_rel, after(grad_qkv, *after_this), att, low_one, low_one_other,
            halves, blocks, places, adds, name, micros, kind,
        )

    def second(value, *others):
        return (after(value, *others), low_two_other)

    tail_a = tail((), (0,), (1, 3), None, (), "tail_a_far", 0.1)
    a_got = swap(tail_a, x_mask)
    tail_b = tail((tail_a,), (1,), (2, 3), None, (), "tail_b_far", 0.1)
    b_got = swap(tail_b, y_mask)

    down_near = weight_grad(
        spot, hidden, second(low_two, tail_b), (2,), None, ((down_got, 1, True),), "down_near", 12
    )
    down_last = swap(down_near, y_mask)
    up_near = weight_grad(
        spot, low_rel, (after(grad_pre, down_near),), (1,), None, ((up_got, 1, True),), "up_near", 16
    )
    up_last = swap(up_near, x_mask)
    a_near = tail((up_near,), (0,), (2,), None, ((a_got, 1, 0, True),), "tail_a_near", 10)
    a_last = swap(a_near, y_mask)
    b_near = tail((a_near,), (1,), (1,), None, ((b_got, 1, 0, True),), "tail_b_near", 10)
    b_last = swap(b_near, x_mask)

    down_adds = ((down_got, 0, True), (down_last, 0, True))
    up_adds = ((up_got, 0, True), (up_last, 0, True))
    a_adds = ((a_got, 0, 0, True), (a_last, 0, 0, True))
    b_adds = ((b_got, 0, 0, True), (b_last, 0, 0, True))
    down_z = weight_grad(
        spot, hidden, second(low_two, b_near), (0,), (1, 3), down_adds, "down_head", 10
    )
    down_z1 = swap_head(down_z, 1)
    up_z = weight_grad(
        spot, low_rel, (after(grad_pre, down_z),), (0,), (1, 3), up_adds, "up_head", 10
    )
    up_z1 = swap_head(up_z, 1)
    tail_z = tail((up_z,), (0, 1), (0,), (1, 3), a_adds + b_adds, "tail_head", 10)
    tail_z1 = swap_head(tail_z, 1)
    down_zz = weight_grad(
        spot, hidden, second(low_two, tail_z), (0,), (2,),
        down_adds + ((down_z1, 1, False),), "down_head_near", 8,
    )
    down_z2 = swap_head(down_zz, 2)
    up_zz = weight_grad(
        spot, low_rel, (after(grad_pre, down_zz),), (0,), (2,),
        up_adds + ((up_z1, 1, False),), "up_head_near", 8,
    )
    up_z2 = swap_head(up_zz, 2)
    tail_zz = tail(
        (up_zz,), (0, 1), (0,), (2,),
        a_adds + ((tail_z1, 1, 0, False),) + b_adds + ((tail_z1, 1, 1, False),),
        "tail_head_near", 8,
    )
    tail_z2 = swap_head(tail_zz, 2)
    exact = BF if low_span > 1 else F32
    grad_w_down = weight_grad(
        spot, hidden, second(low_two, tail_zz), (0,), (0,),
        down_adds + ((down_z1, 0, False), (down_z2, 0, False)), "down_own", 4, exact,
    )[0]
    up_own = weight_grad(
        spot, low_rel, (after(grad_pre, grad_w_down),), (0,), (0,),
        up_adds + ((up_z1, 0, False), (up_z2, 0, False)), "up_own", 4,
    )[0]
    kept = tail(
        (up_own,), (0, 1), (0,), (0,),
        a_adds + ((tail_z1, 0, 0, False), (tail_z2, 0, 0, False))
        + b_adds + ((tail_z1, 0, 1, False), (tail_z2, 0, 1, False)),
        "tail_own", 4,
    ).reshape(256, 512)
    grad_w_down = scatter_low(grad_w_down).astype(F32)
    grad_w_up = finish_split(up_own, HIDE)
    grad_w_qkv = finish_split(kept[:, :qkv_cols], GROUP)
    kept_out = kept[:, qkv_cols:]
    grad_w_out = scatter_low(
        jnp.concatenate([kept_out[:GROUP], kept_out[GROUP:]], axis=1)
    ).astype(F32)
    head_rows = D // n_dp
    sums = jnp.pad(sums, ((0, 0), (0, 0), (0, n_hd * head_cols - GROUP)))
    sums = jnp.repeat(sums, low_span, axis=0)
    mixed = jnp.concatenate([grad_w_heads.reshape(n_dp, head_rows, -1), sums], axis=1)
    mixed = mixed.reshape(n_dp * (head_rows + 16), -1)
    mixed = lax.psum_scatter(mixed, "dp", scatter_dimension=0, tiled=True)
    sums = mixed[head_rows:, :GROUP].reshape(16, 2, GROUP // 2).transpose(1, 0, 2)
    sums = jnp.pad(sums.reshape(32, GROUP // 2), ((0, 0), (0, head_cols - GROUP // 2)))
    mixed = mixed[:head_rows].reshape(head_rows, n_hd, head_cols).transpose(1, 0, 2)
    mixed = jnp.concatenate([mixed, jnp.broadcast_to(sums, (n_hd,) + sums.shape)], axis=1)
    mixed = lax.psum_scatter(
        mixed.reshape(n_hd * (head_rows + 32), head_cols), "head", scatter_dimension=0, tiled=True
    )
    grad_w_heads = mixed[:head_rows]
    sums = mixed[head_rows:, : GROUP // 2].reshape(2, 16, GROUP // 2).transpose(1, 0, 2)
    sums = sums.reshape(16, GROUP)
    grad_tokens = grad_one + gx_own + swap(gx_other, pair_mask)

    place_in = (dp % low_span) * n_hd + hd
    mat = lax.dynamic_slice(sums[:9], (0, place_in * wide), (9, wide))
    mid = FF // n_all
    up_sum = lax.dynamic_slice(sums[9:13].reshape(-1), (place_in * mid,), (mid,))
    return (
        outputs,
        sums[13, 0:1],
        grad_tokens,
        grad_w_qkv,
        grad_w_out,
        grad_w_up,
        grad_w_down,
        grad_w_heads,
        mat[:5],
        up_sum,
        mat[5:7],
        mat[7:9],
        sums[14, 0:1],
    )


def solution(mesh):
    return jax.shard_map(
        on_device,
        mesh=mesh,
        in_specs=(
            P(("dp", "head"), None),
            P("dp", "head"),
            P("dp", "head"),
            P("dp", "head"),
            P("dp", "head"),
            P("dp", "head"),
            P(None, ("dp", "head")),
            P(("dp", "head")),
            P(None, ("dp", "head")),
            P(None, ("dp", "head")),
            P(),
            P("dp"),
            P("dp"),
            P("dp"),
        ),
        out_specs=(
            P(("dp", "head"), None),
            P(),
            P(("dp", "head"), None),
            P("dp", "head"),
            P("dp", "head"),
            P("dp", "head"),
            P("dp", "head"),
            P("dp", "head"),
            P(None, ("dp", "head")),
            P(("dp", "head")),
            P(None, ("dp", "head")),
            P(None, ("dp", "head")),
            P(),
        ),
        check_vma=False,
    )
```

```python
import jax
import jax.numpy as jnp
from jax import lax
from jax.experimental import pallas as pl
from jax.experimental.pallas import tpu as pltpu
from jax.sharding import PartitionSpec as P

D = 1024
HEADS = 16
HEAD_DIM = 64
FF = 4096
EMB = 128
EMB_MID = 96
EMB_SMALL = 64
QLEN = 32

EPS_NORM = 1e-05
EPS_UNIT = 1e-06
SHARPNESS = 0.05
ROPE_BASE = 10000.0
MASKED = -1000000000.0
SQRT_HALF = 0.7071067811865476
GAUSS_SCALE = 0.3989422804014327

BF = jnp.bfloat16
F32 = jnp.float32
STARTS = (0, EMB, EMB + EMB_MID)
WIDTHS = (EMB, EMB_MID, EMB_SMALL)
SLOTS = 3
QUADS = 4
GROUP = 128
HIDE = FF // 8


PAIRS = 4
VMEM_SPEC = pl.BlockSpec(memory_space=pltpu.VMEM)
SMEM_SPEC = pl.BlockSpec(memory_space=pltpu.SMEM)


def dot_nn(a, b):
    return lax.dot_general(a, b, (((1,), (0,)), ((), ())), preferred_element_type=F32)


def dot_tn(a, b):
    return lax.dot_general(a, b, (((0,), (0,)), ((), ())), preferred_element_type=F32)


def dot_nt(a, b):
    return lax.dot_general(a, b, (((1,), (1,)), ((), ())), preferred_element_type=F32)


def params(mib):
    return pltpu.CompilerParams(vmem_limit_bytes=mib << 20)


TIME_UNIT = 1150000000


def cost(micros):
    return pl.CostEstimate(flops=int(micros * TIME_UNIT), bytes_accessed=1, transcendentals=0)


def whole(a):
    zeros = (0,) * len(a.shape)
    return pl.BlockSpec(a.shape, lambda i: zeros, pipeline_mode=pl.Buffered(1))


def call(kernel, outs, args, n_smem, mib, estimate, name, scratch=()):
    return pl.pallas_call(
        kernel,
        out_shape=outs,
        grid=(1,),
        in_specs=[SMEM_SPEC] * n_smem + [whole(a) for a in args[n_smem:]],
        out_specs=[whole(a) for a in outs],
        scratch_shapes=list(scratch),
        compiler_params=params(mib),
        cost_estimate=estimate,
        name=name,
    )(*args)


def norm_parts(values):
    centred = values - jnp.mean(values, axis=-1, keepdims=True)
    variance = jnp.mean(centred * centred, axis=-1, keepdims=True)
    inverse = lax.rsqrt(variance + EPS_NORM)
    return centred * inverse, inverse


def norm_back(grad_out, scaled, inverse, gain):
    grad_scaled = grad_out * gain
    return inverse * (
        grad_scaled
        - jnp.mean(grad_scaled, axis=-1, keepdims=True)
        - scaled * jnp.mean(grad_scaled * scaled, axis=-1, keepdims=True)
    )


def pieces_of(a0, ax, ay, b0, by, bx):
    def piece(rq, rz):
        at = rz // 2
        if rz % 2 == 0:
            return [a0.at[at], ax.at[at], ay.at[0, at], ay.at[1, at]][rq]
        return [b0.at[at], bx.at[0, at], by.at[at], bx.at[1, at]][rq]

    return piece


def lanes_at(index, width=GROUP):
    return pl.ds(pl.multiple_of(index * width, width), width)


def turn(x, cos, sin_a, sin_b):
    return x * cos + pltpu.roll(x, 96, 1) * sin_a + pltpu.roll(x, 32, 1) * sin_b


def head_mask(h, shape):
    lane = lax.broadcasted_iota(jnp.int32, shape, 1)
    return (lane < HEAD_DIM) if h == 0 else (lane >= HEAD_DIM)


def stacked(a):
    zero = jnp.zeros_like(a)
    return jnp.concatenate(
        [jnp.where(head_mask(0, a.shape), a, zero), jnp.where(head_mask(1, a.shape), a, zero)],
        axis=0,
    )


def unstacked(a):
    half = a.shape[0] // 2
    top = a[:half]
    return jnp.where(head_mask(0, top.shape), top, a[half:])


def softmax_rows(q, k, mask):
    mask = jnp.concatenate([mask, mask], axis=0)
    s = jnp.where(mask > 0, dot_nt(q, k), MASKED)
    raised = jnp.exp(s - jnp.max(s, axis=-1, keepdims=True))
    return raised * (1.0 / jnp.sum(raised, axis=-1, keepdims=True))


def attention_forward(
    place, x, a0, ax, ay, b0, by, bx, cos, sin_a, sin_b, mask, qkv, att, part, vec
):
    quad, hd, core = place[0], place[1], place[5]
    piece = pieces_of(a0, ax, ay, b0, by, bx)
    rows = cos.shape[0]
    for rq in range(4):
        for c in range(2):
            at = slice(c * GROUP, (c + 1) * GROUP)
            total = piece(rq, 0)[256:272, at].astype(F32)
            for rz in range(1, 4):
                total += piece(rq, rz)[256:272, at].astype(F32)
            vec[:, lanes_at(2 * (quad ^ rq) + c)] = total
    for rz in range(4):
        z = hd ^ rz
        acc = dot_nn(x[0], piece(0, rz)[0:256, 0:384])
        for rq in range(1, 4):
            acc += dot_nn(x[rq], piece(rq, rz)[0:256, 0:384])
        for j in range(3):
            i = 3 * z + j
            scale = jnp.where(i < PAIRS, HEAD_DIM**-0.5, 1.0).astype(F32)
            near = vec[0:8, lanes_at(2 * (i % 4) + core)]
            row = lax.broadcasted_iota(jnp.int32, near.shape, 0)
            bias = jnp.sum(jnp.where(row == i // 4, near, 0.0), axis=0, keepdims=True)
            for b in range(2):
                here = acc[b * rows : (b + 1) * rows, j * GROUP : (j + 1) * GROUP]
                here = here + bias
                turned = turn(here, cos[...], sin_a[...], sin_b[...])
                here = jnp.where(i < 2 * PAIRS, turned, here) * scale
                qkv[b * rows : (b + 1) * rows, lanes_at(i)] = here.astype(BF)

    def one(it, carry):
        b, r = it // PAIRS, it % PAIRS
        i = quad ^ r
        row = pl.ds(pl.multiple_of(b * rows, rows), rows)
        q = qkv[row, pl.ds(pl.multiple_of(i * GROUP, GROUP), GROUP)]
        k = qkv[row, pl.ds(pl.multiple_of((PAIRS + i) * GROUP, GROUP), GROUP)]
        v = qkv[row, pl.ds(pl.multiple_of((2 * PAIRS + i) * GROUP, GROUP), GROUP)]
        probs = softmax_rows(stacked(q), k, mask[b])
        both = dot_nn(probs.astype(BF), v)
        att[r, row, :] = unstacked(both).astype(BF)
        return carry

    lax.fori_loop(0, 2 * PAIRS, one, 0)
    for rz in range(4):
        for half in range(2):
            sel = slice(half * GROUP, (half + 1) * GROUP)
            acc = dot_nn(att[0], piece(0, rz)[sel, 384:512])
            for rq in range(1, 4):
                acc += dot_nn(att[rq], piece(rq, rz)[sel, 384:512])
            part[:, lanes_at(2 * (hd ^ rz) + half)] = acc


def attention_backward(
    place, own, other, qkv, a0, ax, ay, b0, by, bx, cos, sin_a, sin_b, mask,
    grad_qkv, gx_own, gx_other, sums, ga,
):
    quad, hd = place[0], place[1]
    piece = pieces_of(a0, ax, ay, b0, by, bx)
    rows = cos.shape[0]
    for b, grad in ((0, own), (1, other)):
        for rq in range(4):
            acc = None
            for rz in range(4):
                for half in range(2):
                    w = piece(rq, rz)[half * GROUP : (half + 1) * GROUP, 384:512]
                    term = dot_nt(grad[:, lanes_at(2 * (hd ^ rz) + half)], w)
                    acc = term if acc is None else acc + term
            ga[rq, b * rows : (b + 1) * rows, :] = acc.astype(BF)

    def one(it, carry):
        b, r = it // PAIRS, it % PAIRS
        i = quad ^ r
        row = pl.ds(pl.multiple_of(b * rows, rows), rows)
        at_q = pl.ds(pl.multiple_of(i * GROUP, GROUP), GROUP)
        at_k = pl.ds(pl.multiple_of((PAIRS + i) * GROUP, GROUP), GROUP)
        at_v = pl.ds(pl.multiple_of((2 * PAIRS + i) * GROUP, GROUP), GROUP)
        q, k, v = qkv[row, at_q], qkv[row, at_k], qkv[row, at_v]
        q_pair, grad_pair = stacked(q), stacked(ga[r, row, :])
        probs = softmax_rows(q_pair, k, mask[b])
        gp = dot_nt(grad_pair, v)
        gs = probs * (gp - jnp.sum(probs * gp, axis=-1, keepdims=True))
        gs = gs.astype(BF)
        gq = unstacked(dot_nn(gs, k))
        gk = dot_tn(gs, q_pair)
        gv = dot_tn(probs.astype(BF), grad_pair)
        c, sa, sb = cos[...], -sin_a[...], -sin_b[...]
        grad_qkv[row, at_q] = turn(gq * (HEAD_DIM**-0.5), c, sa, sb).astype(BF)
        grad_qkv[row, at_k] = turn(gk, c, sa, sb).astype(BF)
        grad_qkv[row, at_v] = gv.astype(BF)
        return carry

    lax.fori_loop(0, 2 * PAIRS, one, 0)
    for rq in range(4):
        at = pl.ds(pl.multiple_of((quad ^ rq) * 256, 256), 256)
        acc = None
        for rz in range(4):
            cols = pl.ds(pl.multiple_of((hd ^ rz) * 384, GROUP), 384)
            term = dot_nt(grad_qkv[:, cols], piece(rq, rz)[0:256, 0:384])
            acc = term if acc is None else acc + term
        gx_own[:, at] = acc[:rows]
        gx_other[:, at] = acc[rows:]
    sums[...] = jnp.sum(grad_qkv[...].astype(F32), axis=0, keepdims=True)


def feed_forward(
    place, x, part, recv, vec, wup, wdown,
    scaled_out, inv_out, rel_out, hidden_out, slope_out, own_out, other_out, low,
):
    r = pl.program_id(0)
    rows = scaled_out.shape[0]

    @pl.when(r == 0)
    def _():
        for b in range(2):
            sel = slice(b * rows, (b + 1) * rows)
            swapped = slice((1 - b) * rows, (2 - b) * rows)
            h = x[sel, :].astype(F32) + part[sel, :] + recv[swapped, :] + vec[3:4, :]
            scaled, inverse = norm_parts(h)
            low[sel, :] = (scaled * vec[5:6, :] + vec[7:8, :]).astype(BF)
            if b == 0:
                scaled_out[...] = scaled
                inv_out[...] = inverse
        for q in range(QUADS):
            at = pl.ds(pl.multiple_of((place[0] ^ q) * 256, 256), 256)
            rel_out[q, :, :] = low[:, at]
        own_out[...] = jnp.zeros_like(own_out)
        other_out[...] = jnp.zeros_like(other_out)

    for cb in range(2):
        cols = slice(cb * 256, (cb + 1) * 256)
        w = wup[:, 0, cb * 128 : (cb + 1) * 128, :].reshape(D, 256)
        bias = [
            vec[9 + 2 * cb + k : 10 + 2 * cb + k, lanes_at(2 * (place[0] ^ r) + place[1])]
            for k in range(2)
        ]
        pre = dot_nn(low[...], w) + jnp.concatenate(bias, axis=1)
        gate = 0.5 * (1.0 + lax.erf(pre * SQRT_HALF))
        hidden_out[0, :, cols] = (pre * gate).astype(BF)
        slope_out[0, :, cols] = (
            gate + pre * jnp.exp(-0.5 * pre * pre) * GAUSS_SCALE
        ).astype(BF)
    for z in range(4):
        cols = slice(z * 256, (z + 1) * 256)
        acc = dot_nn(hidden_out[0], wdown[0, z])
        own_out[:, cols] += acc[:rows]
        other_out[:, cols] += acc[rows:]


def feed_forward_back(
    place, own, other, slope, wup, wdown, pre_out, own_out, other_out, sums, both
):
    r = pl.program_id(0)
    rows = own.shape[0]

    @pl.when(r == 0)
    def _():
        both[0:rows, :] = own[...]
        both[rows:, :] = other[...]
        own_out[...] = jnp.zeros_like(own_out)
        other_out[...] = jnp.zeros_like(other_out)

    acc = dot_nt(both[:, 0:256], wdown[0, 0])
    for z in range(1, 4):
        acc += dot_nt(both[:, z * 256 : (z + 1) * 256], wdown[0, z])
    grad = (acc * slope[0].astype(F32)).astype(BF)
    pre_out[...] = grad
    sums[...] = jnp.sum(grad.astype(F32), axis=0, keepdims=True)
    total = None
    for cb in range(2):
        w = wup[:, 0, cb * 128 : (cb + 1) * 128, :].reshape(D, 256)
        term = dot_nt(pre_out[:, cb * 256 : (cb + 1) * 256], w)
        total = term if total is None else total + term
    own_out[...] += total[:rows]
    other_out[...] += total[rows:]


def final_norm(scaled_one, part, recv, vec, windows, out, scaled_out, inv_out, proj):
    h = scaled_one[...] * vec[5:6, :] + vec[7:8, :] + part[...] + recv[...] + vec[4:5, :]
    scaled, inverse = norm_parts(h)
    scaled_out[...] = scaled
    inv_out[...] = inverse
    low = (scaled * vec[6:7, :] + vec[8:9, :]).astype(BF)
    out[...] = low
    proj[...] = dot_nt(windows[...], low).astype(BF)


def soft_maxsim(
    place, temp, lanes, proj_0, proj_1, proj_2, proj_3, windows, out, scaled, inverse_two, vec,
    grad_two, low_two, grad_heads, sums, scalars, gproj, units, shares, similar_low,
):
    hd = place[1]
    rows = out.shape[0]
    projs = (proj_0, proj_1, proj_2, proj_3)
    docs = len(projs) - 1
    row = lax.broadcasted_iota(jnp.int32, (rows, GROUP), 0)
    lane = lax.broadcasted_iota(jnp.int32, (rows, GROUP), 1)
    member = (row // QLEN == lane).astype(F32)
    lens = lanes[0:1, :]
    len_row = jnp.sum(member * lens, axis=1, keepdims=True)
    valid = (row % QLEN).astype(F32) < len_row
    queries = rows // QLEN
    used = lax.broadcasted_iota(jnp.int32, (1, GROUP), 1) < queries
    weight = jnp.where(valid, member, 0.0) / jnp.where(used, lens, 1.0)
    warmth = jnp.exp(jnp.full((1, GROUP), temp[0], F32))
    key = lax.broadcasted_iota(jnp.int32, (rows, rows), 1)
    loss = jnp.zeros((1, GROUP), F32)
    grad_temp = jnp.zeros((1, GROUP), F32)
    for slot in range(SLOTS):
        width = WIDTHS[slot]
        cols = slice(STARTS[slot], STARTS[slot] + width)

        def unit_of(away):
            mapped = projs[away][cols, :].astype(F32)
            inverse = lax.rsqrt(jnp.sum(mapped * mapped, axis=0, keepdims=True) + EPS_UNIT)
            return mapped * inverse, inverse

        for away in range(docs + 1):
            units[0:width, lanes_at(hd ^ away, rows)] = unit_of(away)[0].astype(BF)
        logits = []
        for d in range(docs):
            doc = slice((d + 1) * rows, (d + 2) * rows)
            similar = dot_tn(units[0:width, 0:rows], units[0:width, doc]) * (1.0 / SHARPNESS)
            similar = jnp.where(key < place[2 + d], similar, MASKED)
            top = jnp.max(similar, axis=-1, keepdims=True)
            raised = jnp.exp(similar - top)
            total = jnp.sum(raised, axis=-1, keepdims=True)
            soft = SHARPNESS * (top + jnp.log(total))
            shares[:, d * rows : (d + 1) * rows] = raised * (1.0 / total)
            logits.append(jnp.sum(soft * weight, axis=0, keepdims=True) / warmth)
        top_logit = jnp.maximum(jnp.maximum(logits[0], logits[1]), logits[2])
        exps = [jnp.exp(x - top_logit) for x in logits]
        total = exps[0] + exps[1] + exps[2]
        hits = [(lanes[1:2, :] == float(d)).astype(F32) for d in range(docs)]
        picked = logits[0] * hits[0] + logits[1] * hits[1] + logits[2] * hits[2]
        loss += jnp.where(used, top_logit + jnp.log(total) - picked, 0.0) / queries
        for d in range(docs):
            grad = jnp.where(used, exps[d] / total - hits[d], 0.0) / queries
            grad_temp -= grad * logits[d]
            grad_soft = jnp.sum(weight * (grad / warmth), axis=1, keepdims=True)
            at = slice(d * rows, (d + 1) * rows)
            similar_low[:, at] = (grad_soft * shares[:, at]).astype(BF)

        own = jnp.maximum(hd - 1, 0)
        at = pl.ds(pl.multiple_of(own * rows, rows), rows)
        from_docs = dot_nt(units[0:width, rows:], similar_low[...])
        from_queries = dot_nn(units[0:width, 0:rows], similar_low[:, at])
        grad = jnp.where(hd == 0, from_docs, from_queries)
        unit, inverse = unit_of(0)
        gproj[cols, :] = (
            inverse * (grad - unit * jnp.sum(grad * unit, axis=0, keepdims=True))
        ).astype(BF)

    scalars[0:1, :] = loss
    scalars[1:2, :] = grad_temp
    grad_final = dot_tn(gproj[...], windows[...])
    xhat = scaled[...]
    grad = norm_back(grad_final, xhat, inverse_two[...], vec[6:7, :])
    grad_two[...] = grad
    low_two[...] = grad.astype(BF)
    sums[0:1, :] = jnp.sum(grad_final * xhat, axis=0, keepdims=True)
    sums[1:2, :] = jnp.sum(grad_final, axis=0, keepdims=True)
    sums[2:3, :] = jnp.sum(low_two[...].astype(F32), axis=0, keepdims=True)
    heads = dot_nn(gproj[...], out[...])
    for t in range(2 * QUADS):
        grad_heads[t] = heads[:, t * GROUP : (t + 1) * GROUP]


def first_norm_back(grad_two, own, recv, scaled, inverse, vec, grad_one, low_one, sums):
    grad_out = grad_two[...] + own[...] + recv[...]
    xhat = scaled[...]
    grad = norm_back(grad_out, xhat, inverse[...], vec[5:6, :])
    grad_one[...] = grad
    low_one[...] = grad.astype(BF)
    sums[0:1, :] = jnp.sum(grad_out * xhat, axis=0, keepdims=True)
    sums[1:2, :] = jnp.sum(grad_out, axis=0, keepdims=True)
    sums[2:3, :] = jnp.sum(low_one[...].astype(F32), axis=0, keepdims=True)


def weight_grad(spot, lhs, rhs, blocks, places, adds, name, micros, kind=BF):
    tokens, width = lhs.shape[1:]
    whole_cols = places is None
    places = (None,) if whole_cols else places
    count = len(places)
    tile = rhs[0].shape[1] // (1 if whole_cols else 4)
    step = (blocks[1] - blocks[0]) if len(blocks) > 1 else 0
    parts = len(rhs)
    span = tokens // parts
    n_add = len(adds)

    def column(s, place):
        return 0 if place is None else s[2] ^ place

    def kernel(spot_ref, lhs_ref, *refs):
        out = refs[-1]
        for k in range(count):
            total = None
            for p in range(parts):
                term = dot_tn(lhs_ref[0, p * span : (p + 1) * span, :], refs[k * parts + p][...])
                total = term if total is None else total + term
            for add in refs[count * parts + k * n_add : count * parts + (k + 1) * n_add]:
                total += add[0].astype(F32)
            out[k] = total.astype(kind)

    specs = [pl.BlockSpec((1, tokens, width), lambda i, s: (blocks[0] + step * i, 0, 0))]
    for place in places:
        specs += [pl.BlockSpec((span, tile), lambda i, s, c=place: (0, column(s, c)))] * parts
    for k, place in enumerate(places):
        for _, at, per_block, per_place, aligned in adds:
            at += per_place * k
            if aligned:
                index = lambda i, s, at=at, n=per_block, c=place: (at + n * i, 0, column(s, c))
            else:
                index = lambda i, s, at=at, n=per_block: (at + n * i, 0, 0)
            specs.append(pl.BlockSpec((1, width, tile), index))
    return pl.pallas_call(
        kernel,
        out_shape=jax.ShapeDtypeStruct((len(blocks) * count, width, tile), kind),
        grid_spec=pltpu.PrefetchScalarGridSpec(
            num_scalar_prefetch=1,
            grid=(len(blocks),),
            in_specs=specs,
            out_specs=pl.BlockSpec((count, width, tile), lambda i, s: (i, 0, 0)),
        ),
        compiler_params=params(24),
        cost_estimate=cost(micros),
        name=name,
    )(spot, lhs, *(list(rhs) * count), *([add[0] for add in adds] * count))


def tail_grad(spot, x, grad_qkv, att, own, other, halves, blocks, places, adds, name, micros, kind=BF):
    tokens = x.shape[1]
    whole_cols = places is None
    places = (None,) if whole_cols else places
    count = len(places)
    heads = 4 if whole_cols else 1
    step = (blocks[1] - blocks[0]) if len(blocks) > 1 else 0
    n_half = len(halves)
    rows = tokens // 2
    n_add = len(adds)
    per = n_add // n_half
    lane_blocks = 1 if whole_cols else n_half

    def column(s, place):
        return 0 if place is None else s[2] ^ place

    def kernel(spot_ref, x_ref, att_ref, *refs):
        out = refs[-1]
        at_add = count * (1 + 2 * lane_blocks)
        for c in range(count):
            qkv_ref, *pair = refs[c * (1 + 2 * lane_blocks) : (c + 1) * (1 + 2 * lane_blocks)]
            for k, half in enumerate(halves):
                left_all = dot_tn(x_ref[0, :, half * GROUP : (half + 1) * GROUP], qkv_ref[...])
                for z in range(heads):
                    if whole_cols:
                        lanes = slice((2 * z + half) * GROUP, (2 * z + half + 1) * GROUP)
                        up, down = pair[0][:, lanes], pair[1][:, lanes]
                    else:
                        up, down = pair[2 * k][...], pair[2 * k + 1][...]
                    right = dot_tn(att_ref[0, 0:rows, :], up) + dot_tn(att_ref[0, rows:, :], down)
                    left = left_all[:, z * 384 : (z + 1) * 384]
                    first = at_add + c * n_add + k * per
                    lo = z * 512
                    for add in refs[first : first + per]:
                        left += add[0, 0, :, lo : lo + 384].astype(F32)
                        right += add[0, 0, :, lo + 384 : lo + 512].astype(F32)
                    out[c, k, :, lo : lo + 384] = left.astype(kind)
                    out[c, k, :, lo + 384 : lo + 512] = right.astype(kind)

    specs = [
        pl.BlockSpec((1, tokens, 256), lambda i, s: (blocks[0] + step * i, 0, 0)),
        pl.BlockSpec((1, tokens, GROUP), lambda i, s: (blocks[0] + step * i, 0, 0)),
    ]
    inputs = []
    for place in places:
        specs.append(pl.BlockSpec((tokens, 384 * heads), lambda i, s, c=place: (0, column(s, c))))
        inputs.append(grad_qkv)
        for half in halves[:lane_blocks]:
            if whole_cols:
                index = lambda i, s: (0, 0)
            else:
                index = lambda i, s, c=place, half=half: (0, 2 * column(s, c) + half)
            specs += [pl.BlockSpec((rows, D if whole_cols else GROUP), index)] * 2
            inputs += [own, other]
    for place in places:
        for a, at, k, aligned in adds:
            if aligned:
                index = lambda i, s, at=at, k=k, c=place: (at, k, 0, column(s, c))
            else:
                index = lambda i, s, at=at, k=k: (at, k, 0, 0)
            specs.append(pl.BlockSpec((1, 1, GROUP, 512 * heads), index))
            inputs.append(a)
    return pl.pallas_call(
        kernel,
        out_shape=jax.ShapeDtypeStruct((len(blocks) * count, n_half, GROUP, 512 * heads), kind),
        grid_spec=pltpu.PrefetchScalarGridSpec(
            num_scalar_prefetch=1,
            grid=(len(blocks),),
            in_specs=specs,
            out_specs=pl.BlockSpec(
                (count, n_half, GROUP, 512 * heads), lambda i, s: (i, 0, 0, 0)
            ),
        ),
        compiler_params=params(24),
        cost_estimate=cost(micros),
        name=name,
    )(spot, x, att, *inputs)


def tail_pair(x, grad_qkv, att, own, other, jobs, adds, name, micros):
    tokens = x.shape[1]
    rows = tokens // 2

    def kernel(x_ref, qkv_ref, att_ref, own_ref, other_ref, *refs):
        for n, blocks in enumerate(jobs):
            out = refs[len(adds) + n]
            for k, (r, half) in enumerate(blocks):
                left_all = dot_tn(x_ref[r, :, half * GROUP : (half + 1) * GROUP], qkv_ref[...])
                for z in range(4):
                    lanes = slice((2 * z + half) * GROUP, (2 * z + half + 1) * GROUP)
                    right = dot_tn(att_ref[r, 0:rows, :], own_ref[:, lanes])
                    right += dot_tn(att_ref[r, rows:, :], other_ref[:, lanes])
                    left = left_all[:, z * 384 : (z + 1) * 384]
                    lo = z * 512
                    if adds:
                        left += refs[n][0, 0, :, lo : lo + 384].astype(F32)
                        right += refs[n][0, 0, :, lo + 384 : lo + 512].astype(F32)
                    out[k, 0, :, lo : lo + 384] = left.astype(BF)
                    out[k, 0, :, lo + 384 : lo + 512] = right.astype(BF)

    outs = [jax.ShapeDtypeStruct((len(blocks), 1, GROUP, 2048), BF) for blocks in jobs]
    specs = [whole(a) for a in (x, grad_qkv, att, own, other)]
    specs += [pl.BlockSpec((1, 1, GROUP, 2048), lambda i: (1, 0, 0, 0))] * len(adds)
    return pl.pallas_call(
        kernel,
        out_shape=outs,
        grid=(1,),
        in_specs=specs,
        out_specs=[whole(a) for a in outs],
        compiler_params=params(40),
        cost_estimate=cost(micros),
        name=name,
    )(x, grad_qkv, att, own, other, *adds)


def pack_sums(spot, two, one, up, qkv, scalars, out):
    core, hd = spot[1], spot[2]
    out[...] = jnp.zeros_like(out)
    for i in range(3 * PAIRS):
        out[2 * (i % 4) + core, i // 4 : i // 4 + 1, :] = qkv[0:1, i * GROUP : (i + 1) * GROUP]
    for i in range(4 * QUADS):
        out[2 * (i // 4) + core, 9 + i % 4 : 10 + i % 4, :] = up[
            0:1, i * GROUP : (i + 1) * GROUP
        ]
    once = jnp.where(hd == 0, 1.0, 0.0).astype(F32)
    totals = [jnp.sum(scalars[k : k + 1, :], axis=1, keepdims=True) * once for k in range(2)]
    for t in range(2 * QUADS):
        at = slice(t * GROUP, (t + 1) * GROUP)
        out[t, 3:4, :] = one[2:3, at]
        out[t, 4:5, :] = two[2:3, at]
        out[t, 5:6, :] = one[0:1, at]
        out[t, 6:7, :] = two[0:1, at]
        out[t, 7:8, :] = one[1:2, at]
        out[t, 8:9, :] = two[1:2, at]
        for k in range(2):
            out[t, 13 + k : 14 + k, :] = jnp.broadcast_to(totals[k], (1, GROUP))


def make_windows(tiles, windows, wide):
    cols = windows.shape[0] // 4
    for dp in range(2 * QUADS):
        at = slice(dp * GROUP, (dp + 1) * GROUP)
        for z in range(4):
            lo = z * cols
            wide[lo : lo + 64, at] = tiles[dp, z, :, 0:GROUP].astype(F32)
            rest = tiles[dp, z, 0:16, GROUP:].astype(F32)
            wide[lo + 64 : lo + cols, at] = rest[0 : cols - 64, :]
    windows[...] = wide[...].astype(BF)


def on_device(
    layer_entries,
    triple_projection_matrix,
    attention_exit_matrix,
    expand_matrix,
    contract_matrix,
    nested_projector,
    offset_model_width,
    offset_expanded,
    standardize_factor,
    standardize_offset,
    logarithmic_warmth,
    passage_lengths_each,
    question_lengths,
    relevant_passage,
):
    n_dp = lax.axis_size("dp")
    n_hd = lax.axis_size("head")
    n_all = n_dp * n_hd
    dp = lax.axis_index("dp")
    hd = lax.axis_index("head")
    low_span = n_dp // 8
    quad = dp // (2 * low_span)
    core = (dp // low_span) % 2
    pair_mask = low_span
    x_mask = 2 * low_span
    y_mask = 4 * low_span

    def swap(a, dp_mask=0, hd_mask=0):
        pairs = [
            (d * n_hd + h, (d ^ dp_mask) * n_hd + (h ^ hd_mask))
            for d in range(n_dp)
            for h in range(n_hd)
        ]
        return lax.ppermute(a, ("dp", "head"), pairs)

    def after(value, *others):
        return lax.optimization_barrier((value, *others))[0]

    def joined(bit, own, other):
        return jnp.where(
            bit == 0, jnp.concatenate([own, other], 0), jnp.concatenate([other, own], 0)
        )

    def gather_low(a):
        span = 1
        while span < low_span:
            a = joined((dp // span) % 2, a, swap(a, span))
            span *= 2
        return a

    def scatter_low(a):
        span = low_span // 2
        while span >= 1:
            half = a.shape[0] // 2
            bit = (dp // span) % 2
            give = lax.dynamic_slice_in_dim(a, (1 - bit) * half, half, 0)
            keep = lax.dynamic_slice_in_dim(a, bit * half, half, 0)
            a = (keep.astype(F32) + swap(give, span).astype(F32)).astype(BF)
            span //= 2
        return a

    rows = layer_entries.shape[0]
    docs = passage_lengths_each.shape[0]

    wup_low = gather_low(expand_matrix)
    col_blocks = wup_low.shape[1] // 256
    heads_low = gather_low(nested_projector)
    head_cols = heads_low.shape[1]
    heads_low = jnp.pad(heads_low.T, ((0, GROUP - head_cols), (0, 0)))
    packed_mlp = jnp.concatenate(
        [wup_low[:, i * 256 : (i + 1) * 256] for i in range(col_blocks)]
        + [
            gather_low(contract_matrix),
            jnp.concatenate([heads_low[:64], heads_low[64:]], axis=1),
        ],
        axis=0,
    )
    if low_span > 1:
        dp_groups = [
            [((q * 2 + k) * low_span + s) for q in range(QUADS) for k in range(2)]
            for s in range(low_span)
        ]
        mlp_all = lax.all_gather(
            lax.all_gather(packed_mlp, "head"), "dp", axis_index_groups=dp_groups
        )
    else:
        mlp_all = lax.all_gather(packed_mlp, ("dp", "head"))
    mlp_all = mlp_all.reshape((8, n_hd) + packed_mlp.shape)

    partner_rows = swap(layer_entries, pair_mask)
    lens_own = jnp.concatenate([passage_lengths_each, question_lengths])
    lens_partner = swap(lens_own, pair_mask)
    both = jnp.concatenate([layer_entries, partner_rows], axis=0)
    order = [quad ^ r for r in range(QUADS)]
    both_rel = jnp.stack(
        [lax.dynamic_slice(both, (0, order[r] * 256), (2 * rows, 256)) for r in range(QUADS)]
    )

    wide = offset_model_width.shape[1]
    mine = (jnp.arange(n_hd) == hd).astype(BF)
    vectors = jnp.concatenate([offset_model_width, standardize_factor, standardize_offset], axis=0)
    n_vec = vectors.shape[0]
    vectors = gather_low(vectors[None]).transpose(1, 0, 2)
    vectors = (vectors[:, :, None, :] * mine[None, None, :, None]).reshape(n_vec, GROUP)
    middle = gather_low(offset_expanded[None])
    middle = (middle[:, None, :] * mine[None, :, None]).reshape(4, GROUP)
    vectors = jnp.concatenate([vectors, middle, jnp.zeros((16 - n_vec - 4, GROUP), BF)], axis=0)

    wqkv_low = gather_low(triple_projection_matrix)
    parts = wqkv_low.reshape(wqkv_low.shape[0], -1, 2, GROUP)
    keep, give = (
        lax.dynamic_index_in_dim(parts, k, 2, False).reshape(wqkv_low.shape[0], -1)
        for k in (core, 1 - core)
    )
    qkv_cols = keep.shape[1]
    k_rows = keep.shape[0]
    other = jnp.pad(vectors, ((0, 0), (0, qkv_cols - GROUP)))
    other = swap(jnp.concatenate([give, other], axis=0), pair_mask)
    wout_low = gather_low(attention_exit_matrix)
    wout_own = jnp.concatenate([wout_low[:, :GROUP], wout_low[:, GROUP:]], axis=0)
    vectors = jnp.where(
        core == 0,
        jnp.concatenate([vectors, other[k_rows:, :GROUP]], axis=1),
        jnp.concatenate([other[k_rows:, :GROUP], vectors], axis=1),
    )
    packed = jnp.concatenate(
        [
            jnp.concatenate([joined(core, keep, other[:k_rows]), wout_own], axis=1),
            jnp.pad(vectors, ((0, 0), (0, qkv_cols + GROUP - 2 * GROUP))),
        ],
        axis=0,
    )[None]

    a0 = jnp.concatenate([packed, swap(packed, 0, 2)], axis=0)
    b0 = swap(a0, 0, 1)
    ax = swap(a0, x_mask)
    by = swap(b0, y_mask)
    ay = swap(jnp.stack([a0, ax]), y_mask)
    bx = swap(jnp.stack([b0, by]), x_mask)
    attn_pieces = (a0, ax, ay, b0, by, bx)
    spot = jnp.stack([quad, core, hd]).astype(jnp.int32)

    row_ids = jnp.arange(rows, dtype=jnp.int32)
    is_query = hd == 0

    def valid_of(lens):
        doc_here = lens[jnp.maximum(hd - 1, 0)]
        return jnp.where(
            is_query, row_ids % QLEN < jnp.repeat(lens[docs:], QLEN), row_ids < doc_here
        )

    valid = jnp.stack([valid_of(lens_own), valid_of(lens_partner)])
    segment = jnp.where(is_query, row_ids // QLEN, 0)
    position = jnp.where(is_query, row_ids % QLEN, row_ids)
    mask = ((segment[:, None] == segment[None, :])[None] & valid[:, None, :]).astype(F32)
    halfway = HEAD_DIM // 2
    powers = jnp.arange(halfway, dtype=F32) * (2.0 / HEAD_DIM)
    angles = position.astype(F32)[:, None] * (ROPE_BASE ** (-powers))[None, :]
    cosine, sine = jnp.cos(angles), jnp.sin(angles)
    none = jnp.zeros_like(sine)
    cos = jnp.concatenate([cosine] * 4, axis=1)
    sin_a = jnp.concatenate([-sine, none] * 2, axis=1)
    sin_b = jnp.concatenate([none, sine] * 2, axis=1)
    place = jnp.concatenate(
        [
            jnp.stack([quad, hd]).astype(jnp.int32),
            passage_lengths_each,
            core.reshape(1).astype(jnp.int32),
        ]
    ).astype(jnp.int32)
    tokens = 2 * rows

    qkv, att, part, vec = call(
        attention_forward,
        [
            jax.ShapeDtypeStruct((tokens, 3 * D // 2), BF),
            jax.ShapeDtypeStruct((PAIRS, tokens, GROUP), BF),
            jax.ShapeDtypeStruct((tokens, D), F32),
            jax.ShapeDtypeStruct((16, D), F32),
        ],
        [place, both_rel, *attn_pieces, cos, sin_a, sin_b, mask],
        1, 58, cost(0.1), "attention_forward",
    )
    recv = swap(part, pair_mask)
    def up_map(r, s):
        return (0, s[0] ^ r, s[1], 0)

    def down_map(r, s):
        return (2 * (s[0] ^ r) + s[1], 0, 1, 0)

    def const2(r, s):
        return (0, 0)

    up_spec = pl.BlockSpec((8, 1, 256, 256), up_map)
    down_spec = pl.BlockSpec((1, 4, HIDE, 256), down_map)
    scaled_one, inv_one, low_rel, hidden, slope, out_own, out_other = pl.pallas_call(
        feed_forward,
        out_shape=[
            jax.ShapeDtypeStruct((rows, D), F32),
            jax.ShapeDtypeStruct((rows, 1), F32),
            jax.ShapeDtypeStruct((QUADS, tokens, 256), BF),
            jax.ShapeDtypeStruct((QUADS, tokens, HIDE), BF),
            jax.ShapeDtypeStruct((QUADS, tokens, HIDE), BF),
            jax.ShapeDtypeStruct((rows, D), F32),
            jax.ShapeDtypeStruct((rows, D), F32),
        ],
        grid_spec=pltpu.PrefetchScalarGridSpec(
            num_scalar_prefetch=1,
            grid=(QUADS,),
            in_specs=[
                pl.BlockSpec((tokens, D), const2),
                pl.BlockSpec((tokens, D), const2),
                pl.BlockSpec((tokens, D), const2),
                pl.BlockSpec((16, D), const2),
                up_spec,
                down_spec,
            ],
            out_specs=[
                pl.BlockSpec((rows, D), const2),
                pl.BlockSpec((rows, 1), const2),
                pl.BlockSpec((QUADS, tokens, 256), lambda r, s: (0, 0, 0)),
                pl.BlockSpec((1, tokens, HIDE), lambda r, s: (r, 0, 0)),
                pl.BlockSpec((1, tokens, HIDE), lambda r, s: (r, 0, 0)),
                pl.BlockSpec((rows, D), const2),
                pl.BlockSpec((rows, D), const2),
            ],
            scratch_shapes=[pltpu.VMEM((tokens, D), BF)],
        ),
        compiler_params=params(58),
        cost_estimate=cost(12),
        name="feed_forward",
    )(spot, both, part, recv, vec, mlp_all, mlp_all)
    all_cols = n_hd * head_cols
    windows = pl.pallas_call(
        make_windows,
        out_shape=jax.ShapeDtypeStruct((all_cols, D), BF),
        grid=(1,),
        in_specs=[pl.BlockSpec((8, 4, 64, 256), lambda i: (0, 0, 16, 0))],
        out_specs=pl.BlockSpec((all_cols, D), lambda i: (0, 0)),
        scratch_shapes=[pltpu.VMEM((all_cols, D), F32)],
        compiler_params=params(58),
        cost_estimate=cost(1),
        name="make_windows",
    )(mlp_all)
    recv = swap(out_other, pair_mask)
    outputs, scaled_two, inv_two, own_proj = call(
        final_norm,
        [
            jax.ShapeDtypeStruct((rows, D), BF),
            jax.ShapeDtypeStruct((rows, D), F32),
            jax.ShapeDtypeStruct((rows, 1), F32),
            jax.ShapeDtypeStruct((all_cols, rows), BF),
        ],
        [scaled_one, out_own, recv, vec, windows],
        0, 16, cost(2.6), "final_norm",
    )
    projs = [own_proj] + [swap(own_proj, 0, k) for k in range(1, n_hd)]
    lanes = jnp.stack(
        [
            jnp.pad(question_lengths.astype(F32), (0, GROUP - question_lengths.shape[0])),
            jnp.pad(relevant_passage.astype(F32), (0, GROUP - relevant_passage.shape[0])),
        ]
    )
    grad_two, low_two, grad_heads, sums_two, scalars = call(
        soft_maxsim,
        [
            jax.ShapeDtypeStruct((rows, D), F32),
            jax.ShapeDtypeStruct((rows, D), BF),
            jax.ShapeDtypeStruct((2 * QUADS, all_cols, GROUP), F32),
            jax.ShapeDtypeStruct((3, D), F32),
            jax.ShapeDtypeStruct((2, GROUP), F32),
        ],
        [place, logarithmic_warmth, lanes, *projs, windows, outputs, scaled_two, inv_two, vec],
        2, 24, cost(4.3), "soft_maxsim", [
            pltpu.VMEM((all_cols, rows), BF),
            pltpu.VMEM((EMB, (docs + 1) * rows), BF),
            pltpu.VMEM((rows, docs * rows), F32),
            pltpu.VMEM((rows, docs * rows), BF),
        ],
    )

    low_two_other = swap(low_two, pair_mask)

    def swap_head(a, mask):
        return swap(a, 0, mask)

    def finish_split(a, group):
        count = a.shape[0] // 2
        give = lax.dynamic_slice_in_dim(a, (1 - core) * count, count, 0)
        keep = lax.dynamic_slice_in_dim(a, core * count, count, 0)
        other = swap(give, pair_mask)
        keep = keep.reshape(count, -1, 1, group)
        other = other.reshape(count, -1, 1, group)
        whole = jnp.where(
            core == 0,
            jnp.concatenate([keep, other], axis=2),
            jnp.concatenate([other, keep], axis=2),
        ).reshape(count, -1)
        return scatter_low(whole).astype(F32)

    down_far = weight_grad(
        spot, hidden, (low_two, low_two_other), (1, 3), None, (), "down_far", 0.1
    )
    down_got = swap(down_far, x_mask)
    low_two_next = after(low_two, down_far)
    grad_pre, gn_own, gn_other, bias_up_grad = pl.pallas_call(
        feed_forward_back,
        out_shape=[
            jax.ShapeDtypeStruct((tokens, QUADS * HIDE), BF),
            jax.ShapeDtypeStruct((rows, D), F32),
            jax.ShapeDtypeStruct((rows, D), F32),
            jax.ShapeDtypeStruct((1, QUADS * HIDE), F32),
        ],
        grid_spec=pltpu.PrefetchScalarGridSpec(
            num_scalar_prefetch=1,
            grid=(QUADS,),
            in_specs=[
                pl.BlockSpec((rows, D), const2),
                pl.BlockSpec((rows, D), const2),
                pl.BlockSpec((1, tokens, HIDE), lambda r, s: (r, 0, 0)),
                up_spec,
                down_spec,
            ],
            out_specs=[
                pl.BlockSpec((tokens, HIDE), lambda r, s: (0, s[0] ^ r)),
                pl.BlockSpec((rows, D), const2),
                pl.BlockSpec((rows, D), const2),
                pl.BlockSpec((1, HIDE), lambda r, s: (0, s[0] ^ r)),
            ],
            scratch_shapes=[pltpu.VMEM((tokens, D), BF)],
        ),
        compiler_params=params(58),
        cost_estimate=cost(0.1),
        name="feed_forward_back",
    )(spot, low_two_next, low_two_other, slope, mlp_all, mlp_all)
    up_far = weight_grad(spot, low_rel, (grad_pre,), (2, 3), None, (), "up_far", 0.1)
    up_got = swap(up_far, y_mask)
    recv = swap(gn_other, pair_mask)
    grad_one, low_one, sums_one = call(
        first_norm_back,
        [
            jax.ShapeDtypeStruct((rows, D), F32),
            jax.ShapeDtypeStruct((rows, D), BF),
            jax.ShapeDtypeStruct((3, D), F32),
        ],
        [grad_two, after(gn_own, up_far), recv, scaled_one, inv_one, vec],
        0, 16, cost(0.1), "first_norm_back",
    )
    low_one_other = swap(low_one, pair_mask)
    grad_qkv, gx_own, gx_other, bias_qkv_grad = call(
        attention_backward,
        [
            jax.ShapeDtypeStruct((tokens, 3 * D // 2), BF),
            jax.ShapeDtypeStruct((rows, D), F32),
            jax.ShapeDtypeStruct((rows, D), F32),
            jax.ShapeDtypeStruct((1, 3 * D // 2), F32),
        ],
        [place, low_one, low_one_other, qkv, *attn_pieces, cos, sin_a, sin_b, mask],
        1, 58, cost(0.1), "attention_backward", [pltpu.VMEM((PAIRS, tokens, GROUP), BF)],
    )
    sums = pl.pallas_call(
        pack_sums,
        out_shape=jax.ShapeDtypeStruct((2 * QUADS, 16, GROUP), F32),
        in_specs=[SMEM_SPEC] + [VMEM_SPEC] * 5,
        out_specs=VMEM_SPEC,
        cost_estimate=cost(0.1),
        name="pack_sums",
    )(spot, sums_two, sums_one, bias_up_grad, bias_qkv_grad, scalars)

    def tail(after_this, halves, blocks, places, adds, name, micros, kind=BF):
        return tail_grad(
            spot, both_rel, after(grad_qkv, *after_this), att, low_one, low_one_other,
            halves, blocks, places, adds, name, micros, kind,
        )

    def second(value, *others):
        return (after(value, *others), low_two_other)

    tail_args = (both_rel, grad_qkv, att, low_one, low_one_other)
    tail_a, tail_b = tail_pair(
        *tail_args, (((1, 0), (3, 0)), ((2, 1), (3, 1))), (), "tail_far", 0.1
    )
    a_got = swap(tail_a, x_mask)
    b_got = swap(tail_b, y_mask)

    down_z = weight_grad(
        spot, hidden, second(low_two, tail_b), (0, 2), (1, 3),
        ((down_got, 0, 1, 0, True),), "down_head", 12,
    )
    down_z1 = swap_head(down_z, 1)
    up_near = weight_grad(
        spot, low_rel, (after(grad_pre, down_z),), (1,), None,
        ((up_got, 1, 0, 0, True),), "up_near", 16,
    )
    up_last = swap(up_near, x_mask)
    down_zz = weight_grad(
        spot, hidden, second(low_two, up_near), (0, 2), (2,),
        ((down_got, 0, 1, 0, True), (down_z1, 1, 2, 0, False)), "down_head_near", 10,
    )
    down_z2 = swap_head(down_zz, 2)
    a_near, b_near = tail_pair(
        both_rel, after(grad_qkv, down_zz), att, low_one, low_one_other,
        (((2, 0),), ((1, 1),)), (a_got, b_got), "tail_near", 10,
    )
    a_last = swap(a_near, y_mask)
    b_last = swap(b_near, x_mask)
    up_adds = ((up_got, 0, 0, 0, True), (up_last, 0, 0, 0, True))
    up_z = weight_grad(
        spot, low_rel, (after(grad_pre, b_near),), (0,), (1, 3), up_adds, "up_head", 10
    )
    up_z1 = swap_head(up_z, 1)
    a_adds = ((a_got, 0, 0, True), (a_last, 0, 0, True))
    b_adds = ((b_got, 0, 0, True), (b_last, 0, 0, True))
    tail_z = tail((up_z,), (0, 1), (0,), (1, 3), a_adds + b_adds, "tail_head", 10)
    tail_z1 = swap_head(tail_z, 1)
    down_y = weight_grad(
        spot, hidden, second(low_two, tail_z), (2,), (0,),
        ((down_got, 1, 0, 0, True), (down_z1, 2, 0, 0, False), (down_z2, 1, 0, 0, False)),
        "down_near", 8,
    )
    down_last = swap(down_y, y_mask)
    up_zz = weight_grad(
        spot, low_rel, (after(grad_pre, down_y),), (0,), (2,),
        up_adds + ((up_z1, 1, 0, 0, False),), "up_head_near", 8,
    )
    up_z2 = swap_head(up_zz, 2)
    tail_zz = tail(
        (up_zz,), (0, 1), (0,), (2,),
        a_adds + ((tail_z1, 1, 0, False),) + b_adds + ((tail_z1, 1, 1, False),),
        "tail_head_near", 8,
    )
    tail_z2 = swap_head(tail_zz, 2)
    exact = BF if low_span > 1 else F32
    grad_w_down = weight_grad(
        spot, hidden, second(low_two, tail_zz), (0,), (0,),
        (
            (down_got, 0, 0, 0, True), (down_z1, 0, 0, 0, False),
            (down_z2, 0, 0, 0, False), (down_last, 0, 0, 0, False),
        ),
        "down_own", 4, exact,
    )[0]
    up_own = weight_grad(
        spot, low_rel, (after(grad_pre, grad_w_down),), (0,), (0,),
        up_adds + ((up_z1, 0, 0, 0, False), (up_z2, 0, 0, 0, False)), "up_own", 4,
    )[0]
    kept = tail(
        (up_own,), (0, 1), (0,), (0,),
        a_adds + ((tail_z1, 0, 0, False), (tail_z2, 0, 0, False))
        + b_adds + ((tail_z1, 0, 1, False), (tail_z2, 0, 1, False)),
        "tail_own", 4,
    ).reshape(256, 512)
    grad_w_down = scatter_low(grad_w_down).astype(F32)
    grad_w_up = finish_split(up_own, HIDE)
    grad_w_qkv = finish_split(kept[:, :qkv_cols], GROUP)
    kept_out = kept[:, qkv_cols:]
    grad_w_out = scatter_low(
        jnp.concatenate([kept_out[:GROUP], kept_out[GROUP:]], axis=1)
    ).astype(F32)
    mixed = jnp.concatenate([grad_heads, sums], axis=1)
    mixed = jnp.repeat(mixed, low_span, axis=0) if low_span > 1 else mixed
    mixed = lax.psum_scatter(
        mixed.reshape(n_dp * (all_cols + 16), GROUP), "dp", scatter_dimension=0, tiled=True
    )
    shard = (head_cols + 16 + 31) // 32 * 32
    sums = jnp.pad(mixed[all_cols:], ((0, shard - head_cols - 16), (0, 0)))
    sums = jnp.broadcast_to(sums, (n_hd,) + sums.shape)
    mixed = jnp.concatenate([mixed[:all_cols].reshape(n_hd, head_cols, GROUP), sums], axis=1)
    mixed = lax.psum_scatter(
        mixed.reshape(n_hd * shard, GROUP), "head", scatter_dimension=0, tiled=True
    )
    head_rows = D // n_dp
    grad_w_heads = lax.dynamic_slice(
        mixed, (0, (dp % low_span) * head_rows), (head_cols, head_rows)
    ).T
    sums = mixed[head_cols : head_cols + 16]
    grad_tokens = grad_one + gx_own + swap(gx_other, pair_mask)

    place_in = (dp % low_span) * n_hd + hd
    mat = lax.dynamic_slice(sums[:9], (0, place_in * wide), (9, wide))
    mid = FF // n_all
    up_sum = lax.dynamic_slice(sums[9:13].reshape(-1), (place_in * mid,), (mid,))
    return (
        outputs,
        sums[13, 0:1],
        grad_tokens,
        grad_w_qkv,
        grad_w_out,
        grad_w_up,
        grad_w_down,
        grad_w_heads,
        mat[:5],
        up_sum,
        mat[5:7],
        mat[7:9],
        sums[14, 0:1],
    )


def solution(mesh):
    return jax.shard_map(
        on_device,
        mesh=mesh,
        in_specs=(
            P(("dp", "head"), None),
            P("dp", "head"),
            P("dp", "head"),
            P("dp", "head"),
            P("dp", "head"),
            P("dp", "head"),
            P(None, ("dp", "head")),
            P(("dp", "head")),
            P(None, ("dp", "head")),
            P(None, ("dp", "head")),
            P(),
            P("dp"),
            P("dp"),
            P("dp"),
        ),
        out_specs=(
            P(("dp", "head"), None),
            P(),
            P(("dp", "head"), None),
            P("dp", "head"),
            P("dp", "head"),
            P("dp", "head"),
            P("dp", "head"),
            P("dp", "head"),
            P(None, ("dp", "head")),
            P(("dp", "head")),
            P(None, ("dp", "head")),
            P(None, ("dp", "head")),
            P(),
        ),
        check_vma=False,
    )
```

```python
import jax
import jax.numpy as jnp
from jax import lax
from jax.experimental import pallas as pl
from jax.experimental.pallas import tpu as pltpu
from jax.sharding import PartitionSpec as P

D = 1024
HEADS = 16
HEAD_DIM = 64
FF = 4096
EMB = 128
EMB_MID = 96
EMB_SMALL = 64
QLEN = 32

EPS_NORM = 1e-05
EPS_UNIT = 1e-06
SHARPNESS = 0.05
ROPE_BASE = 10000.0
MASKED = -1000000000.0
SQRT_HALF = 0.7071067811865476
GAUSS_SCALE = 0.3989422804014327

BF = jnp.bfloat16
F32 = jnp.float32
STARTS = (0, EMB, EMB + EMB_MID)
WIDTHS = (EMB, EMB_MID, EMB_SMALL)
SLOTS = 3
QUADS = 4
GROUP = 128
HIDE = FF // 8


PAIRS = 4
VMEM_SPEC = pl.BlockSpec(memory_space=pltpu.VMEM)
SMEM_SPEC = pl.BlockSpec(memory_space=pltpu.SMEM)


def dot_nn(a, b):
    return lax.dot_general(a, b, (((1,), (0,)), ((), ())), preferred_element_type=F32)


def dot_tn(a, b):
    return lax.dot_general(a, b, (((0,), (0,)), ((), ())), preferred_element_type=F32)


def dot_nt(a, b):
    return lax.dot_general(a, b, (((1,), (1,)), ((), ())), preferred_element_type=F32)


def params(mib):
    return pltpu.CompilerParams(vmem_limit_bytes=mib << 20)


TIME_UNIT = 1150000000


def cost(micros):
    return pl.CostEstimate(flops=int(micros * TIME_UNIT), bytes_accessed=1, transcendentals=0)


def whole(a):
    zeros = (0,) * len(a.shape)
    return pl.BlockSpec(a.shape, lambda i: zeros, pipeline_mode=pl.Buffered(1))


def call(kernel, outs, args, n_smem, mib, estimate, name, scratch=()):
    return pl.pallas_call(
        kernel,
        out_shape=outs,
        grid=(1,),
        in_specs=[SMEM_SPEC] * n_smem + [whole(a) for a in args[n_smem:]],
        out_specs=[whole(a) for a in outs],
        scratch_shapes=list(scratch),
        compiler_params=params(mib),
        cost_estimate=estimate,
        name=name,
    )(*args)


def norm_parts(values):
    centred = values - jnp.mean(values, axis=-1, keepdims=True)
    variance = jnp.mean(centred * centred, axis=-1, keepdims=True)
    inverse = lax.rsqrt(variance + EPS_NORM)
    return centred * inverse, inverse


def norm_back(grad_out, scaled, inverse, gain):
    grad_scaled = grad_out * gain
    return inverse * (
        grad_scaled
        - jnp.mean(grad_scaled, axis=-1, keepdims=True)
        - scaled * jnp.mean(grad_scaled * scaled, axis=-1, keepdims=True)
    )


def pieces_of(a0, ax, ay, b0, by, bx):
    def piece(rq, rz):
        at = rz // 2
        if rz % 2 == 0:
            return [a0.at[at], ax.at[at], ay.at[0, at], ay.at[1, at]][rq]
        return [b0.at[at], bx.at[0, at], by.at[at], bx.at[1, at]][rq]

    return piece


def exit_tile(piece, rq, rz):
    return jnp.concatenate(
        [
            jnp.concatenate([piece(q, rz)[0:128, 384:512], piece(q, rz)[128:256, 384:512]], axis=1)
            for q in (rq, rq + 1)
        ],
        axis=0,
    )


def lanes_at(index, width=GROUP):
    return pl.ds(pl.multiple_of(index * width, width), width)


def turn(x, cos, sin_a, sin_b):
    return x * cos + pltpu.roll(x, 96, 1) * sin_a + pltpu.roll(x, 32, 1) * sin_b


def head_mask(h, shape):
    lane = lax.broadcasted_iota(jnp.int32, shape, 1)
    return (lane < HEAD_DIM) if h == 0 else (lane >= HEAD_DIM)


def stacked(a):
    zero = jnp.zeros_like(a)
    return jnp.concatenate(
        [jnp.where(head_mask(0, a.shape), a, zero), jnp.where(head_mask(1, a.shape), a, zero)],
        axis=0,
    )


def unstacked(a):
    half = a.shape[0] // 2
    top = a[:half]
    return jnp.where(head_mask(0, top.shape), top, a[half:])


def softmax_rows(q, k, mask):
    mask = jnp.concatenate([mask, mask], axis=0)
    s = jnp.where(mask > 0, dot_nt(q, k), MASKED)
    raised = jnp.exp(s - jnp.max(s, axis=-1, keepdims=True))
    return raised * (1.0 / jnp.sum(raised, axis=-1, keepdims=True))


def attention_forward(
    place, x, a0, ax, ay, b0, by, bx, cos, sin_a, sin_b, mask, qkv, att, part, vec
):
    quad, hd, core = place[0], place[1], place[5]
    piece = pieces_of(a0, ax, ay, b0, by, bx)
    rows = cos.shape[0]
    for rq in range(4):
        for c in range(2):
            at = slice(c * GROUP, (c + 1) * GROUP)
            total = piece(rq, 0)[256:272, at].astype(F32)
            for rz in range(1, 4):
                total += piece(rq, rz)[256:272, at].astype(F32)
            vec[:, lanes_at(2 * (quad ^ rq) + c)] = total
    for rz in range(4):
        z = hd ^ rz
        acc = dot_nn(x[0], piece(0, rz)[0:256, 0:384])
        for rq in range(1, 4):
            acc += dot_nn(x[rq], piece(rq, rz)[0:256, 0:384])
        for j in range(3):
            i = 3 * z + j
            scale = jnp.where(i < PAIRS, HEAD_DIM**-0.5, 1.0).astype(F32)
            near = vec[0:8, lanes_at(2 * (i % 4) + core)]
            row = lax.broadcasted_iota(jnp.int32, near.shape, 0)
            bias = jnp.sum(jnp.where(row == i // 4, near, 0.0), axis=0, keepdims=True)
            for b in range(2):
                here = acc[b * rows : (b + 1) * rows, j * GROUP : (j + 1) * GROUP]
                here = here + bias
                turned = turn(here, cos[...], sin_a[...], sin_b[...])
                here = jnp.where(i < 2 * PAIRS, turned, here) * scale
                qkv[b * rows : (b + 1) * rows, lanes_at(i)] = here.astype(BF)

    def one(it, carry):
        b, r = it // PAIRS, it % PAIRS
        i = quad ^ r
        row = pl.ds(pl.multiple_of(b * rows, rows), rows)
        q = qkv[row, pl.ds(pl.multiple_of(i * GROUP, GROUP), GROUP)]
        k = qkv[row, pl.ds(pl.multiple_of((PAIRS + i) * GROUP, GROUP), GROUP)]
        v = qkv[row, pl.ds(pl.multiple_of((2 * PAIRS + i) * GROUP, GROUP), GROUP)]
        probs = softmax_rows(stacked(q), k, mask[b])
        both = dot_nn(probs.astype(BF), v)
        att[r, row, :] = unstacked(both).astype(BF)
        return carry

    lax.fori_loop(0, 2 * PAIRS, one, 0)
    pairs = [jnp.concatenate([att[0], att[1]], axis=1), jnp.concatenate([att[2], att[3]], axis=1)]
    for rz in range(4):
        acc = dot_nn(pairs[0], exit_tile(piece, 0, rz)) + dot_nn(pairs[1], exit_tile(piece, 2, rz))
        part[:, lanes_at(hd ^ rz, 256)] = acc


def attention_backward(
    place, own, other, qkv, a0, ax, ay, b0, by, bx, cos, sin_a, sin_b, mask,
    grad_qkv, gx_own, gx_other, sums, ga,
):
    quad, hd = place[0], place[1]
    piece = pieces_of(a0, ax, ay, b0, by, bx)
    rows = cos.shape[0]
    for rq in (0, 2):
        sums_of = [None, None]
        for rz in range(4):
            w = exit_tile(piece, rq, rz)
            for b, grad in ((0, own), (1, other)):
                term = dot_nt(grad[:, lanes_at(hd ^ rz, 256)], w)
                sums_of[b] = term if sums_of[b] is None else sums_of[b] + term
        for b in range(2):
            at = slice(b * rows, (b + 1) * rows)
            ga[rq, at, :] = sums_of[b][:, 0:GROUP].astype(BF)
            ga[rq + 1, at, :] = sums_of[b][:, GROUP:].astype(BF)

    def one(it, carry):
        b, r = it // PAIRS, it % PAIRS
        i = quad ^ r
        row = pl.ds(pl.multiple_of(b * rows, rows), rows)
        at_q = pl.ds(pl.multiple_of(i * GROUP, GROUP), GROUP)
        at_k = pl.ds(pl.multiple_of((PAIRS + i) * GROUP, GROUP), GROUP)
        at_v = pl.ds(pl.multiple_of((2 * PAIRS + i) * GROUP, GROUP), GROUP)
        q, k, v = qkv[row, at_q], qkv[row, at_k], qkv[row, at_v]
        q_pair, grad_pair = stacked(q), stacked(ga[r, row, :])
        probs = softmax_rows(q_pair, k, mask[b])
        gp = dot_nt(grad_pair, v)
        gs = probs * (gp - jnp.sum(probs * gp, axis=-1, keepdims=True))
        gs = gs.astype(BF)
        gq = unstacked(dot_nn(gs, k))
        gk = dot_tn(gs, q_pair)
        gv = dot_tn(probs.astype(BF), grad_pair)
        c, sa, sb = cos[...], -sin_a[...], -sin_b[...]
        grad_qkv[row, at_q] = turn(gq * (HEAD_DIM**-0.5), c, sa, sb).astype(BF)
        grad_qkv[row, at_k] = turn(gk, c, sa, sb).astype(BF)
        grad_qkv[row, at_v] = gv.astype(BF)
        return carry

    lax.fori_loop(0, 2 * PAIRS, one, 0)
    for rq in range(4):
        at = pl.ds(pl.multiple_of((quad ^ rq) * 256, 256), 256)
        acc = None
        for rz in range(4):
            cols = pl.ds(pl.multiple_of((hd ^ rz) * 384, GROUP), 384)
            term = dot_nt(grad_qkv[:, cols], piece(rq, rz)[0:256, 0:384])
            acc = term if acc is None else acc + term
        gx_own[:, at] = acc[:rows]
        gx_other[:, at] = acc[rows:]
    sums[...] = jnp.sum(grad_qkv[...].astype(F32), axis=0, keepdims=True)


def first_norm(place, x, part, recv, vec, scaled_out, inv_out, low, rel_out):
    rows = scaled_out.shape[0]
    for b in range(2):
        sel = slice(b * rows, (b + 1) * rows)
        swapped = slice((1 - b) * rows, (2 - b) * rows)
        h = x[sel, :].astype(F32) + part[sel, :] + recv[swapped, :] + vec[3:4, :]
        scaled, inverse = norm_parts(h)
        low[sel, :] = (scaled * vec[5:6, :] + vec[7:8, :]).astype(BF)
        if b == 0:
            scaled_out[...] = scaled
            inv_out[...] = inverse
    for q in range(QUADS):
        rel_out[q, :, :] = low[:, lanes_at(place[0] ^ q, 256)]


def feed_forward(place, low, vec, wup, wdown, hidden_out, slope_out, own_out, other_out, kept):
    step = pl.program_id(0)
    rows = own_out.shape[0]

    @pl.when(step < QUADS)
    def _():
        for cb in range(2):
            cols = slice(cb * 256, (cb + 1) * 256)
            w = wup[:, 0, cb * 128 : (cb + 1) * 128, :].reshape(D, 256)
            bias = [
                vec[9 + 2 * cb + k : 10 + 2 * cb + k, lanes_at(2 * (place[0] ^ step) + place[1])]
                for k in range(2)
            ]
            pre = dot_nn(low[...], w) + jnp.concatenate(bias, axis=1)
            gate = 0.5 * (1.0 + lax.erf(pre * SQRT_HALF))
            hidden = (pre * gate).astype(BF)
            hidden_out[0, :, cols] = hidden
            kept[step, :, cols] = hidden
            slope_out[0, :, cols] = (
                gate + pre * jnp.exp(-0.5 * pre * pre) * GAUSS_SCALE
            ).astype(BF)

    @pl.when(step >= QUADS)
    def _():
        acc = dot_nn(kept[0], wdown[place[0], 0, 0])
        for r in range(1, QUADS):
            acc += dot_nn(kept[r], wdown[place[0] ^ r, 0, 0])
        own_out[...] = acc[:rows]
        other_out[...] = acc[rows:]


def feed_forward_back(
    place, own, other, slope, wup, wdown, pre_out, own_out, other_out, sums, both
):
    r = pl.program_id(0)
    rows = own.shape[0]

    @pl.when(r == 0)
    def _():
        both[0:rows, :] = own[...]
        both[rows:, :] = other[...]
        own_out[...] = jnp.zeros_like(own_out)
        other_out[...] = jnp.zeros_like(other_out)

    acc = dot_nt(both[:, 0:256], wdown[0, 0])
    for z in range(1, 4):
        acc += dot_nt(both[:, z * 256 : (z + 1) * 256], wdown[0, z])
    grad = (acc * slope[0].astype(F32)).astype(BF)
    pre_out[...] = grad
    sums[...] = jnp.sum(grad.astype(F32), axis=0, keepdims=True)
    total = None
    for cb in range(2):
        w = wup[:, 0, cb * 128 : (cb + 1) * 128, :].reshape(D, 256)
        term = dot_nt(pre_out[:, cb * 256 : (cb + 1) * 256], w)
        total = term if total is None else total + term
    own_out[...] += total[:rows]
    other_out[...] += total[rows:]


def final_norm(scaled_one, part, recv, vec, windows, out, scaled_out, inv_out, proj):
    h = scaled_one[...] * vec[5:6, :] + vec[7:8, :] + part[...] + recv[...] + vec[4:5, :]
    scaled, inverse = norm_parts(h)
    scaled_out[...] = scaled
    inv_out[...] = inverse
    low = (scaled * vec[6:7, :] + vec[8:9, :]).astype(BF)
    out[...] = low
    proj[...] = dot_nt(windows[...], low).astype(BF)


def soft_maxsim(
    place, temp, lanes, proj_0, proj_1, proj_2, proj_3, windows, out, scaled, inverse_two, vec,
    grad_two, low_two, grad_heads, sums, scalars, gproj, units, shares, similar_low,
):
    hd = place[1]
    rows = out.shape[0]
    projs = (proj_0, proj_1, proj_2, proj_3)
    docs = len(projs) - 1
    row = lax.broadcasted_iota(jnp.int32, (rows, GROUP), 0)
    lane = lax.broadcasted_iota(jnp.int32, (rows, GROUP), 1)
    member = (row // QLEN == lane).astype(F32)
    lens = lanes[0:1, :]
    len_row = jnp.sum(member * lens, axis=1, keepdims=True)
    valid = (row % QLEN).astype(F32) < len_row
    queries = rows // QLEN
    used = lax.broadcasted_iota(jnp.int32, (1, GROUP), 1) < queries
    weight = jnp.where(valid, member, 0.0) / jnp.where(used, lens, 1.0)
    warmth = jnp.exp(jnp.full((1, GROUP), temp[0], F32))
    key = lax.broadcasted_iota(jnp.int32, (rows, rows), 1)
    loss = jnp.zeros((1, GROUP), F32)
    grad_temp = jnp.zeros((1, GROUP), F32)
    for slot in range(SLOTS):
        width = WIDTHS[slot]
        cols = slice(STARTS[slot], STARTS[slot] + width)

        def unit_of(away):
            mapped = projs[away][cols, :].astype(F32)
            inverse = lax.rsqrt(jnp.sum(mapped * mapped, axis=0, keepdims=True) + EPS_UNIT)
            return mapped * inverse, inverse

        for away in range(docs + 1):
            units[0:width, lanes_at(hd ^ away, rows)] = unit_of(away)[0].astype(BF)
        logits = []
        for d in range(docs):
            doc = slice((d + 1) * rows, (d + 2) * rows)
            similar = dot_tn(units[0:width, 0:rows], units[0:width, doc]) * (1.0 / SHARPNESS)
            similar = jnp.where(key < place[2 + d], similar, MASKED)
            top = jnp.max(similar, axis=-1, keepdims=True)
            raised = jnp.exp(similar - top)
            total = jnp.sum(raised, axis=-1, keepdims=True)
            soft = SHARPNESS * (top + jnp.log(total))
            shares[:, d * rows : (d + 1) * rows] = raised * (1.0 / total)
            logits.append(jnp.sum(soft * weight, axis=0, keepdims=True) / warmth)
        top_logit = jnp.maximum(jnp.maximum(logits[0], logits[1]), logits[2])
        exps = [jnp.exp(x - top_logit) for x in logits]
        total = exps[0] + exps[1] + exps[2]
        hits = [(lanes[1:2, :] == float(d)).astype(F32) for d in range(docs)]
        picked = logits[0] * hits[0] + logits[1] * hits[1] + logits[2] * hits[2]
        loss += jnp.where(used, top_logit + jnp.log(total) - picked, 0.0) / queries
        for d in range(docs):
            grad = jnp.where(used, exps[d] / total - hits[d], 0.0) / queries
            grad_temp -= grad * logits[d]
            grad_soft = jnp.sum(weight * (grad / warmth), axis=1, keepdims=True)
            at = slice(d * rows, (d + 1) * rows)
            similar_low[:, at] = (grad_soft * shares[:, at]).astype(BF)

        own = jnp.maximum(hd - 1, 0)
        at = pl.ds(pl.multiple_of(own * rows, rows), rows)
        from_docs = dot_nt(units[0:width, rows:], similar_low[...])
        from_queries = dot_nn(units[0:width, 0:rows], similar_low[:, at])
        grad = jnp.where(hd == 0, from_docs, from_queries)
        unit, inverse = unit_of(0)
        gproj[cols, :] = (
            inverse * (grad - unit * jnp.sum(grad * unit, axis=0, keepdims=True))
        ).astype(BF)

    scalars[0:1, :] = loss
    scalars[1:2, :] = grad_temp
    grad_final = dot_tn(gproj[...], windows[...])
    xhat = scaled[...]
    grad = norm_back(grad_final, xhat, inverse_two[...], vec[6:7, :])
    grad_two[...] = grad
    low_two[...] = grad.astype(BF)
    sums[0:1, :] = jnp.sum(grad_final * xhat, axis=0, keepdims=True)
    sums[1:2, :] = jnp.sum(grad_final, axis=0, keepdims=True)
    sums[2:3, :] = jnp.sum(low_two[...].astype(F32), axis=0, keepdims=True)
    heads = dot_nn(gproj[...], out[...])
    for t in range(2 * QUADS):
        grad_heads[t, 0 : heads.shape[0], :] = heads[:, t * GROUP : (t + 1) * GROUP]


def first_norm_back(grad_two, own, recv, scaled, inverse, vec, grad_one, low_one, sums):
    grad_out = grad_two[...] + own[...] + recv[...]
    xhat = scaled[...]
    grad = norm_back(grad_out, xhat, inverse[...], vec[5:6, :])
    grad_one[...] = grad
    low_one[...] = grad.astype(BF)
    sums[0:1, :] = jnp.sum(grad_out * xhat, axis=0, keepdims=True)
    sums[1:2, :] = jnp.sum(grad_out, axis=0, keepdims=True)
    sums[2:3, :] = jnp.sum(low_one[...].astype(F32), axis=0, keepdims=True)


def weight_grad(spot, lhs, rhs, blocks, places, adds, name, micros, kind=BF):
    tokens, width = lhs.shape[1:]
    whole_cols = places is None
    places = (None,) if whole_cols else places
    count = len(places)
    tile = rhs[0].shape[1] // (1 if whole_cols else 4)
    step = (blocks[1] - blocks[0]) if len(blocks) > 1 else 0
    parts = len(rhs)
    span = tokens // parts
    n_add = len(adds)

    def column(s, place):
        return 0 if place is None else s[2] ^ place

    def kernel(spot_ref, lhs_ref, *refs):
        out = refs[-1]
        for k in range(count):
            total = None
            for p in range(parts):
                term = dot_tn(lhs_ref[0, p * span : (p + 1) * span, :], refs[k * parts + p][...])
                total = term if total is None else total + term
            for add in refs[count * parts + k * n_add : count * parts + (k + 1) * n_add]:
                total += add[0].astype(F32)
            out[k] = total.astype(kind)

    specs = [pl.BlockSpec((1, tokens, width), lambda i, s: (blocks[0] + step * i, 0, 0))]
    for place in places:
        specs += [pl.BlockSpec((span, tile), lambda i, s, c=place: (0, column(s, c)))] * parts
    for k, place in enumerate(places):
        for _, at, per_block, per_place, aligned in adds:
            at += per_place * k
            if aligned:
                index = lambda i, s, at=at, n=per_block, c=place: (at + n * i, 0, column(s, c))
            else:
                index = lambda i, s, at=at, n=per_block: (at + n * i, 0, 0)
            specs.append(pl.BlockSpec((1, width, tile), index))
    return pl.pallas_call(
        kernel,
        out_shape=jax.ShapeDtypeStruct((len(blocks) * count, width, tile), kind),
        grid_spec=pltpu.PrefetchScalarGridSpec(
            num_scalar_prefetch=1,
            grid=(len(blocks),),
            in_specs=specs,
            out_specs=pl.BlockSpec((count, width, tile), lambda i, s: (i, 0, 0)),
        ),
        compiler_params=params(24),
        cost_estimate=cost(micros),
        name=name,
    )(spot, lhs, *(list(rhs) * count), *([add[0] for add in adds] * count))


def tail_grad(spot, x, grad_qkv, att, own, other, halves, blocks, places, adds, name, micros, kind=BF):
    tokens = x.shape[1]
    whole_cols = places is None
    places = (None,) if whole_cols else places
    count = len(places)
    heads = 4 if whole_cols else 1
    step = (blocks[1] - blocks[0]) if len(blocks) > 1 else 0
    n_half = len(halves)
    rows = tokens // 2
    n_add = len(adds)
    per = n_add // n_half
    lane_blocks = 1 if whole_cols else n_half

    def column(s, place):
        return 0 if place is None else s[2] ^ place

    def kernel(spot_ref, x_ref, att_ref, *refs):
        out = refs[-1]
        at_add = count * (1 + 2 * lane_blocks)
        for c in range(count):
            qkv_ref, *pair = refs[c * (1 + 2 * lane_blocks) : (c + 1) * (1 + 2 * lane_blocks)]
            for k, half in enumerate(halves):
                left_all = dot_tn(x_ref[0, :, half * GROUP : (half + 1) * GROUP], qkv_ref[...])
                for z in range(heads):
                    if whole_cols:
                        lanes = slice((2 * z + half) * GROUP, (2 * z + half + 1) * GROUP)
                        up, down = pair[0][:, lanes], pair[1][:, lanes]
                    else:
                        up, down = pair[2 * k][...], pair[2 * k + 1][...]
                    right = dot_tn(att_ref[0, 0:rows, :], up) + dot_tn(att_ref[0, rows:, :], down)
                    left = left_all[:, z * 384 : (z + 1) * 384]
                    first = at_add + c * n_add + k * per
                    lo = z * 512
                    for add in refs[first : first + per]:
                        left += add[0, 0, :, lo : lo + 384].astype(F32)
                        right += add[0, 0, :, lo + 384 : lo + 512].astype(F32)
                    out[c, k, :, lo : lo + 384] = left.astype(kind)
                    out[c, k, :, lo + 384 : lo + 512] = right.astype(kind)

    specs = [
        pl.BlockSpec((1, tokens, 256), lambda i, s: (blocks[0] + step * i, 0, 0)),
        pl.BlockSpec((1, tokens, GROUP), lambda i, s: (blocks[0] + step * i, 0, 0)),
    ]
    inputs = []
    for place in places:
        specs.append(pl.BlockSpec((tokens, 384 * heads), lambda i, s, c=place: (0, column(s, c))))
        inputs.append(grad_qkv)
        for half in halves[:lane_blocks]:
            if whole_cols:
                index = lambda i, s: (0, 0)
            else:
                index = lambda i, s, c=place, half=half: (0, 2 * column(s, c) + half)
            specs += [pl.BlockSpec((rows, D if whole_cols else GROUP), index)] * 2
            inputs += [own, other]
    for place in places:
        for a, at, k, aligned in adds:
            if aligned:
                index = lambda i, s, at=at, k=k, c=place: (at, k, 0, column(s, c))
            else:
                index = lambda i, s, at=at, k=k: (at, k, 0, 0)
            specs.append(pl.BlockSpec((1, 1, GROUP, 512 * heads), index))
            inputs.append(a)
    return pl.pallas_call(
        kernel,
        out_shape=jax.ShapeDtypeStruct((len(blocks) * count, n_half, GROUP, 512 * heads), kind),
        grid_spec=pltpu.PrefetchScalarGridSpec(
            num_scalar_prefetch=1,
            grid=(len(blocks),),
            in_specs=specs,
            out_specs=pl.BlockSpec(
                (count, n_half, GROUP, 512 * heads), lambda i, s: (i, 0, 0, 0)
            ),
        ),
        compiler_params=params(58),
        cost_estimate=cost(micros),
        name=name,
    )(spot, x, att, *inputs)


def tail_pair(x, grad_qkv, att, own, other, jobs, adds, name, micros):
    tokens = x.shape[1]
    rows = tokens // 2

    def kernel(x_ref, qkv_ref, att_ref, own_ref, other_ref, *refs):
        for n, blocks in enumerate(jobs):
            out = refs[len(adds) + n]
            for k, (r, half) in enumerate(blocks):
                left_all = dot_tn(x_ref[r, :, half * GROUP : (half + 1) * GROUP], qkv_ref[...])
                for z in range(4):
                    lanes = slice((2 * z + half) * GROUP, (2 * z + half + 1) * GROUP)
                    right = dot_tn(att_ref[r, 0:rows, :], own_ref[:, lanes])
                    right += dot_tn(att_ref[r, rows:, :], other_ref[:, lanes])
                    left = left_all[:, z * 384 : (z + 1) * 384]
                    lo = z * 512
                    if adds:
                        left += refs[n][0, 0, :, lo : lo + 384].astype(F32)
                        right += refs[n][0, 0, :, lo + 384 : lo + 512].astype(F32)
                    out[k, 0, :, lo : lo + 384] = left.astype(BF)
                    out[k, 0, :, lo + 384 : lo + 512] = right.astype(BF)

    outs = [jax.ShapeDtypeStruct((len(blocks), 1, GROUP, 2048), BF) for blocks in jobs]
    specs = [whole(a) for a in (x, grad_qkv, att, own, other)]
    specs += [pl.BlockSpec((1, 1, GROUP, 2048), lambda i: (1, 0, 0, 0))] * len(adds)
    return pl.pallas_call(
        kernel,
        out_shape=outs,
        grid=(1,),
        in_specs=specs,
        out_specs=[whole(a) for a in outs],
        compiler_params=params(24 if adds else 58),
        cost_estimate=cost(micros),
        name=name,
    )(x, grad_qkv, att, own, other, *adds)


def pack_sums(spot, two, one, up, qkv, scalars, heads, out):
    core, hd = spot[1], spot[2]
    out[...] = jnp.zeros_like(out)
    for i in range(3 * PAIRS):
        out[2 * (i % 4) + core, i // 4 : i // 4 + 1, :] = qkv[0:1, i * GROUP : (i + 1) * GROUP]
    for i in range(4 * QUADS):
        out[2 * (i // 4) + core, 9 + i % 4 : 10 + i % 4, :] = up[
            0:1, i * GROUP : (i + 1) * GROUP
        ]
    once = jnp.where(hd == 0, 1.0, 0.0).astype(F32)
    totals = [jnp.sum(scalars[k : k + 1, :], axis=1, keepdims=True) * once for k in range(2)]
    for t in range(2 * QUADS):
        at = slice(t * GROUP, (t + 1) * GROUP)
        out[t, 3:4, :] = one[2:3, at]
        out[t, 4:5, :] = two[2:3, at]
        out[t, 5:6, :] = one[0:1, at]
        out[t, 6:7, :] = two[0:1, at]
        out[t, 7:8, :] = one[1:2, at]
        out[t, 8:9, :] = two[1:2, at]
        for k in range(2):
            out[t, 13 + k : 14 + k, :] = jnp.broadcast_to(totals[k], (1, GROUP))


def make_windows(tiles, windows, wide):
    cols = windows.shape[0] // 4
    for dp in range(2 * QUADS):
        at = slice(dp * GROUP, (dp + 1) * GROUP)
        for z in range(4):
            lo = z * cols
            wide[lo : lo + 64, at] = tiles[dp, z, :, 0:GROUP].astype(F32)
            rest = tiles[dp, z, 0:16, GROUP:].astype(F32)
            wide[lo + 64 : lo + cols, at] = rest[0 : cols - 64, :]
    windows[...] = wide[...].astype(BF)


def on_device(
    layer_entries,
    triple_projection_matrix,
    attention_exit_matrix,
    expand_matrix,
    contract_matrix,
    nested_projector,
    offset_model_width,
    offset_expanded,
    standardize_factor,
    standardize_offset,
    logarithmic_warmth,
    passage_lengths_each,
    question_lengths,
    relevant_passage,
):
    n_dp = lax.axis_size("dp")
    n_hd = lax.axis_size("head")
    n_all = n_dp * n_hd
    dp = lax.axis_index("dp")
    hd = lax.axis_index("head")
    low_span = n_dp // 8
    quad = dp // (2 * low_span)
    core = (dp // low_span) % 2
    pair_mask = low_span
    x_mask = 2 * low_span
    y_mask = 4 * low_span

    def swap(a, dp_mask=0, hd_mask=0):
        pairs = [
            (d * n_hd + h, (d ^ dp_mask) * n_hd + (h ^ hd_mask))
            for d in range(n_dp)
            for h in range(n_hd)
        ]
        return lax.ppermute(a, ("dp", "head"), pairs)

    def after(value, *others):
        return lax.optimization_barrier((value, *others))[0]

    def joined(bit, own, other):
        return jnp.where(
            bit == 0, jnp.concatenate([own, other], 0), jnp.concatenate([other, own], 0)
        )

    def gather_low(a):
        span = 1
        while span < low_span:
            a = joined((dp // span) % 2, a, swap(a, span))
            span *= 2
        return a

    def scatter_low(a):
        span = low_span // 2
        while span >= 1:
            half = a.shape[0] // 2
            bit = (dp // span) % 2
            give = lax.dynamic_slice_in_dim(a, (1 - bit) * half, half, 0)
            keep = lax.dynamic_slice_in_dim(a, bit * half, half, 0)
            a = (keep.astype(F32) + swap(give, span).astype(F32)).astype(BF)
            span //= 2
        return a

    rows = layer_entries.shape[0]
    docs = passage_lengths_each.shape[0]

    wup_low = gather_low(expand_matrix)
    col_blocks = wup_low.shape[1] // 256
    heads_low = gather_low(nested_projector)
    head_cols = heads_low.shape[1]
    heads_low = jnp.pad(heads_low.T, ((0, GROUP - head_cols), (0, 0)))
    packed_mlp = jnp.concatenate(
        [wup_low[:, i * 256 : (i + 1) * 256] for i in range(col_blocks)]
        + [
            gather_low(contract_matrix),
            jnp.concatenate([heads_low[:64], heads_low[64:]], axis=1),
        ],
        axis=0,
    )
    if low_span > 1:
        dp_groups = [
            [((q * 2 + k) * low_span + s) for q in range(QUADS) for k in range(2)]
            for s in range(low_span)
        ]
        mlp_all = lax.all_gather(
            lax.all_gather(packed_mlp, "head"), "dp", axis_index_groups=dp_groups
        )
    else:
        mlp_all = lax.all_gather(packed_mlp, ("dp", "head"))
    mlp_all = mlp_all.reshape((8, n_hd) + packed_mlp.shape)

    partner_rows = swap(layer_entries, pair_mask)
    lens_own = jnp.concatenate([passage_lengths_each, question_lengths])
    lens_partner = swap(lens_own, pair_mask)
    both = jnp.concatenate([layer_entries, partner_rows], axis=0)
    order = [quad ^ r for r in range(QUADS)]
    both_rel = jnp.stack(
        [lax.dynamic_slice(both, (0, order[r] * 256), (2 * rows, 256)) for r in range(QUADS)]
    )

    wide = offset_model_width.shape[1]
    mine = (jnp.arange(n_hd) == hd).astype(BF)
    vectors = jnp.concatenate([offset_model_width, standardize_factor, standardize_offset], axis=0)
    n_vec = vectors.shape[0]
    vectors = gather_low(vectors[None]).transpose(1, 0, 2)
    vectors = (vectors[:, :, None, :] * mine[None, None, :, None]).reshape(n_vec, GROUP)
    middle = gather_low(offset_expanded[None])
    middle = (middle[:, None, :] * mine[None, :, None]).reshape(4, GROUP)
    vectors = jnp.concatenate([vectors, middle, jnp.zeros((16 - n_vec - 4, GROUP), BF)], axis=0)

    wqkv_low = gather_low(triple_projection_matrix)
    parts = wqkv_low.reshape(wqkv_low.shape[0], -1, 2, GROUP)
    keep, give = (
        lax.dynamic_index_in_dim(parts, k, 2, False).reshape(wqkv_low.shape[0], -1)
        for k in (core, 1 - core)
    )
    qkv_cols = keep.shape[1]
    k_rows = keep.shape[0]
    other = jnp.pad(vectors, ((0, 0), (0, qkv_cols - GROUP)))
    other = swap(jnp.concatenate([give, other], axis=0), pair_mask)
    wout_low = gather_low(attention_exit_matrix)
    wout_own = jnp.concatenate([wout_low[:, :GROUP], wout_low[:, GROUP:]], axis=0)
    vectors = jnp.where(
        core == 0,
        jnp.concatenate([vectors, other[k_rows:, :GROUP]], axis=1),
        jnp.concatenate([other[k_rows:, :GROUP], vectors], axis=1),
    )
    packed = jnp.concatenate(
        [
            jnp.concatenate([joined(core, keep, other[:k_rows]), wout_own], axis=1),
            jnp.pad(vectors, ((0, 0), (0, qkv_cols + GROUP - 2 * GROUP))),
        ],
        axis=0,
    )[None]

    a0 = jnp.concatenate([packed, swap(packed, 0, 2)], axis=0)
    b0 = swap(a0, 0, 1)
    ax = swap(a0, x_mask)
    by = swap(b0, y_mask)
    ay = swap(jnp.stack([a0, ax]), y_mask)
    bx = swap(jnp.stack([b0, by]), x_mask)
    attn_pieces = (a0, ax, ay, b0, by, bx)
    spot = jnp.stack([quad, core, hd]).astype(jnp.int32)

    row_ids = jnp.arange(rows, dtype=jnp.int32)
    is_query = hd == 0

    def valid_of(lens):
        doc_here = lens[jnp.maximum(hd - 1, 0)]
        return jnp.where(
            is_query, row_ids % QLEN < jnp.repeat(lens[docs:], QLEN), row_ids < doc_here
        )

    valid = jnp.stack([valid_of(lens_own), valid_of(lens_partner)])
    segment = jnp.where(is_query, row_ids // QLEN, 0)
    position = jnp.where(is_query, row_ids % QLEN, row_ids)
    mask = ((segment[:, None] == segment[None, :])[None] & valid[:, None, :]).astype(F32)
    halfway = HEAD_DIM // 2
    powers = jnp.arange(halfway, dtype=F32) * (2.0 / HEAD_DIM)
    angles = position.astype(F32)[:, None] * (ROPE_BASE ** (-powers))[None, :]
    cosine, sine = jnp.cos(angles), jnp.sin(angles)
    none = jnp.zeros_like(sine)
    cos = jnp.concatenate([cosine] * 4, axis=1)
    sin_a = jnp.concatenate([-sine, none] * 2, axis=1)
    sin_b = jnp.concatenate([none, sine] * 2, axis=1)
    place = jnp.concatenate(
        [
            jnp.stack([quad, hd]).astype(jnp.int32),
            passage_lengths_each,
            core.reshape(1).astype(jnp.int32),
        ]
    ).astype(jnp.int32)
    tokens = 2 * rows

    qkv, att, part, vec = call(
        attention_forward,
        [
            jax.ShapeDtypeStruct((tokens, 3 * D // 2), BF),
            jax.ShapeDtypeStruct((PAIRS, tokens, GROUP), BF),
            jax.ShapeDtypeStruct((tokens, D), F32),
            jax.ShapeDtypeStruct((16, D), F32),
        ],
        [place, both_rel, *attn_pieces, cos, sin_a, sin_b, mask],
        1, 58, cost(0.1), "attention_forward",
    )
    recv = swap(part, pair_mask)
    scaled_one, inv_one, low_both, low_rel = call(
        first_norm,
        [
            jax.ShapeDtypeStruct((rows, D), F32),
            jax.ShapeDtypeStruct((rows, 1), F32),
            jax.ShapeDtypeStruct((tokens, D), BF),
            jax.ShapeDtypeStruct((QUADS, tokens, 256), BF),
        ],
        [place, both, part, recv, vec],
        1, 24, cost(1), "first_norm",
    )

    def const2(r, s):
        return (0, 0)

    def hide(r, s):
        return s[0] ^ jnp.minimum(r, QUADS - 1)

    def column(r):
        return jnp.maximum(r - QUADS, 0)

    by_core = mlp_all.reshape((QUADS, 2) + mlp_all.shape[1:])
    up_spec = pl.BlockSpec((8, 1, 256, 256), lambda r, s: (0, s[0] ^ r, s[1], 0))
    down_spec = pl.BlockSpec((1, 4, HIDE, 256), lambda r, s: (2 * (s[0] ^ r) + s[1], 0, 1, 0))
    hidden_spec = pl.BlockSpec(
        (1, tokens, HIDE), lambda r, s: (jnp.minimum(r, QUADS - 1), 0, 0)
    )
    column_spec = pl.BlockSpec((rows, 256), lambda r, s: (0, column(r)))
    hidden, slope, out_own, out_other = pl.pallas_call(
        feed_forward,
        out_shape=[
            jax.ShapeDtypeStruct((QUADS, tokens, HIDE), BF),
            jax.ShapeDtypeStruct((QUADS, tokens, HIDE), BF),
            jax.ShapeDtypeStruct((rows, D), F32),
            jax.ShapeDtypeStruct((rows, D), F32),
        ],
        grid_spec=pltpu.PrefetchScalarGridSpec(
            num_scalar_prefetch=1,
            grid=(2 * QUADS,),
            in_specs=[
                pl.BlockSpec((tokens, D), const2),
                pl.BlockSpec((16, D), const2),
                pl.BlockSpec((8, 1, 256, 256), lambda r, s: (0, hide(r, s), s[1], 0)),
                pl.BlockSpec(
                    (QUADS, 1, 1, HIDE, 256), lambda r, s: (0, s[1], column(r), 1, 0)
                ),
            ],
            out_specs=[hidden_spec, hidden_spec, column_spec, column_spec],
            scratch_shapes=[pltpu.VMEM((QUADS, tokens, HIDE), BF)],
        ),
        compiler_params=params(58),
        cost_estimate=cost(12),
        name="feed_forward",
    )(spot, low_both, vec, mlp_all, by_core)
    all_cols = n_hd * head_cols
    windows = pl.pallas_call(
        make_windows,
        out_shape=jax.ShapeDtypeStruct((all_cols, D), BF),
        grid=(1,),
        in_specs=[pl.BlockSpec((8, 4, 64, 256), lambda i: (0, 0, 16, 0))],
        out_specs=pl.BlockSpec((all_cols, D), lambda i: (0, 0)),
        scratch_shapes=[pltpu.VMEM((all_cols, D), F32)],
        compiler_params=params(58),
        cost_estimate=cost(1),
        name="make_windows",
    )(mlp_all)
    recv = swap(out_other, pair_mask)
    outputs, scaled_two, inv_two, own_proj = call(
        final_norm,
        [
            jax.ShapeDtypeStruct((rows, D), BF),
            jax.ShapeDtypeStruct((rows, D), F32),
            jax.ShapeDtypeStruct((rows, 1), F32),
            jax.ShapeDtypeStruct((all_cols, rows), BF),
        ],
        [scaled_one, out_own, recv, vec, windows],
        0, 16, cost(2.6), "final_norm",
    )
    projs = [own_proj] + [swap(own_proj, 0, k) for k in range(1, n_hd)]
    lanes = jnp.stack(
        [
            jnp.pad(question_lengths.astype(F32), (0, GROUP - question_lengths.shape[0])),
            jnp.pad(relevant_passage.astype(F32), (0, GROUP - relevant_passage.shape[0])),
        ]
    )
    grad_two, low_two, grad_heads, sums_two, scalars = call(
        soft_maxsim,
        [
            jax.ShapeDtypeStruct((rows, D), F32),
            jax.ShapeDtypeStruct((rows, D), BF),
            jax.ShapeDtypeStruct((2 * QUADS, all_cols + 16, GROUP), F32),
            jax.ShapeDtypeStruct((3, D), F32),
            jax.ShapeDtypeStruct((2, GROUP), F32),
        ],
        [place, logarithmic_warmth, lanes, *projs, windows, outputs, scaled_two, inv_two, vec],
        2, 24, cost(4.3), "soft_maxsim", [
            pltpu.VMEM((all_cols, rows), BF),
            pltpu.VMEM((EMB, (docs + 1) * rows), BF),
            pltpu.VMEM((rows, docs * rows), F32),
            pltpu.VMEM((rows, docs * rows), BF),
        ],
    )

    low_two_other = swap(low_two, pair_mask)

    def swap_head(a, mask):
        return swap(a, 0, mask)

    def finish_split(a, group):
        count = a.shape[0] // 2
        give = lax.dynamic_slice_in_dim(a, (1 - core) * count, count, 0)
        keep = lax.dynamic_slice_in_dim(a, core * count, count, 0)
        other = swap(give, pair_mask)
        keep = keep.reshape(count, -1, 1, group)
        other = other.reshape(count, -1, 1, group)
        whole = jnp.where(
            core == 0,
            jnp.concatenate([keep, other], axis=2),
            jnp.concatenate([other, keep], axis=2),
        ).reshape(count, -1)
        return scatter_low(whole).astype(F32)

    down_far = weight_grad(
        spot, hidden, (low_two, low_two_other), (1, 3), None, (), "down_far", 0.1
    )
    down_got = swap(down_far, x_mask)
    low_two_next = after(low_two, down_far)
    grad_pre, gn_own, gn_other, bias_up_grad = pl.pallas_call(
        feed_forward_back,
        out_shape=[
            jax.ShapeDtypeStruct((tokens, QUADS * HIDE), BF),
            jax.ShapeDtypeStruct((rows, D), F32),
            jax.ShapeDtypeStruct((rows, D), F32),
            jax.ShapeDtypeStruct((1, QUADS * HIDE), F32),
        ],
        grid_spec=pltpu.PrefetchScalarGridSpec(
            num_scalar_prefetch=1,
            grid=(QUADS,),
            in_specs=[
                pl.BlockSpec((rows, D), const2),
                pl.BlockSpec((rows, D), const2),
                pl.BlockSpec((1, tokens, HIDE), lambda r, s: (r, 0, 0)),
                up_spec,
                down_spec,
            ],
            out_specs=[
                pl.BlockSpec((tokens, HIDE), lambda r, s: (0, s[0] ^ r)),
                pl.BlockSpec((rows, D), const2),
                pl.BlockSpec((rows, D), const2),
                pl.BlockSpec((1, HIDE), lambda r, s: (0, s[0] ^ r)),
            ],
            scratch_shapes=[pltpu.VMEM((tokens, D), BF)],
        ),
        compiler_params=params(58),
        cost_estimate=cost(0.1),
        name="feed_forward_back",
    )(spot, low_two_next, low_two_other, slope, mlp_all, mlp_all)
    up_far = weight_grad(spot, low_rel, (grad_pre,), (2, 3), None, (), "up_far", 0.1)
    up_got = swap(up_far, y_mask)
    recv = swap(gn_other, pair_mask)
    grad_one, low_one, sums_one = call(
        first_norm_back,
        [
            jax.ShapeDtypeStruct((rows, D), F32),
            jax.ShapeDtypeStruct((rows, D), BF),
            jax.ShapeDtypeStruct((3, D), F32),
        ],
        [grad_two, after(gn_own, up_far), recv, scaled_one, inv_one, vec],
        0, 16, cost(0.1), "first_norm_back",
    )
    low_one_other = swap(low_one, pair_mask)
    grad_qkv, gx_own, gx_other, bias_qkv_grad = call(
        attention_backward,
        [
            jax.ShapeDtypeStruct((tokens, 3 * D // 2), BF),
            jax.ShapeDtypeStruct((rows, D), F32),
            jax.ShapeDtypeStruct((rows, D), F32),
            jax.ShapeDtypeStruct((1, 3 * D // 2), F32),
        ],
        [place, low_one, low_one_other, qkv, *attn_pieces, cos, sin_a, sin_b, mask],
        1, 58, cost(0.1), "attention_backward", [pltpu.VMEM((PAIRS, tokens, GROUP), BF)],
    )
    mixed = pl.pallas_call(
        pack_sums,
        out_shape=jax.ShapeDtypeStruct(grad_heads.shape, F32),
        grid=(1,),
        in_specs=[SMEM_SPEC]
        + [whole(a) for a in (sums_two, sums_one, bias_up_grad, bias_qkv_grad, scalars)]
        + [pl.BlockSpec(memory_space=pl.ANY)],
        out_specs=pl.BlockSpec((2 * QUADS, 16, GROUP), lambda i: (0, all_cols // 16, 0)),
        input_output_aliases={6: 0},
        compiler_params=params(24),
        cost_estimate=cost(0.1),
        name="pack_sums",
    )(spot, sums_two, sums_one, bias_up_grad, bias_qkv_grad, scalars, grad_heads)

    def tail(after_this, halves, blocks, places, adds, name, micros, kind=BF):
        return tail_grad(
            spot, both_rel, after(grad_qkv, *after_this), att, low_one, low_one_other,
            halves, blocks, places, adds, name, micros, kind,
        )

    def second(value, *others):
        return (after(value, *others), low_two_other)

    tail_args = (both_rel, grad_qkv, att, low_one, low_one_other)
    tail_a, tail_b = tail_pair(
        *tail_args, (((1, 0), (3, 0)), ((2, 1), (3, 1))), (), "tail_far", 0.1
    )
    a_got = swap(tail_a, x_mask)
    b_got = swap(tail_b, y_mask)

    down_z = weight_grad(
        spot, hidden, second(low_two, tail_b), (0, 2), (1, 3),
        ((down_got, 0, 1, 0, True),), "down_head", 6,
    )
    down_z1 = swap_head(down_z, 1)
    up_near = weight_grad(
        spot, low_rel, (after(grad_pre, down_z),), (1,), None,
        ((up_got, 1, 0, 0, True),), "up_near", 8,
    )
    up_last = swap(up_near, x_mask)
    down_zz = weight_grad(
        spot, hidden, second(low_two, up_near), (0, 2), (2,),
        ((down_got, 0, 1, 0, True), (down_z1, 1, 2, 0, False)), "down_head_near", 5,
    )
    down_z2 = swap_head(down_zz, 2)
    a_near, b_near = tail_pair(
        both_rel, after(grad_qkv, down_zz), att, low_one, low_one_other,
        (((2, 0),), ((1, 1),)), (a_got, b_got), "tail_near", 5,
    )
    a_last = swap(a_near, y_mask)
    b_last = swap(b_near, x_mask)
    up_adds = ((up_got, 0, 0, 0, True), (up_last, 0, 0, 0, True))
    up_z = weight_grad(
        spot, low_rel, (after(grad_pre, b_near),), (0,), (1, 3), up_adds, "up_head", 5
    )
    up_z1 = swap_head(up_z, 1)
    down_y = weight_grad(
        spot, hidden, second(low_two, up_z), (2,), (0,),
        ((down_got, 1, 0, 0, True), (down_z1, 2, 0, 0, False), (down_z2, 1, 0, 0, False)),
        "down_near", 0.1,
    )
    down_last = swap(down_y, y_mask)
    a_adds = ((a_got, 0, 0, True), (a_last, 0, 0, True))
    b_adds = ((b_got, 0, 0, True), (b_last, 0, 0, True))
    tail_z = tail((down_y,), (0, 1), (0,), (1, 3), a_adds + b_adds, "tail_head", 5)
    tail_z1 = swap_head(tail_z, 1)
    up_zz = weight_grad(
        spot, low_rel, (after(grad_pre, tail_z),), (0,), (2,),
        up_adds + ((up_z1, 1, 0, 0, False),), "up_head_near", 4,
    )
    up_z2 = swap_head(up_zz, 2)
    tail_zz = tail(
        (up_zz,), (0, 1), (0,), (2,),
        a_adds + ((tail_z1, 1, 0, False),) + b_adds + ((tail_z1, 1, 1, False),),
        "tail_head_near", 4,
    )
    tail_z2 = swap_head(tail_zz, 2)
    exact = BF if low_span > 1 else F32
    grad_w_down = weight_grad(
        spot, hidden, second(low_two, tail_zz), (0,), (0,),
        (
            (down_got, 0, 0, 0, True), (down_z1, 0, 0, 0, False),
            (down_z2, 0, 0, 0, False), (down_last, 0, 0, 0, False),
        ),
        "down_own", 4, exact,
    )[0]
    up_own = weight_grad(
        spot, low_rel, (after(grad_pre, grad_w_down),), (0,), (0,),
        up_adds + ((up_z1, 0, 0, 0, False), (up_z2, 0, 0, 0, False)), "up_own", 4,
    )[0]
    kept = tail(
        (up_own,), (0, 1), (0,), (0,),
        a_adds + ((tail_z1, 0, 0, False), (tail_z2, 0, 0, False))
        + b_adds + ((tail_z1, 0, 1, False), (tail_z2, 0, 1, False)),
        "tail_own", 4,
    ).reshape(256, 512)
    grad_w_down = scatter_low(grad_w_down).astype(F32)
    grad_w_up = finish_split(up_own, HIDE)
    grad_w_qkv = finish_split(kept[:, :qkv_cols], GROUP)
    kept_out = kept[:, qkv_cols:]
    grad_w_out = scatter_low(
        jnp.concatenate([kept_out[:GROUP], kept_out[GROUP:]], axis=1)
    ).astype(F32)
    mixed = jnp.repeat(mixed, low_span, axis=0) if low_span > 1 else mixed
    mixed = lax.psum_scatter(
        mixed.reshape(n_dp * (all_cols + 16), GROUP), "dp", scatter_dimension=0, tiled=True
    )
    shard = (head_cols + 16 + 31) // 32 * 32
    sums = jnp.pad(mixed[all_cols:], ((0, shard - head_cols - 16), (0, 0)))
    sums = jnp.broadcast_to(sums, (n_hd,) + sums.shape)
    mixed = jnp.concatenate([mixed[:all_cols].reshape(n_hd, head_cols, GROUP), sums], axis=1)
    mixed = lax.psum_scatter(
        mixed.reshape(n_hd * shard, GROUP), "head", scatter_dimension=0, tiled=True
    )
    head_rows = D // n_dp
    grad_w_heads = lax.dynamic_slice(
        mixed, (0, (dp % low_span) * head_rows), (head_cols, head_rows)
    ).T
    sums = mixed[head_cols : head_cols + 16]
    grad_tokens = grad_one + gx_own + swap(gx_other, pair_mask)

    place_in = (dp % low_span) * n_hd + hd
    mat = lax.dynamic_slice(sums[:9], (0, place_in * wide), (9, wide))
    mid = FF // n_all
    up_sum = lax.dynamic_slice(sums[9:13].reshape(-1), (place_in * mid,), (mid,))
    return (
        outputs,
        sums[13, 0:1],
        grad_tokens,
        grad_w_qkv,
        grad_w_out,
        grad_w_up,
        grad_w_down,
        grad_w_heads,
        mat[:5],
        up_sum,
        mat[5:7],
        mat[7:9],
        sums[14, 0:1],
    )


def solution(mesh):
    return jax.shard_map(
        on_device,
        mesh=mesh,
        in_specs=(
            P(("dp", "head"), None),
            P("dp", "head"),
            P("dp", "head"),
            P("dp", "head"),
            P("dp", "head"),
            P("dp", "head"),
            P(None, ("dp", "head")),
            P(("dp", "head")),
            P(None, ("dp", "head")),
            P(None, ("dp", "head")),
            P(),
            P("dp"),
            P("dp"),
            P("dp"),
        ),
        out_specs=(
            P(("dp", "head"), None),
            P(),
            P(("dp", "head"), None),
            P("dp", "head"),
            P("dp", "head"),
            P("dp", "head"),
            P("dp", "head"),
            P("dp", "head"),
            P(None, ("dp", "head")),
            P(("dp", "head")),
            P(None, ("dp", "head")),
            P(None, ("dp", "head")),
            P(),
        ),
        check_vma=False,
    )
```

```python
import jax
import jax.numpy as jnp
from jax import lax
from jax.experimental import pallas as pl
from jax.experimental.pallas import tpu as pltpu
from jax.sharding import PartitionSpec as P

D = 1024
HEADS = 16
HEAD_DIM = 64
FF = 4096
EMB = 128
EMB_MID = 96
EMB_SMALL = 64
QLEN = 32

EPS_NORM = 1e-05
EPS_UNIT = 1e-06
SHARPNESS = 0.05
ROPE_BASE = 10000.0
MASKED = -1000000000.0
SQRT_HALF = 0.7071067811865476
GAUSS_SCALE = 0.3989422804014327

BF = jnp.bfloat16
F32 = jnp.float32
STARTS = (0, EMB, EMB + EMB_MID)
WIDTHS = (EMB, EMB_MID, EMB_SMALL)
SLOTS = 3
QUADS = 4
GROUP = 128
HIDE = FF // 8


PAIRS = 4
VMEM_SPEC = pl.BlockSpec(memory_space=pltpu.VMEM)
SMEM_SPEC = pl.BlockSpec(memory_space=pltpu.SMEM)


def dot_nn(a, b):
    return lax.dot_general(a, b, (((1,), (0,)), ((), ())), preferred_element_type=F32)


def dot_tn(a, b):
    return lax.dot_general(a, b, (((0,), (0,)), ((), ())), preferred_element_type=F32)


def dot_nt(a, b):
    return lax.dot_general(a, b, (((1,), (1,)), ((), ())), preferred_element_type=F32)


def params(mib):
    return pltpu.CompilerParams(vmem_limit_bytes=mib << 20)


TIME_UNIT = 1150000000


def cost(micros):
    return pl.CostEstimate(flops=int(micros * TIME_UNIT), bytes_accessed=1, transcendentals=0)


def whole(a):
    zeros = (0,) * len(a.shape)
    return pl.BlockSpec(a.shape, lambda i: zeros, pipeline_mode=pl.Buffered(1))


def call(kernel, outs, args, n_smem, mib, estimate, name, scratch=()):
    return pl.pallas_call(
        kernel,
        out_shape=outs,
        grid=(1,),
        in_specs=[SMEM_SPEC] * n_smem + [whole(a) for a in args[n_smem:]],
        out_specs=[whole(a) for a in outs],
        scratch_shapes=list(scratch),
        compiler_params=params(mib),
        cost_estimate=estimate,
        name=name,
    )(*args)


def norm_parts(values):
    centred = values - jnp.mean(values, axis=-1, keepdims=True)
    variance = jnp.mean(centred * centred, axis=-1, keepdims=True)
    inverse = lax.rsqrt(variance + EPS_NORM)
    return centred * inverse, inverse


def norm_back(grad_out, scaled, inverse, gain):
    grad_scaled = grad_out * gain
    return inverse * (
        grad_scaled
        - jnp.mean(grad_scaled, axis=-1, keepdims=True)
        - scaled * jnp.mean(grad_scaled * scaled, axis=-1, keepdims=True)
    )


def pieces_of(a0, ax, ay, b0, by, bx):
    def piece(rq, rz):
        at = rz // 2
        if rz % 2 == 0:
            return [a0.at[at], ax.at[at], ay.at[0, at], ay.at[1, at]][rq]
        return [b0.at[at], bx.at[0, at], by.at[at], bx.at[1, at]][rq]

    return piece


def exit_tile(piece, rq, rz):
    return jnp.concatenate(
        [
            jnp.concatenate([piece(q, rz)[0:128, 384:512], piece(q, rz)[128:256, 384:512]], axis=1)
            for q in (rq, rq + 1)
        ],
        axis=0,
    )


def lanes_at(index, width=GROUP):
    return pl.ds(pl.multiple_of(index * width, width), width)


def turn(x, cos, sin_a, sin_b):
    return x * cos + pltpu.roll(x, 96, 1) * sin_a + pltpu.roll(x, 32, 1) * sin_b


def head_mask(h, shape):
    lane = lax.broadcasted_iota(jnp.int32, shape, 1)
    return (lane < HEAD_DIM) if h == 0 else (lane >= HEAD_DIM)


def stacked(a):
    zero = jnp.zeros_like(a)
    return jnp.concatenate(
        [jnp.where(head_mask(0, a.shape), a, zero), jnp.where(head_mask(1, a.shape), a, zero)],
        axis=0,
    )


def unstacked(a):
    half = a.shape[0] // 2
    top = a[:half]
    return jnp.where(head_mask(0, top.shape), top, a[half:])


def softmax_rows(q, k, mask):
    mask = jnp.concatenate([mask, mask], axis=0)
    s = jnp.where(mask > 0, dot_nt(q, k), MASKED)
    raised = jnp.exp(s - jnp.max(s, axis=-1, keepdims=True))
    return raised * (1.0 / jnp.sum(raised, axis=-1, keepdims=True))


def attention_forward(
    place, x, a0, ax, ay, b0, by, bx, cos, sin_a, sin_b, mask, qkv, att, part, vec
):
    quad, hd, core = place[0], place[1], place[5]
    piece = pieces_of(a0, ax, ay, b0, by, bx)
    rows = cos.shape[0]
    for rq in range(4):
        for c in range(2):
            at = slice(c * GROUP, (c + 1) * GROUP)
            total = piece(rq, 0)[256:272, at].astype(F32)
            for rz in range(1, 4):
                total += piece(rq, rz)[256:272, at].astype(F32)
            vec[:, lanes_at(2 * (quad ^ rq) + c)] = total
    for rz in range(4):
        z = hd ^ rz
        acc = dot_nn(x[0], piece(0, rz)[0:256, 0:384])
        for rq in range(1, 4):
            acc += dot_nn(x[rq], piece(rq, rz)[0:256, 0:384])
        for j in range(3):
            i = 3 * z + j
            scale = jnp.where(i < PAIRS, HEAD_DIM**-0.5, 1.0).astype(F32)
            near = vec[0:8, lanes_at(2 * (i % 4) + core)]
            row = lax.broadcasted_iota(jnp.int32, near.shape, 0)
            bias = jnp.sum(jnp.where(row == i // 4, near, 0.0), axis=0, keepdims=True)
            for b in range(2):
                here = acc[b * rows : (b + 1) * rows, j * GROUP : (j + 1) * GROUP]
                here = here + bias
                turned = turn(here, cos[...], sin_a[...], sin_b[...])
                here = jnp.where(i < 2 * PAIRS, turned, here) * scale
                qkv[b * rows : (b + 1) * rows, lanes_at(i)] = here.astype(BF)

    def one(it, carry):
        b, r = it // PAIRS, it % PAIRS
        i = quad ^ r
        row = pl.ds(pl.multiple_of(b * rows, rows), rows)
        q = qkv[row, pl.ds(pl.multiple_of(i * GROUP, GROUP), GROUP)]
        k = qkv[row, pl.ds(pl.multiple_of((PAIRS + i) * GROUP, GROUP), GROUP)]
        v = qkv[row, pl.ds(pl.multiple_of((2 * PAIRS + i) * GROUP, GROUP), GROUP)]
        probs = softmax_rows(stacked(q), k, mask[b])
        both = dot_nn(probs.astype(BF), v)
        att[r, row, :] = unstacked(both).astype(BF)
        return carry

    lax.fori_loop(0, 2 * PAIRS, one, 0)
    pairs = [jnp.concatenate([att[0], att[1]], axis=1), jnp.concatenate([att[2], att[3]], axis=1)]
    for rz in range(4):
        acc = dot_nn(pairs[0], exit_tile(piece, 0, rz)) + dot_nn(pairs[1], exit_tile(piece, 2, rz))
        part[:, lanes_at(hd ^ rz, 256)] = acc


def attention_backward(
    place, own, other, qkv, a0, ax, ay, b0, by, bx, cos, sin_a, sin_b, mask,
    grad_qkv, gx_own, gx_other, sums, ga,
):
    quad, hd = place[0], place[1]
    piece = pieces_of(a0, ax, ay, b0, by, bx)
    rows = cos.shape[0]
    for rq in (0, 2):
        sums_of = [None, None]
        for rz in range(4):
            w = exit_tile(piece, rq, rz)
            for b, grad in ((0, own), (1, other)):
                term = dot_nt(grad[:, lanes_at(hd ^ rz, 256)], w)
                sums_of[b] = term if sums_of[b] is None else sums_of[b] + term
        for b in range(2):
            at = slice(b * rows, (b + 1) * rows)
            ga[rq, at, :] = sums_of[b][:, 0:GROUP].astype(BF)
            ga[rq + 1, at, :] = sums_of[b][:, GROUP:].astype(BF)

    def one(it, carry):
        b, r = it // PAIRS, it % PAIRS
        i = quad ^ r
        row = pl.ds(pl.multiple_of(b * rows, rows), rows)
        at_q = pl.ds(pl.multiple_of(i * GROUP, GROUP), GROUP)
        at_k = pl.ds(pl.multiple_of((PAIRS + i) * GROUP, GROUP), GROUP)
        at_v = pl.ds(pl.multiple_of((2 * PAIRS + i) * GROUP, GROUP), GROUP)
        q, k, v = qkv[row, at_q], qkv[row, at_k], qkv[row, at_v]
        q_pair, grad_pair = stacked(q), stacked(ga[r, row, :])
        probs = softmax_rows(q_pair, k, mask[b])
        gp = dot_nt(grad_pair, v)
        gs = probs * (gp - jnp.sum(probs * gp, axis=-1, keepdims=True))
        gs = gs.astype(BF)
        gq = unstacked(dot_nn(gs, k))
        gk = dot_tn(gs, q_pair)
        gv = dot_tn(probs.astype(BF), grad_pair)
        c, sa, sb = cos[...], -sin_a[...], -sin_b[...]
        grad_qkv[row, at_q] = turn(gq * (HEAD_DIM**-0.5), c, sa, sb).astype(BF)
        grad_qkv[row, at_k] = turn(gk, c, sa, sb).astype(BF)
        grad_qkv[row, at_v] = gv.astype(BF)
        return carry

    lax.fori_loop(0, 2 * PAIRS, one, 0)
    for rq in range(4):
        at = pl.ds(pl.multiple_of((quad ^ rq) * 256, 256), 256)
        acc = None
        for rz in range(4):
            cols = pl.ds(pl.multiple_of((hd ^ rz) * 384, GROUP), 384)
            term = dot_nt(grad_qkv[:, cols], piece(rq, rz)[0:256, 0:384])
            acc = term if acc is None else acc + term
        gx_own[:, at] = acc[:rows]
        gx_other[:, at] = acc[rows:]
    sums[...] = jnp.sum(grad_qkv[...].astype(F32), axis=0, keepdims=True)


def first_norm(place, x, part, recv, vec, scaled_out, inv_out, low, rel_out):
    rows = scaled_out.shape[0]
    for b in range(2):
        sel = slice(b * rows, (b + 1) * rows)
        swapped = slice((1 - b) * rows, (2 - b) * rows)
        h = x[sel, :].astype(F32) + part[sel, :] + recv[swapped, :] + vec[3:4, :]
        scaled, inverse = norm_parts(h)
        low[sel, :] = (scaled * vec[5:6, :] + vec[7:8, :]).astype(BF)
        if b == 0:
            scaled_out[...] = scaled
            inv_out[...] = inverse
    for q in range(QUADS):
        rel_out[q, :, :] = low[:, lanes_at(place[0] ^ q, 256)]


def feed_forward(place, low, vec, wup, wdown, hidden_out, slope_out, own_out, other_out, kept):
    step = pl.program_id(0)
    rows = own_out.shape[0]

    @pl.when(step < QUADS)
    def _():
        for cb in range(2):
            cols = slice(cb * 256, (cb + 1) * 256)
            w = wup[:, 0, cb * 128 : (cb + 1) * 128, :].reshape(D, 256)
            bias = [
                vec[9 + 2 * cb + k : 10 + 2 * cb + k, lanes_at(2 * (place[0] ^ step) + place[1])]
                for k in range(2)
            ]
            pre = dot_nn(low[...], w) + jnp.concatenate(bias, axis=1)
            gate = 0.5 * (1.0 + lax.erf(pre * SQRT_HALF))
            hidden = (pre * gate).astype(BF)
            hidden_out[0, :, cols] = hidden
            kept[step, :, cols] = hidden
            slope_out[0, :, cols] = (
                gate + pre * jnp.exp(-0.5 * pre * pre) * GAUSS_SCALE
            ).astype(BF)

    @pl.when(step >= QUADS)
    def _():
        acc = dot_nn(kept[0], wdown[place[0], 0, 0])
        for r in range(1, QUADS):
            acc += dot_nn(kept[r], wdown[place[0] ^ r, 0, 0])
        own_out[...] = acc[:rows]
        other_out[...] = acc[rows:]


def feed_forward_back(
    place, own, other, slope, wup, wdown, pre_out, own_out, other_out, sums, both
):
    r = pl.program_id(0)
    rows = own.shape[0]

    @pl.when(r == 0)
    def _():
        both[0:rows, :] = own[...]
        both[rows:, :] = other[...]
        own_out[...] = jnp.zeros_like(own_out)
        other_out[...] = jnp.zeros_like(other_out)

    acc = dot_nt(both[:, 0:256], wdown[0, 0])
    for z in range(1, 4):
        acc += dot_nt(both[:, z * 256 : (z + 1) * 256], wdown[0, z])
    grad = (acc * slope[0].astype(F32)).astype(BF)
    pre_out[...] = grad
    sums[...] = jnp.sum(grad.astype(F32), axis=0, keepdims=True)
    total = None
    for cb in range(2):
        w = wup[:, 0, cb * 128 : (cb + 1) * 128, :].reshape(D, 256)
        term = dot_nt(pre_out[:, cb * 256 : (cb + 1) * 256], w)
        total = term if total is None else total + term
    own_out[...] += total[:rows]
    other_out[...] += total[rows:]


def final_norm(scaled_one, part, recv, vec, windows, out, scaled_out, inv_out, proj):
    h = scaled_one[...] * vec[5:6, :] + vec[7:8, :] + part[...] + recv[...] + vec[4:5, :]
    scaled, inverse = norm_parts(h)
    scaled_out[...] = scaled
    inv_out[...] = inverse
    low = (scaled * vec[6:7, :] + vec[8:9, :]).astype(BF)
    out[...] = low
    proj[...] = dot_nt(windows[...], low).astype(BF)


def soft_maxsim(
    place, temp, lanes, proj_0, proj_1, proj_2, proj_3, windows, out, scaled, inverse_two, vec,
    grad_two, low_two, grad_heads, sums, scalars, gproj, units, shares, similar_low,
):
    hd = place[1]
    rows = out.shape[0]
    projs = (proj_0, proj_1, proj_2, proj_3)
    docs = len(projs) - 1
    row = lax.broadcasted_iota(jnp.int32, (rows, GROUP), 0)
    lane = lax.broadcasted_iota(jnp.int32, (rows, GROUP), 1)
    member = (row // QLEN == lane).astype(F32)
    lens = lanes[0:1, :]
    len_row = jnp.sum(member * lens, axis=1, keepdims=True)
    valid = (row % QLEN).astype(F32) < len_row
    queries = rows // QLEN
    used = lax.broadcasted_iota(jnp.int32, (1, GROUP), 1) < queries
    weight = jnp.where(valid, member, 0.0) / jnp.where(used, lens, 1.0)
    warmth = jnp.exp(jnp.full((1, GROUP), temp[0], F32))
    key = lax.broadcasted_iota(jnp.int32, (rows, rows), 1)
    loss = jnp.zeros((1, GROUP), F32)
    grad_temp = jnp.zeros((1, GROUP), F32)
    for slot in range(SLOTS):
        width = WIDTHS[slot]
        cols = slice(STARTS[slot], STARTS[slot] + width)

        def unit_of(away):
            mapped = projs[away][cols, :].astype(F32)
            inverse = lax.rsqrt(jnp.sum(mapped * mapped, axis=0, keepdims=True) + EPS_UNIT)
            return mapped * inverse, inverse

        for away in range(docs + 1):
            units[0:width, lanes_at(hd ^ away, rows)] = unit_of(away)[0].astype(BF)
        logits = []
        for d in range(docs):
            doc = slice((d + 1) * rows, (d + 2) * rows)
            similar = dot_tn(units[0:width, 0:rows], units[0:width, doc]) * (1.0 / SHARPNESS)
            similar = jnp.where(key < place[2 + d], similar, MASKED)
            top = jnp.max(similar, axis=-1, keepdims=True)
            raised = jnp.exp(similar - top)
            total = jnp.sum(raised, axis=-1, keepdims=True)
            soft = SHARPNESS * (top + jnp.log(total))
            shares[:, d * rows : (d + 1) * rows] = raised * (1.0 / total)
            logits.append(jnp.sum(soft * weight, axis=0, keepdims=True) / warmth)
        top_logit = jnp.maximum(jnp.maximum(logits[0], logits[1]), logits[2])
        exps = [jnp.exp(x - top_logit) for x in logits]
        total = exps[0] + exps[1] + exps[2]
        hits = [(lanes[1:2, :] == float(d)).astype(F32) for d in range(docs)]
        picked = logits[0] * hits[0] + logits[1] * hits[1] + logits[2] * hits[2]
        loss += jnp.where(used, top_logit + jnp.log(total) - picked, 0.0) / queries
        for d in range(docs):
            grad = jnp.where(used, exps[d] / total - hits[d], 0.0) / queries
            grad_temp -= grad * logits[d]
            grad_soft = jnp.sum(weight * (grad / warmth), axis=1, keepdims=True)
            at = slice(d * rows, (d + 1) * rows)
            similar_low[:, at] = (grad_soft * shares[:, at]).astype(BF)

        own = jnp.maximum(hd - 1, 0)
        at = pl.ds(pl.multiple_of(own * rows, rows), rows)
        from_docs = dot_nt(units[0:width, rows:], similar_low[...])
        from_queries = dot_nn(units[0:width, 0:rows], similar_low[:, at])
        grad = jnp.where(hd == 0, from_docs, from_queries)
        unit, inverse = unit_of(0)
        gproj[cols, :] = (
            inverse * (grad - unit * jnp.sum(grad * unit, axis=0, keepdims=True))
        ).astype(BF)

    scalars[0:1, :] = loss
    scalars[1:2, :] = grad_temp
    grad_final = dot_tn(gproj[...], windows[...])
    xhat = scaled[...]
    grad = norm_back(grad_final, xhat, inverse_two[...], vec[6:7, :])
    grad_two[...] = grad
    low_two[...] = grad.astype(BF)
    sums[0:1, :] = jnp.sum(grad_final * xhat, axis=0, keepdims=True)
    sums[1:2, :] = jnp.sum(grad_final, axis=0, keepdims=True)
    sums[2:3, :] = jnp.sum(low_two[...].astype(F32), axis=0, keepdims=True)
    heads = dot_nn(gproj[...], out[...])
    for t in range(2 * QUADS):
        grad_heads[t, 0 : heads.shape[0], :] = heads[:, t * GROUP : (t + 1) * GROUP]


def first_norm_back(grad_two, own, recv, scaled, inverse, vec, grad_one, low_one, sums):
    grad_out = grad_two[...] + own[...] + recv[...]
    xhat = scaled[...]
    grad = norm_back(grad_out, xhat, inverse[...], vec[5:6, :])
    grad_one[...] = grad
    low_one[...] = grad.astype(BF)
    sums[0:1, :] = jnp.sum(grad_out * xhat, axis=0, keepdims=True)
    sums[1:2, :] = jnp.sum(grad_out, axis=0, keepdims=True)
    sums[2:3, :] = jnp.sum(low_one[...].astype(F32), axis=0, keepdims=True)


def weight_grad(spot, lhs, rhs, blocks, places, adds, name, micros, kind=BF):
    tokens, width = lhs.shape[1:]
    whole_cols = places is None
    places = (None,) if whole_cols else places
    count = len(places)
    tile = rhs[0].shape[1] // (1 if whole_cols else 4)
    step = (blocks[1] - blocks[0]) if len(blocks) > 1 else 0
    parts = len(rhs)
    span = tokens // parts
    n_add = len(adds)

    def column(s, place):
        return 0 if place is None else s[2] ^ place

    def kernel(spot_ref, lhs_ref, *refs):
        out = refs[-1]
        for k in range(count):
            total = None
            for p in range(parts):
                term = dot_tn(lhs_ref[0, p * span : (p + 1) * span, :], refs[k * parts + p][...])
                total = term if total is None else total + term
            for add in refs[count * parts + k * n_add : count * parts + (k + 1) * n_add]:
                total += add[0].astype(F32)
            out[k] = total.astype(kind)

    specs = [pl.BlockSpec((1, tokens, width), lambda i, s: (blocks[0] + step * i, 0, 0))]
    for place in places:
        specs += [pl.BlockSpec((span, tile), lambda i, s, c=place: (0, column(s, c)))] * parts
    for k, place in enumerate(places):
        for _, at, per_block, per_place, aligned in adds:
            at += per_place * k
            if aligned:
                index = lambda i, s, at=at, n=per_block, c=place: (at + n * i, 0, column(s, c))
            else:
                index = lambda i, s, at=at, n=per_block: (at + n * i, 0, 0)
            specs.append(pl.BlockSpec((1, width, tile), index))
    return pl.pallas_call(
        kernel,
        out_shape=jax.ShapeDtypeStruct((len(blocks) * count, width, tile), kind),
        grid_spec=pltpu.PrefetchScalarGridSpec(
            num_scalar_prefetch=1,
            grid=(len(blocks),),
            in_specs=specs,
            out_specs=pl.BlockSpec((count, width, tile), lambda i, s: (i, 0, 0)),
        ),
        compiler_params=params(24),
        cost_estimate=cost(micros),
        name=name,
    )(spot, lhs, *(list(rhs) * count), *([add[0] for add in adds] * count))


def tail_grad(spot, x, grad_qkv, att, own, other, halves, blocks, places, adds, name, micros, kind=BF):
    tokens = x.shape[1]
    whole_cols = places is None
    places = (None,) if whole_cols else places
    count = len(places)
    heads = 4 if whole_cols else 1
    step = (blocks[1] - blocks[0]) if len(blocks) > 1 else 0
    n_half = len(halves)
    rows = tokens // 2
    n_add = len(adds)
    per = n_add // n_half
    lane_blocks = 1 if whole_cols else n_half

    def column(s, place):
        return 0 if place is None else s[2] ^ place

    def kernel(spot_ref, x_ref, att_ref, *refs):
        out = refs[-1]
        at_add = count * (1 + 2 * lane_blocks)
        for c in range(count):
            qkv_ref, *pair = refs[c * (1 + 2 * lane_blocks) : (c + 1) * (1 + 2 * lane_blocks)]
            for k, half in enumerate(halves):
                left_all = dot_tn(x_ref[0, :, half * GROUP : (half + 1) * GROUP], qkv_ref[...])
                for z in range(heads):
                    if whole_cols:
                        lanes = slice((2 * z + half) * GROUP, (2 * z + half + 1) * GROUP)
                        up, down = pair[0][:, lanes], pair[1][:, lanes]
                    else:
                        up, down = pair[2 * k][...], pair[2 * k + 1][...]
                    right = dot_tn(att_ref[0, 0:rows, :], up) + dot_tn(att_ref[0, rows:, :], down)
                    left = left_all[:, z * 384 : (z + 1) * 384]
                    first = at_add + c * n_add + k * per
                    lo = z * 512
                    for add in refs[first : first + per]:
                        left += add[0, 0, :, lo : lo + 384].astype(F32)
                        right += add[0, 0, :, lo + 384 : lo + 512].astype(F32)
                    out[c, k, :, lo : lo + 384] = left.astype(kind)
                    out[c, k, :, lo + 384 : lo + 512] = right.astype(kind)

    specs = [
        pl.BlockSpec((1, tokens, 256), lambda i, s: (blocks[0] + step * i, 0, 0)),
        pl.BlockSpec((1, tokens, GROUP), lambda i, s: (blocks[0] + step * i, 0, 0)),
    ]
    inputs = []
    for place in places:
        specs.append(pl.BlockSpec((tokens, 384 * heads), lambda i, s, c=place: (0, column(s, c))))
        inputs.append(grad_qkv)
        for half in halves[:lane_blocks]:
            if whole_cols:
                index = lambda i, s: (0, 0)
            else:
                index = lambda i, s, c=place, half=half: (0, 2 * column(s, c) + half)
            specs += [pl.BlockSpec((rows, D if whole_cols else GROUP), index)] * 2
            inputs += [own, other]
    for place in places:
        for a, at, k, aligned in adds:
            if aligned:
                index = lambda i, s, at=at, k=k, c=place: (at, k, 0, column(s, c))
            else:
                index = lambda i, s, at=at, k=k: (at, k, 0, 0)
            specs.append(pl.BlockSpec((1, 1, GROUP, 512 * heads), index))
            inputs.append(a)
    return pl.pallas_call(
        kernel,
        out_shape=jax.ShapeDtypeStruct((len(blocks) * count, n_half, GROUP, 512 * heads), kind),
        grid_spec=pltpu.PrefetchScalarGridSpec(
            num_scalar_prefetch=1,
            grid=(len(blocks),),
            in_specs=specs,
            out_specs=pl.BlockSpec(
                (count, n_half, GROUP, 512 * heads), lambda i, s: (i, 0, 0, 0)
            ),
        ),
        compiler_params=params(58),
        cost_estimate=cost(micros),
        name=name,
    )(spot, x, att, *inputs)


def tail_pair(x, grad_qkv, att, own, other, jobs, adds, name, micros):
    tokens = x.shape[1]
    rows = tokens // 2

    def kernel(x_ref, qkv_ref, att_ref, own_ref, other_ref, *refs):
        for n, blocks in enumerate(jobs):
            out = refs[len(adds) + n]
            for k, (r, half) in enumerate(blocks):
                left_all = dot_tn(x_ref[r, :, half * GROUP : (half + 1) * GROUP], qkv_ref[...])
                for z in range(4):
                    lanes = slice((2 * z + half) * GROUP, (2 * z + half + 1) * GROUP)
                    right = dot_tn(att_ref[r, 0:rows, :], own_ref[:, lanes])
                    right += dot_tn(att_ref[r, rows:, :], other_ref[:, lanes])
                    left = left_all[:, z * 384 : (z + 1) * 384]
                    lo = z * 512
                    if adds:
                        left += refs[n][0, 0, :, lo : lo + 384].astype(F32)
                        right += refs[n][0, 0, :, lo + 384 : lo + 512].astype(F32)
                    out[k, 0, :, lo : lo + 384] = left.astype(BF)
                    out[k, 0, :, lo + 384 : lo + 512] = right.astype(BF)

    outs = [jax.ShapeDtypeStruct((len(blocks), 1, GROUP, 2048), BF) for blocks in jobs]
    specs = [whole(a) for a in (x, grad_qkv, att, own, other)]
    specs += [pl.BlockSpec((1, 1, GROUP, 2048), lambda i: (1, 0, 0, 0))] * len(adds)
    return pl.pallas_call(
        kernel,
        out_shape=outs,
        grid=(1,),
        in_specs=specs,
        out_specs=[whole(a) for a in outs],
        compiler_params=params(24 if adds else 58),
        cost_estimate=cost(micros),
        name=name,
    )(x, grad_qkv, att, own, other, *adds)


def pack_sums(spot, two, one, up, qkv, scalars, heads, out):
    core, hd = spot[1], spot[2]
    out[...] = jnp.zeros_like(out)
    for i in range(3 * PAIRS):
        out[2 * (i % 4) + core, i // 4 : i // 4 + 1, :] = qkv[0:1, i * GROUP : (i + 1) * GROUP]
    for i in range(4 * QUADS):
        out[2 * (i // 4) + core, 9 + i % 4 : 10 + i % 4, :] = up[
            0:1, i * GROUP : (i + 1) * GROUP
        ]
    once = jnp.where(hd == 0, 1.0, 0.0).astype(F32)
    totals = [jnp.sum(scalars[k : k + 1, :], axis=1, keepdims=True) * once for k in range(2)]
    for t in range(2 * QUADS):
        at = slice(t * GROUP, (t + 1) * GROUP)
        out[t, 3:4, :] = one[2:3, at]
        out[t, 4:5, :] = two[2:3, at]
        out[t, 5:6, :] = one[0:1, at]
        out[t, 6:7, :] = two[0:1, at]
        out[t, 7:8, :] = one[1:2, at]
        out[t, 8:9, :] = two[1:2, at]
        for k in range(2):
            out[t, 13 + k : 14 + k, :] = jnp.broadcast_to(totals[k], (1, GROUP))


def pack_matrices(up, down, heads, out):
    rows = up.shape[0]
    groups = up.shape[1] // 256
    for i in range(groups):
        out[i * rows : (i + 1) * rows, :] = up[:, i * 256 : (i + 1) * 256]
    at = groups * rows
    out[at : at + down.shape[0], :] = down[...]
    at += down.shape[0]
    out[at : at + 64, 0:GROUP] = heads[0:64, :]
    out[at : at + 64, GROUP:] = heads[64:, :]


def make_windows(tiles, windows, wide):
    cols = windows.shape[0] // 4
    for dp in range(2 * QUADS):
        at = slice(dp * GROUP, (dp + 1) * GROUP)
        for z in range(4):
            lo = z * cols
            wide[lo : lo + 64, at] = tiles[dp, z, :, 0:GROUP].astype(F32)
            rest = tiles[dp, z, 0:16, GROUP:].astype(F32)
            wide[lo + 64 : lo + cols, at] = rest[0 : cols - 64, :]
    windows[...] = wide[...].astype(BF)


def on_device(
    layer_entries,
    triple_projection_matrix,
    attention_exit_matrix,
    expand_matrix,
    contract_matrix,
    nested_projector,
    offset_model_width,
    offset_expanded,
    standardize_factor,
    standardize_offset,
    logarithmic_warmth,
    passage_lengths_each,
    question_lengths,
    relevant_passage,
):
    n_dp = lax.axis_size("dp")
    n_hd = lax.axis_size("head")
    n_all = n_dp * n_hd
    dp = lax.axis_index("dp")
    hd = lax.axis_index("head")
    low_span = n_dp // 8
    quad = dp // (2 * low_span)
    core = (dp // low_span) % 2
    pair_mask = low_span
    x_mask = 2 * low_span
    y_mask = 4 * low_span

    def swap(a, dp_mask=0, hd_mask=0):
        pairs = [
            (d * n_hd + h, (d ^ dp_mask) * n_hd + (h ^ hd_mask))
            for d in range(n_dp)
            for h in range(n_hd)
        ]
        return lax.ppermute(a, ("dp", "head"), pairs)

    def after(value, *others):
        return lax.optimization_barrier((value, *others))[0]

    def joined(bit, own, other):
        return jnp.where(
            bit == 0, jnp.concatenate([own, other], 0), jnp.concatenate([other, own], 0)
        )

    def gather_low(a):
        span = 1
        while span < low_span:
            a = joined((dp // span) % 2, a, swap(a, span))
            span *= 2
        return a

    def scatter_low(a):
        span = low_span // 2
        while span >= 1:
            half = a.shape[0] // 2
            bit = (dp // span) % 2
            give = lax.dynamic_slice_in_dim(a, (1 - bit) * half, half, 0)
            keep = lax.dynamic_slice_in_dim(a, bit * half, half, 0)
            a = (keep.astype(F32) + swap(give, span).astype(F32)).astype(BF)
            span //= 2
        return a

    rows = layer_entries.shape[0]
    docs = passage_lengths_each.shape[0]

    wup_low = gather_low(expand_matrix)
    col_blocks = wup_low.shape[1] // 256
    heads_low = gather_low(nested_projector)
    head_cols = heads_low.shape[1]
    heads_low = jnp.pad(heads_low.T, ((0, GROUP - head_cols), (0, 0)))
    wdown_low = gather_low(contract_matrix)
    (packed_mlp,) = call(
        pack_matrices,
        [jax.ShapeDtypeStruct((wup_low.shape[0] * col_blocks + wdown_low.shape[0] + 64, 256), BF)],
        [wup_low, wdown_low, heads_low],
        0, 16, cost(0.1), "pack_matrices",
    )
    if low_span > 1:
        dp_groups = [
            [((q * 2 + k) * low_span + s) for q in range(QUADS) for k in range(2)]
            for s in range(low_span)
        ]
        mlp_all = lax.all_gather(
            lax.all_gather(packed_mlp, "head"), "dp", axis_index_groups=dp_groups
        )
    else:
        mlp_all = lax.all_gather(packed_mlp, ("dp", "head"))
    mlp_all = mlp_all.reshape((8, n_hd) + packed_mlp.shape)

    partner_rows = swap(layer_entries, pair_mask)
    lens_own = jnp.concatenate([passage_lengths_each, question_lengths])
    lens_partner = swap(lens_own, pair_mask)
    both = jnp.concatenate([layer_entries, partner_rows], axis=0)
    order = [quad ^ r for r in range(QUADS)]
    both_rel = jnp.stack(
        [lax.dynamic_slice(both, (0, order[r] * 256), (2 * rows, 256)) for r in range(QUADS)]
    )

    wide = offset_model_width.shape[1]
    mine = (jnp.arange(n_hd) == hd).astype(BF)
    vectors = jnp.concatenate([offset_model_width, standardize_factor, standardize_offset], axis=0)
    n_vec = vectors.shape[0]
    vectors = gather_low(vectors[None]).transpose(1, 0, 2)
    vectors = (vectors[:, :, None, :] * mine[None, None, :, None]).reshape(n_vec, GROUP)
    middle = gather_low(offset_expanded[None])
    middle = (middle[:, None, :] * mine[None, :, None]).reshape(4, GROUP)
    vectors = jnp.concatenate([vectors, middle, jnp.zeros((16 - n_vec - 4, GROUP), BF)], axis=0)

    wqkv_low = gather_low(triple_projection_matrix)
    parts = wqkv_low.reshape(wqkv_low.shape[0], -1, 2, GROUP)
    keep, give = (
        lax.dynamic_index_in_dim(parts, k, 2, False).reshape(wqkv_low.shape[0], -1)
        for k in (core, 1 - core)
    )
    qkv_cols = keep.shape[1]
    k_rows = keep.shape[0]
    other = jnp.pad(vectors, ((0, 0), (0, qkv_cols - GROUP)))
    other = swap(jnp.concatenate([give, other], axis=0), pair_mask)
    wout_low = gather_low(attention_exit_matrix)
    wout_own = jnp.concatenate([wout_low[:, :GROUP], wout_low[:, GROUP:]], axis=0)
    vectors = jnp.where(
        core == 0,
        jnp.concatenate([vectors, other[k_rows:, :GROUP]], axis=1),
        jnp.concatenate([other[k_rows:, :GROUP], vectors], axis=1),
    )
    packed = jnp.concatenate(
        [
            jnp.concatenate([joined(core, keep, other[:k_rows]), wout_own], axis=1),
            jnp.pad(vectors, ((0, 0), (0, qkv_cols + GROUP - 2 * GROUP))),
        ],
        axis=0,
    )[None]

    a0 = jnp.concatenate([packed, swap(packed, 0, 2)], axis=0)
    b0 = swap(a0, 0, 1)
    ax = swap(a0, x_mask)
    by = swap(b0, y_mask)
    ay = swap(jnp.stack([a0, ax]), y_mask)
    bx = swap(jnp.stack([b0, by]), x_mask)
    attn_pieces = (a0, ax, ay, b0, by, bx)
    spot = jnp.stack([quad, core, hd]).astype(jnp.int32)

    row_ids = jnp.arange(rows, dtype=jnp.int32)
    is_query = hd == 0

    def valid_of(lens):
        doc_here = lens[jnp.maximum(hd - 1, 0)]
        return jnp.where(
            is_query, row_ids % QLEN < jnp.repeat(lens[docs:], QLEN), row_ids < doc_here
        )

    valid = jnp.stack([valid_of(lens_own), valid_of(lens_partner)])
    segment = jnp.where(is_query, row_ids // QLEN, 0)
    position = jnp.where(is_query, row_ids % QLEN, row_ids)
    mask = ((segment[:, None] == segment[None, :])[None] & valid[:, None, :]).astype(F32)
    halfway = HEAD_DIM // 2
    powers = jnp.arange(halfway, dtype=F32) * (2.0 / HEAD_DIM)
    angles = position.astype(F32)[:, None] * (ROPE_BASE ** (-powers))[None, :]
    cosine, sine = jnp.cos(angles), jnp.sin(angles)
    none = jnp.zeros_like(sine)
    cos = jnp.concatenate([cosine] * 4, axis=1)
    sin_a = jnp.concatenate([-sine, none] * 2, axis=1)
    sin_b = jnp.concatenate([none, sine] * 2, axis=1)
    place = jnp.concatenate(
        [
            jnp.stack([quad, hd]).astype(jnp.int32),
            passage_lengths_each,
            core.reshape(1).astype(jnp.int32),
        ]
    ).astype(jnp.int32)
    tokens = 2 * rows

    qkv, att, part, vec = call(
        attention_forward,
        [
            jax.ShapeDtypeStruct((tokens, 3 * D // 2), BF),
            jax.ShapeDtypeStruct((PAIRS, tokens, GROUP), BF),
            jax.ShapeDtypeStruct((tokens, D), F32),
            jax.ShapeDtypeStruct((16, D), F32),
        ],
        [place, both_rel, *attn_pieces, cos, sin_a, sin_b, mask],
        1, 58, cost(0.1), "attention_forward",
    )
    recv = swap(part, pair_mask)
    scaled_one, inv_one, low_both, low_rel = call(
        first_norm,
        [
            jax.ShapeDtypeStruct((rows, D), F32),
            jax.ShapeDtypeStruct((rows, 1), F32),
            jax.ShapeDtypeStruct((tokens, D), BF),
            jax.ShapeDtypeStruct((QUADS, tokens, 256), BF),
        ],
        [place, both, part, recv, vec],
        1, 24, cost(1), "first_norm",
    )

    def const2(r, s):
        return (0, 0)

    def hide(r, s):
        return s[0] ^ jnp.minimum(r, QUADS - 1)

    def column(r):
        return jnp.maximum(r - QUADS, 0)

    by_core = mlp_all.reshape((QUADS, 2) + mlp_all.shape[1:])
    up_spec = pl.BlockSpec((8, 1, 256, 256), lambda r, s: (0, s[0] ^ r, s[1], 0))
    down_spec = pl.BlockSpec((1, 4, HIDE, 256), lambda r, s: (2 * (s[0] ^ r) + s[1], 0, 1, 0))
    hidden_spec = pl.BlockSpec(
        (1, tokens, HIDE), lambda r, s: (jnp.minimum(r, QUADS - 1), 0, 0)
    )
    column_spec = pl.BlockSpec((rows, 256), lambda r, s: (0, column(r)))
    hidden, slope, out_own, out_other = pl.pallas_call(
        feed_forward,
        out_shape=[
            jax.ShapeDtypeStruct((QUADS, tokens, HIDE), BF),
            jax.ShapeDtypeStruct((QUADS, tokens, HIDE), BF),
            jax.ShapeDtypeStruct((rows, D), F32),
            jax.ShapeDtypeStruct((rows, D), F32),
        ],
        grid_spec=pltpu.PrefetchScalarGridSpec(
            num_scalar_prefetch=1,
            grid=(2 * QUADS,),
            in_specs=[
                pl.BlockSpec((tokens, D), const2),
                pl.BlockSpec((16, D), const2),
                pl.BlockSpec((8, 1, 256, 256), lambda r, s: (0, hide(r, s), s[1], 0)),
                pl.BlockSpec(
                    (QUADS, 1, 1, HIDE, 256), lambda r, s: (0, s[1], column(r), 1, 0)
                ),
            ],
            out_specs=[hidden_spec, hidden_spec, column_spec, column_spec],
            scratch_shapes=[pltpu.VMEM((QUADS, tokens, HIDE), BF)],
        ),
        compiler_params=params(58),
        cost_estimate=cost(12),
        name="feed_forward",
    )(spot, low_both, vec, mlp_all, by_core)
    all_cols = n_hd * head_cols
    windows = pl.pallas_call(
        make_windows,
        out_shape=jax.ShapeDtypeStruct((all_cols, D), BF),
        grid=(1,),
        in_specs=[pl.BlockSpec((8, 4, 64, 256), lambda i: (0, 0, 16, 0))],
        out_specs=pl.BlockSpec((all_cols, D), lambda i: (0, 0)),
        scratch_shapes=[pltpu.VMEM((all_cols, D), F32)],
        compiler_params=params(58),
        cost_estimate=cost(1),
        name="make_windows",
    )(mlp_all)
    recv = swap(out_other, pair_mask)
    outputs, scaled_two, inv_two, own_proj = call(
        final_norm,
        [
            jax.ShapeDtypeStruct((rows, D), BF),
            jax.ShapeDtypeStruct((rows, D), F32),
            jax.ShapeDtypeStruct((rows, 1), F32),
            jax.ShapeDtypeStruct((all_cols, rows), BF),
        ],
        [scaled_one, out_own, recv, vec, windows],
        0, 16, cost(2.6), "final_norm",
    )
    projs = [own_proj] + [swap(own_proj, 0, k) for k in range(1, n_hd)]
    lanes = jnp.stack(
        [
            jnp.pad(question_lengths.astype(F32), (0, GROUP - question_lengths.shape[0])),
            jnp.pad(relevant_passage.astype(F32), (0, GROUP - relevant_passage.shape[0])),
        ]
    )
    grad_two, low_two, grad_heads, sums_two, scalars = call(
        soft_maxsim,
        [
            jax.ShapeDtypeStruct((rows, D), F32),
            jax.ShapeDtypeStruct((rows, D), BF),
            jax.ShapeDtypeStruct((2 * QUADS, all_cols + 16, GROUP), F32),
            jax.ShapeDtypeStruct((3, D), F32),
            jax.ShapeDtypeStruct((2, GROUP), F32),
        ],
        [place, logarithmic_warmth, lanes, *projs, windows, outputs, scaled_two, inv_two, vec],
        2, 24, cost(4.3), "soft_maxsim", [
            pltpu.VMEM((all_cols, rows), BF),
            pltpu.VMEM((EMB, (docs + 1) * rows), BF),
            pltpu.VMEM((rows, docs * rows), F32),
            pltpu.VMEM((rows, docs * rows), BF),
        ],
    )

    low_two_other = swap(low_two, pair_mask)

    def swap_head(a, mask):
        return swap(a, 0, mask)

    def finish_split(a, group):
        count = a.shape[0] // 2
        give = lax.dynamic_slice_in_dim(a, (1 - core) * count, count, 0)
        keep = lax.dynamic_slice_in_dim(a, core * count, count, 0)
        other = swap(give, pair_mask)
        keep = keep.reshape(count, -1, 1, group)
        other = other.reshape(count, -1, 1, group)
        whole = jnp.where(
            core == 0,
            jnp.concatenate([keep, other], axis=2),
            jnp.concatenate([other, keep], axis=2),
        ).reshape(count, -1)
        return scatter_low(whole).astype(F32)

    down_far = weight_grad(
        spot, hidden, (low_two, low_two_other), (1, 3), None, (), "down_far", 0.1
    )
    down_got = swap(down_far, x_mask)
    low_two_next = after(low_two, down_far)
    grad_pre, gn_own, gn_other, bias_up_grad = pl.pallas_call(
        feed_forward_back,
        out_shape=[
            jax.ShapeDtypeStruct((tokens, QUADS * HIDE), BF),
            jax.ShapeDtypeStruct((rows, D), F32),
            jax.ShapeDtypeStruct((rows, D), F32),
            jax.ShapeDtypeStruct((1, QUADS * HIDE), F32),
        ],
        grid_spec=pltpu.PrefetchScalarGridSpec(
            num_scalar_prefetch=1,
            grid=(QUADS,),
            in_specs=[
                pl.BlockSpec((rows, D), const2),
                pl.BlockSpec((rows, D), const2),
                pl.BlockSpec((1, tokens, HIDE), lambda r, s: (r, 0, 0)),
                up_spec,
                down_spec,
            ],
            out_specs=[
                pl.BlockSpec((tokens, HIDE), lambda r, s: (0, s[0] ^ r)),
                pl.BlockSpec((rows, D), const2),
                pl.BlockSpec((rows, D), const2),
                pl.BlockSpec((1, HIDE), lambda r, s: (0, s[0] ^ r)),
            ],
            scratch_shapes=[pltpu.VMEM((tokens, D), BF)],
        ),
        compiler_params=params(58),
        cost_estimate=cost(0.1),
        name="feed_forward_back",
    )(spot, low_two_next, low_two_other, slope, mlp_all, mlp_all)
    up_far = weight_grad(spot, low_rel, (grad_pre,), (2, 3), None, (), "up_far", 0.1)
    up_got = swap(up_far, y_mask)
    recv = swap(gn_other, pair_mask)
    grad_one, low_one, sums_one = call(
        first_norm_back,
        [
            jax.ShapeDtypeStruct((rows, D), F32),
            jax.ShapeDtypeStruct((rows, D), BF),
            jax.ShapeDtypeStruct((3, D), F32),
        ],
        [grad_two, after(gn_own, up_far), recv, scaled_one, inv_one, vec],
        0, 16, cost(0.1), "first_norm_back",
    )
    low_one_other = swap(low_one, pair_mask)
    grad_qkv, gx_own, gx_other, bias_qkv_grad = call(
        attention_backward,
        [
            jax.ShapeDtypeStruct((tokens, 3 * D // 2), BF),
            jax.ShapeDtypeStruct((rows, D), F32),
            jax.ShapeDtypeStruct((rows, D), F32),
            jax.ShapeDtypeStruct((1, 3 * D // 2), F32),
        ],
        [place, low_one, low_one_other, qkv, *attn_pieces, cos, sin_a, sin_b, mask],
        1, 58, cost(0.1), "attention_backward", [pltpu.VMEM((PAIRS, tokens, GROUP), BF)],
    )
    mixed = pl.pallas_call(
        pack_sums,
        out_shape=jax.ShapeDtypeStruct(grad_heads.shape, F32),
        grid=(1,),
        in_specs=[SMEM_SPEC]
        + [whole(a) for a in (sums_two, sums_one, bias_up_grad, bias_qkv_grad, scalars)]
        + [pl.BlockSpec(memory_space=pl.ANY)],
        out_specs=pl.BlockSpec((2 * QUADS, 16, GROUP), lambda i: (0, all_cols // 16, 0)),
        input_output_aliases={6: 0},
        compiler_params=params(24),
        cost_estimate=cost(0.1),
        name="pack_sums",
    )(spot, sums_two, sums_one, bias_up_grad, bias_qkv_grad, scalars, grad_heads)

    def tail(after_this, halves, blocks, places, adds, name, micros, kind=BF):
        return tail_grad(
            spot, both_rel, after(grad_qkv, *after_this), att, low_one, low_one_other,
            halves, blocks, places, adds, name, micros, kind,
        )

    def second(value, *others):
        return (after(value, *others), low_two_other)

    tail_args = (both_rel, grad_qkv, att, low_one, low_one_other)
    tail_a, tail_b = tail_pair(
        *tail_args, (((1, 0), (3, 0)), ((2, 1), (3, 1))), (), "tail_far", 0.1
    )
    a_got = swap(tail_a, x_mask)
    b_got = swap(tail_b, y_mask)

    down_z = weight_grad(
        spot, hidden, second(low_two, tail_b), (0, 2), (1, 3),
        ((down_got, 0, 1, 0, True),), "down_head", 6,
    )
    down_z1 = swap_head(down_z, 1)
    up_near = weight_grad(
        spot, low_rel, (after(grad_pre, down_z),), (1,), None,
        ((up_got, 1, 0, 0, True),), "up_near", 8,
    )
    up_last = swap(up_near, x_mask)
    down_zz = weight_grad(
        spot, hidden, second(low_two, up_near), (0, 2), (2,),
        ((down_got, 0, 1, 0, True), (down_z1, 1, 2, 0, False)), "down_head_near", 5,
    )
    down_z2 = swap_head(down_zz, 2)
    a_near, b_near = tail_pair(
        both_rel, after(grad_qkv, down_zz), att, low_one, low_one_other,
        (((2, 0),), ((1, 1),)), (a_got, b_got), "tail_near", 5,
    )
    a_last = swap(a_near, y_mask)
    b_last = swap(b_near, x_mask)
    up_adds = ((up_got, 0, 0, 0, True), (up_last, 0, 0, 0, True))
    up_z = weight_grad(
        spot, low_rel, (after(grad_pre, b_near),), (0,), (1, 3), up_adds, "up_head", 5
    )
    up_z1 = swap_head(up_z, 1)
    down_y = weight_grad(
        spot, hidden, second(low_two, up_z), (2,), (0,),
        ((down_got, 1, 0, 0, True), (down_z1, 2, 0, 0, False), (down_z2, 1, 0, 0, False)),
        "down_near", 0.1,
    )
    down_last = swap(down_y, y_mask)
    a_adds = ((a_got, 0, 0, True), (a_last, 0, 0, True))
    b_adds = ((b_got, 0, 0, True), (b_last, 0, 0, True))
    tail_z = tail((down_y,), (0, 1), (0,), (1, 3), a_adds + b_adds, "tail_head", 5)
    tail_z1 = swap_head(tail_z, 1)
    up_zz = weight_grad(
        spot, low_rel, (after(grad_pre, tail_z),), (0,), (2,),
        up_adds + ((up_z1, 1, 0, 0, False),), "up_head_near", 4,
    )
    up_z2 = swap_head(up_zz, 2)
    tail_zz = tail(
        (up_zz,), (0, 1), (0,), (2,),
        a_adds + ((tail_z1, 1, 0, False),) + b_adds + ((tail_z1, 1, 1, False),),
        "tail_head_near", 4,
    )
    tail_z2 = swap_head(tail_zz, 2)
    exact = BF if low_span > 1 else F32
    grad_w_down = weight_grad(
        spot, hidden, second(low_two, tail_zz), (0,), (0,),
        (
            (down_got, 0, 0, 0, True), (down_z1, 0, 0, 0, False),
            (down_z2, 0, 0, 0, False), (down_last, 0, 0, 0, False),
        ),
        "down_own", 4, exact,
    )[0]
    up_own = weight_grad(
        spot, low_rel, (after(grad_pre, grad_w_down),), (0,), (0,),
        up_adds + ((up_z1, 0, 0, 0, False), (up_z2, 0, 0, 0, False)), "up_own", 4,
    )[0]
    kept = tail(
        (up_own,), (0, 1), (0,), (0,),
        a_adds + ((tail_z1, 0, 0, False), (tail_z2, 0, 0, False))
        + b_adds + ((tail_z1, 0, 1, False), (tail_z2, 0, 1, False)),
        "tail_own", 4,
    ).reshape(256, 512)
    grad_w_down = scatter_low(grad_w_down).astype(F32)
    grad_w_up = finish_split(up_own, HIDE)
    grad_w_qkv = finish_split(kept[:, :qkv_cols], GROUP)
    kept_out = kept[:, qkv_cols:]
    grad_w_out = scatter_low(
        jnp.concatenate([kept_out[:GROUP], kept_out[GROUP:]], axis=1)
    ).astype(F32)
    mixed = jnp.repeat(mixed, low_span, axis=0) if low_span > 1 else mixed
    mixed = lax.psum_scatter(
        mixed.reshape(n_dp * (all_cols + 16), GROUP), "dp", scatter_dimension=0, tiled=True
    )
    shard = (head_cols + 16 + 31) // 32 * 32
    sums = jnp.pad(mixed[all_cols:], ((0, shard - head_cols - 16), (0, 0)))
    sums = jnp.broadcast_to(sums, (n_hd,) + sums.shape)
    mixed = jnp.concatenate([mixed[:all_cols].reshape(n_hd, head_cols, GROUP), sums], axis=1)
    mixed = lax.psum_scatter(
        mixed.reshape(n_hd * shard, GROUP), "head", scatter_dimension=0, tiled=True
    )
    head_rows = D // n_dp
    grad_w_heads = lax.dynamic_slice(
        mixed, (0, (dp % low_span) * head_rows), (head_cols, head_rows)
    ).T
    sums = mixed[head_cols : head_cols + 16]
    grad_tokens = grad_one + gx_own + swap(gx_other, pair_mask)

    place_in = (dp % low_span) * n_hd + hd
    mat = lax.dynamic_slice(sums[:9], (0, place_in * wide), (9, wide))
    mid = FF // n_all
    up_sum = lax.dynamic_slice(sums[9:13].reshape(-1), (place_in * mid,), (mid,))
    return (
        outputs,
        sums[13, 0:1],
        grad_tokens,
        grad_w_qkv,
        grad_w_out,
        grad_w_up,
        grad_w_down,
        grad_w_heads,
        mat[:5],
        up_sum,
        mat[5:7],
        mat[7:9],
        sums[14, 0:1],
    )


def solution(mesh):
    return jax.shard_map(
        on_device,
        mesh=mesh,
        in_specs=(
            P(("dp", "head"), None),
            P("dp", "head"),
            P("dp", "head"),
            P("dp", "head"),
            P("dp", "head"),
            P("dp", "head"),
            P(None, ("dp", "head")),
            P(("dp", "head")),
            P(None, ("dp", "head")),
            P(None, ("dp", "head")),
            P(),
            P("dp"),
            P("dp"),
            P("dp"),
        ),
        out_specs=(
            P(("dp", "head"), None),
            P(),
            P(("dp", "head"), None),
            P("dp", "head"),
            P("dp", "head"),
            P("dp", "head"),
            P("dp", "head"),
            P("dp", "head"),
            P(None, ("dp", "head")),
            P(("dp", "head")),
            P(None, ("dp", "head")),
            P(None, ("dp", "head")),
            P(),
        ),
        check_vma=False,
    )
```

```python
import jax
import jax.numpy as jnp
from jax import lax
from jax.experimental import pallas as pl
from jax.experimental.pallas import tpu as pltpu
from jax.sharding import PartitionSpec as P

D = 1024
HEADS = 16
HEAD_DIM = 64
FF = 4096
EMB = 128
EMB_MID = 96
EMB_SMALL = 64
QLEN = 32

EPS_NORM = 1e-05
EPS_UNIT = 1e-06
SHARPNESS = 0.05
ROPE_BASE = 10000.0
MASKED = -1000000000.0
SQRT_HALF = 0.7071067811865476
GAUSS_SCALE = 0.3989422804014327

BF = jnp.bfloat16
F32 = jnp.float32
STARTS = (0, EMB, EMB + EMB_MID)
WIDTHS = (EMB, EMB_MID, EMB_SMALL)
SLOTS = 3
QUADS = 4
GROUP = 128
HIDE = FF // 8


PAIRS = 4
VMEM_SPEC = pl.BlockSpec(memory_space=pltpu.VMEM)
SMEM_SPEC = pl.BlockSpec(memory_space=pltpu.SMEM)


def dot_nn(a, b):
    return lax.dot_general(a, b, (((1,), (0,)), ((), ())), preferred_element_type=F32)


def dot_tn(a, b):
    return lax.dot_general(a, b, (((0,), (0,)), ((), ())), preferred_element_type=F32)


def dot_nt(a, b):
    return lax.dot_general(a, b, (((1,), (1,)), ((), ())), preferred_element_type=F32)


def params(mib):
    return pltpu.CompilerParams(vmem_limit_bytes=mib << 20)


TIME_UNIT = 1150000000


def cost(micros):
    return pl.CostEstimate(flops=int(micros * TIME_UNIT), bytes_accessed=1, transcendentals=0)


def whole(a):
    zeros = (0,) * len(a.shape)
    return pl.BlockSpec(a.shape, lambda i: zeros, pipeline_mode=pl.Buffered(1))


def call(kernel, outs, args, n_smem, mib, estimate, name, scratch=()):
    return pl.pallas_call(
        kernel,
        out_shape=outs,
        grid=(1,),
        in_specs=[SMEM_SPEC] * n_smem + [whole(a) for a in args[n_smem:]],
        out_specs=[whole(a) for a in outs],
        scratch_shapes=list(scratch),
        compiler_params=params(mib),
        cost_estimate=estimate,
        name=name,
    )(*args)


def norm_parts(values):
    centred = values - jnp.mean(values, axis=-1, keepdims=True)
    variance = jnp.mean(centred * centred, axis=-1, keepdims=True)
    inverse = lax.rsqrt(variance + EPS_NORM)
    return centred * inverse, inverse


def norm_back(grad_out, scaled, inverse, gain):
    grad_scaled = grad_out * gain
    return inverse * (
        grad_scaled
        - jnp.mean(grad_scaled, axis=-1, keepdims=True)
        - scaled * jnp.mean(grad_scaled * scaled, axis=-1, keepdims=True)
    )


def pieces_of(a0, ax, ay, b0, by, bx):
    def piece(rq, rz):
        at = rz // 2
        if rz % 2 == 0:
            return [a0.at[at], ax.at[at], ay.at[0, at], ay.at[1, at]][rq]
        return [b0.at[at], bx.at[0, at], by.at[at], bx.at[1, at]][rq]

    return piece


def exit_tile(piece, rq, rz):
    return jnp.concatenate(
        [
            jnp.concatenate([piece(q, rz)[0:128, 384:512], piece(q, rz)[128:256, 384:512]], axis=1)
            for q in (rq, rq + 1)
        ],
        axis=0,
    )


def lanes_at(index, width=GROUP):
    return pl.ds(pl.multiple_of(index * width, width), width)


def turn(x, cos, sin_a, sin_b):
    return x * cos + pltpu.roll(x, 96, 1) * sin_a + pltpu.roll(x, 32, 1) * sin_b


def head_mask(h, shape):
    lane = lax.broadcasted_iota(jnp.int32, shape, 1)
    return (lane < HEAD_DIM) if h == 0 else (lane >= HEAD_DIM)


def stacked(a):
    zero = jnp.zeros_like(a)
    return jnp.concatenate(
        [jnp.where(head_mask(0, a.shape), a, zero), jnp.where(head_mask(1, a.shape), a, zero)],
        axis=0,
    )


def unstacked(a):
    half = a.shape[0] // 2
    top = a[:half]
    return jnp.where(head_mask(0, top.shape), top, a[half:])


def softmax_rows(q, k, mask):
    mask = jnp.concatenate([mask, mask], axis=0)
    s = jnp.where(mask > 0, dot_nt(q, k), MASKED)
    raised = jnp.exp(s - jnp.max(s, axis=-1, keepdims=True))
    return raised * (1.0 / jnp.sum(raised, axis=-1, keepdims=True))


def attention_forward(
    place, x, a0, ax, ay, b0, by, bx, cos, sin_a, sin_b, mask, qkv, att, part, vec
):
    quad, hd, core = place[0], place[1], place[5]
    piece = pieces_of(a0, ax, ay, b0, by, bx)
    rows = cos.shape[0]
    for rq in range(4):
        for c in range(2):
            at = slice(c * GROUP, (c + 1) * GROUP)
            total = piece(rq, 0)[256:272, at].astype(F32)
            for rz in range(1, 4):
                total += piece(rq, rz)[256:272, at].astype(F32)
            vec[:, lanes_at(2 * (quad ^ rq) + c)] = total
    for rz in range(4):
        z = hd ^ rz
        acc = dot_nn(x[0], piece(0, rz)[0:256, 0:384])
        for rq in range(1, 4):
            acc += dot_nn(x[rq], piece(rq, rz)[0:256, 0:384])
        for j in range(3):
            i = 3 * z + j
            scale = jnp.where(i < PAIRS, HEAD_DIM**-0.5, 1.0).astype(F32)
            near = vec[0:8, lanes_at(2 * (i % 4) + core)]
            row = lax.broadcasted_iota(jnp.int32, near.shape, 0)
            bias = jnp.sum(jnp.where(row == i // 4, near, 0.0), axis=0, keepdims=True)
            for b in range(2):
                here = acc[b * rows : (b + 1) * rows, j * GROUP : (j + 1) * GROUP]
                here = here + bias
                turned = turn(here, cos[...], sin_a[...], sin_b[...])
                here = jnp.where(i < 2 * PAIRS, turned, here) * scale
                qkv[b * rows : (b + 1) * rows, lanes_at(i)] = here.astype(BF)

    def one(it, carry):
        b, r = it // PAIRS, it % PAIRS
        i = quad ^ r
        row = pl.ds(pl.multiple_of(b * rows, rows), rows)
        q = qkv[row, pl.ds(pl.multiple_of(i * GROUP, GROUP), GROUP)]
        k = qkv[row, pl.ds(pl.multiple_of((PAIRS + i) * GROUP, GROUP), GROUP)]
        v = qkv[row, pl.ds(pl.multiple_of((2 * PAIRS + i) * GROUP, GROUP), GROUP)]
        probs = softmax_rows(stacked(q), k, mask[b])
        both = dot_nn(probs.astype(BF), v)
        att[r, row, :] = unstacked(both).astype(BF)
        return carry

    lax.fori_loop(0, 2 * PAIRS, one, 0)
    pairs = [jnp.concatenate([att[0], att[1]], axis=1), jnp.concatenate([att[2], att[3]], axis=1)]
    for rz in range(4):
        acc = dot_nn(pairs[0], exit_tile(piece, 0, rz)) + dot_nn(pairs[1], exit_tile(piece, 2, rz))
        part[:, lanes_at(hd ^ rz, 256)] = acc


def attention_backward(
    place, own, other, qkv, a0, ax, ay, b0, by, bx, cos, sin_a, sin_b, mask,
    grad_qkv, gx_own, gx_other, sums, ga,
):
    quad, hd = place[0], place[1]
    piece = pieces_of(a0, ax, ay, b0, by, bx)
    rows = cos.shape[0]
    for rq in (0, 2):
        sums_of = [None, None]
        for rz in range(4):
            w = exit_tile(piece, rq, rz)
            for b, grad in ((0, own), (1, other)):
                term = dot_nt(grad[:, lanes_at(hd ^ rz, 256)], w)
                sums_of[b] = term if sums_of[b] is None else sums_of[b] + term
        for b in range(2):
            at = slice(b * rows, (b + 1) * rows)
            ga[rq, at, :] = sums_of[b][:, 0:GROUP].astype(BF)
            ga[rq + 1, at, :] = sums_of[b][:, GROUP:].astype(BF)

    def one(it, carry):
        b, r = it // PAIRS, it % PAIRS
        i = quad ^ r
        row = pl.ds(pl.multiple_of(b * rows, rows), rows)
        at_q = pl.ds(pl.multiple_of(i * GROUP, GROUP), GROUP)
        at_k = pl.ds(pl.multiple_of((PAIRS + i) * GROUP, GROUP), GROUP)
        at_v = pl.ds(pl.multiple_of((2 * PAIRS + i) * GROUP, GROUP), GROUP)
        q, k, v = qkv[row, at_q], qkv[row, at_k], qkv[row, at_v]
        q_pair, grad_pair = stacked(q), stacked(ga[r, row, :])
        probs = softmax_rows(q_pair, k, mask[b])
        gp = dot_nt(grad_pair, v)
        gs = probs * (gp - jnp.sum(probs * gp, axis=-1, keepdims=True))
        gs = gs.astype(BF)
        gq = unstacked(dot_nn(gs, k))
        gk = dot_tn(gs, q_pair)
        gv = dot_tn(probs.astype(BF), grad_pair)
        c, sa, sb = cos[...], -sin_a[...], -sin_b[...]
        grad_qkv[row, at_q] = turn(gq * (HEAD_DIM**-0.5), c, sa, sb).astype(BF)
        grad_qkv[row, at_k] = turn(gk, c, sa, sb).astype(BF)
        grad_qkv[row, at_v] = gv.astype(BF)
        return carry

    lax.fori_loop(0, 2 * PAIRS, one, 0)
    for rq in range(4):
        at = pl.ds(pl.multiple_of((quad ^ rq) * 256, 256), 256)
        acc = None
        for rz in range(4):
            cols = pl.ds(pl.multiple_of((hd ^ rz) * 384, GROUP), 384)
            term = dot_nt(grad_qkv[:, cols], piece(rq, rz)[0:256, 0:384])
            acc = term if acc is None else acc + term
        gx_own[:, at] = acc[:rows]
        gx_other[:, at] = acc[rows:]
    sums[...] = jnp.sum(grad_qkv[...].astype(F32), axis=0, keepdims=True)


def first_norm(place, x, part, recv, vec, scaled_out, inv_out, low, rel_out):
    rows = scaled_out.shape[0]
    for b in range(2):
        sel = slice(b * rows, (b + 1) * rows)
        swapped = slice((1 - b) * rows, (2 - b) * rows)
        h = x[sel, :].astype(F32) + part[sel, :] + recv[swapped, :] + vec[3:4, :]
        scaled, inverse = norm_parts(h)
        low[sel, :] = (scaled * vec[5:6, :] + vec[7:8, :]).astype(BF)
        if b == 0:
            scaled_out[...] = scaled
            inv_out[...] = inverse
    for q in range(QUADS):
        rel_out[q, :, :] = low[:, lanes_at(place[0] ^ q, 256)]


def feed_forward(place, low, vec, wup, wdown, hidden_out, slope_out, own_out, other_out, kept):
    step = pl.program_id(0)
    rows = own_out.shape[0]

    @pl.when(step < QUADS)
    def _():
        for cb in range(2):
            cols = slice(cb * 256, (cb + 1) * 256)
            w = wup[:, 0, cb * 128 : (cb + 1) * 128, :].reshape(D, 256)
            bias = [
                vec[9 + 2 * cb + k : 10 + 2 * cb + k, lanes_at(2 * (place[0] ^ step) + place[1])]
                for k in range(2)
            ]
            pre = dot_nn(low[...], w) + jnp.concatenate(bias, axis=1)
            gate = 0.5 * (1.0 + lax.erf(pre * SQRT_HALF))
            hidden = (pre * gate).astype(BF)
            hidden_out[0, :, cols] = hidden
            kept[step, :, cols] = hidden
            slope_out[0, :, cols] = (
                gate + pre * jnp.exp(-0.5 * pre * pre) * GAUSS_SCALE
            ).astype(BF)

    @pl.when(step >= QUADS)
    def _():
        acc = dot_nn(kept[0], wdown[place[0], 0, 0])
        for r in range(1, QUADS):
            acc += dot_nn(kept[r], wdown[place[0] ^ r, 0, 0])
        own_out[...] = acc[:rows]
        other_out[...] = acc[rows:]


def feed_forward_back(
    place, own, other, slope, wup, wdown, pre_out, own_out, other_out, sums, both
):
    r = pl.program_id(0)
    rows = own.shape[0]

    @pl.when(r == 0)
    def _():
        both[0:rows, :] = own[...]
        both[rows:, :] = other[...]
        own_out[...] = jnp.zeros_like(own_out)
        other_out[...] = jnp.zeros_like(other_out)

    acc = dot_nt(both[:, 0:256], wdown[0, 0])
    for z in range(1, 4):
        acc += dot_nt(both[:, z * 256 : (z + 1) * 256], wdown[0, z])
    grad = (acc * slope[0].astype(F32)).astype(BF)
    pre_out[...] = grad
    sums[...] = jnp.sum(grad.astype(F32), axis=0, keepdims=True)
    total = None
    for cb in range(2):
        w = wup[:, 0, cb * 128 : (cb + 1) * 128, :].reshape(D, 256)
        term = dot_nt(pre_out[:, cb * 256 : (cb + 1) * 256], w)
        total = term if total is None else total + term
    own_out[...] += total[:rows]
    other_out[...] += total[rows:]


def final_norm(scaled_one, part, recv, vec, windows, out, scaled_out, inv_out, proj):
    h = scaled_one[...] * vec[5:6, :] + vec[7:8, :] + part[...] + recv[...] + vec[4:5, :]
    scaled, inverse = norm_parts(h)
    scaled_out[...] = scaled
    inv_out[...] = inverse
    low = (scaled * vec[6:7, :] + vec[8:9, :]).astype(BF)
    out[...] = low
    proj[...] = dot_nt(windows[...], low).astype(BF)


def soft_maxsim(
    place, temp, lanes, proj_0, proj_1, proj_2, proj_3, windows, out, scaled, inverse_two, vec,
    grad_two, low_two, grad_heads, sums, scalars, gproj, units, shares, similar_low,
):
    hd = place[1]
    rows = out.shape[0]
    projs = (proj_0, proj_1, proj_2, proj_3)
    docs = len(projs) - 1
    row = lax.broadcasted_iota(jnp.int32, (rows, GROUP), 0)
    lane = lax.broadcasted_iota(jnp.int32, (rows, GROUP), 1)
    member = (row // QLEN == lane).astype(F32)
    lens = lanes[0:1, :]
    len_row = jnp.sum(member * lens, axis=1, keepdims=True)
    valid = (row % QLEN).astype(F32) < len_row
    queries = rows // QLEN
    used = lax.broadcasted_iota(jnp.int32, (1, GROUP), 1) < queries
    weight = jnp.where(valid, member, 0.0) / jnp.where(used, lens, 1.0)
    warmth = jnp.exp(jnp.full((1, GROUP), temp[0], F32))
    key = lax.broadcasted_iota(jnp.int32, (rows, rows), 1)
    loss = jnp.zeros((1, GROUP), F32)
    grad_temp = jnp.zeros((1, GROUP), F32)
    for slot in range(SLOTS):
        width = WIDTHS[slot]
        cols = slice(STARTS[slot], STARTS[slot] + width)

        def unit_of(away):
            mapped = projs[away][cols, :].astype(F32)
            inverse = lax.rsqrt(jnp.sum(mapped * mapped, axis=0, keepdims=True) + EPS_UNIT)
            return mapped * inverse, inverse

        for away in range(docs + 1):
            units[0:width, lanes_at(hd ^ away, rows)] = unit_of(away)[0].astype(BF)
        logits = []
        for d in range(docs):
            doc = slice((d + 1) * rows, (d + 2) * rows)
            similar = dot_tn(units[0:width, 0:rows], units[0:width, doc]) * (1.0 / SHARPNESS)
            similar = jnp.where(key < place[2 + d], similar, MASKED)
            top = jnp.max(similar, axis=-1, keepdims=True)
            raised = jnp.exp(similar - top)
            total = jnp.sum(raised, axis=-1, keepdims=True)
            soft = SHARPNESS * (top + jnp.log(total))
            shares[:, d * rows : (d + 1) * rows] = raised * (1.0 / total)
            logits.append(jnp.sum(soft * weight, axis=0, keepdims=True) / warmth)
        top_logit = jnp.maximum(jnp.maximum(logits[0], logits[1]), logits[2])
        exps = [jnp.exp(x - top_logit) for x in logits]
        total = exps[0] + exps[1] + exps[2]
        hits = [(lanes[1:2, :] == float(d)).astype(F32) for d in range(docs)]
        picked = logits[0] * hits[0] + logits[1] * hits[1] + logits[2] * hits[2]
        loss += jnp.where(used, top_logit + jnp.log(total) - picked, 0.0) / queries
        for d in range(docs):
            grad = jnp.where(used, exps[d] / total - hits[d], 0.0) / queries
            grad_temp -= grad * logits[d]
            grad_soft = jnp.sum(weight * (grad / warmth), axis=1, keepdims=True)
            at = slice(d * rows, (d + 1) * rows)
            similar_low[:, at] = (grad_soft * shares[:, at]).astype(BF)

        own = jnp.maximum(hd - 1, 0)
        at = pl.ds(pl.multiple_of(own * rows, rows), rows)
        from_docs = dot_nt(units[0:width, rows:], similar_low[...])
        from_queries = dot_nn(units[0:width, 0:rows], similar_low[:, at])
        grad = jnp.where(hd == 0, from_docs, from_queries)
        unit, inverse = unit_of(0)
        gproj[cols, :] = (
            inverse * (grad - unit * jnp.sum(grad * unit, axis=0, keepdims=True))
        ).astype(BF)

    scalars[0:1, :] = loss
    scalars[1:2, :] = grad_temp
    grad_final = dot_tn(gproj[...], windows[...])
    xhat = scaled[...]
    grad = norm_back(grad_final, xhat, inverse_two[...], vec[6:7, :])
    grad_two[...] = grad
    low_two[...] = grad.astype(BF)
    sums[0:1, :] = jnp.sum(grad_final * xhat, axis=0, keepdims=True)
    sums[1:2, :] = jnp.sum(grad_final, axis=0, keepdims=True)
    sums[2:3, :] = jnp.sum(low_two[...].astype(F32), axis=0, keepdims=True)
    heads = dot_nn(gproj[...], out[...])
    for t in range(2 * QUADS):
        grad_heads[t, 0 : heads.shape[0], :] = heads[:, t * GROUP : (t + 1) * GROUP]


def first_norm_back(grad_two, own, recv, scaled, inverse, vec, grad_one, low_one, sums):
    grad_out = grad_two[...] + own[...] + recv[...]
    xhat = scaled[...]
    grad = norm_back(grad_out, xhat, inverse[...], vec[5:6, :])
    grad_one[...] = grad
    low_one[...] = grad.astype(BF)
    sums[0:1, :] = jnp.sum(grad_out * xhat, axis=0, keepdims=True)
    sums[1:2, :] = jnp.sum(grad_out, axis=0, keepdims=True)
    sums[2:3, :] = jnp.sum(low_one[...].astype(F32), axis=0, keepdims=True)


def weight_grad(spot, lhs, rhs, blocks, places, adds, name, micros, kind=BF):
    tokens, width = lhs.shape[1:]
    whole_cols = places is None
    places = (None,) if whole_cols else places
    count = len(places)
    tile = rhs[0].shape[1] // (1 if whole_cols else 4)
    step = (blocks[1] - blocks[0]) if len(blocks) > 1 else 0
    parts = len(rhs)
    span = tokens // parts
    n_add = len(adds)

    def column(s, place):
        return 0 if place is None else s[2] ^ place

    def kernel(spot_ref, lhs_ref, *refs):
        out = refs[-1]
        for k in range(count):
            total = None
            for p in range(parts):
                term = dot_tn(lhs_ref[0, p * span : (p + 1) * span, :], refs[k * parts + p][...])
                total = term if total is None else total + term
            for add in refs[count * parts + k * n_add : count * parts + (k + 1) * n_add]:
                total += add[0].astype(F32)
            out[k] = total.astype(kind)

    specs = [pl.BlockSpec((1, tokens, width), lambda i, s: (blocks[0] + step * i, 0, 0))]
    for place in places:
        specs += [pl.BlockSpec((span, tile), lambda i, s, c=place: (0, column(s, c)))] * parts
    for k, place in enumerate(places):
        for _, at, per_block, per_place, aligned in adds:
            at += per_place * k
            if aligned:
                index = lambda i, s, at=at, n=per_block, c=place: (at + n * i, 0, column(s, c))
            else:
                index = lambda i, s, at=at, n=per_block: (at + n * i, 0, 0)
            specs.append(pl.BlockSpec((1, width, tile), index))
    return pl.pallas_call(
        kernel,
        out_shape=jax.ShapeDtypeStruct((len(blocks) * count, width, tile), kind),
        grid_spec=pltpu.PrefetchScalarGridSpec(
            num_scalar_prefetch=1,
            grid=(len(blocks),),
            in_specs=specs,
            out_specs=pl.BlockSpec((count, width, tile), lambda i, s: (i, 0, 0)),
        ),
        compiler_params=params(24),
        cost_estimate=cost(micros),
        name=name,
    )(spot, lhs, *(list(rhs) * count), *([add[0] for add in adds] * count))


def tail_grad(spot, x, grad_qkv, att, own, other, halves, blocks, places, adds, name, micros, finish=False):
    tokens = x.shape[1]
    whole_cols = places is None
    places = (None,) if whole_cols else places
    count = len(places)
    heads = 4 if whole_cols else 1
    step = (blocks[1] - blocks[0]) if len(blocks) > 1 else 0
    n_half = len(halves)
    rows = tokens // 2
    n_add = len(adds)
    per = n_add // n_half
    lane_blocks = 1 if whole_cols else n_half

    def column(s, place):
        return 0 if place is None else s[2] ^ place

    def kernel(spot_ref, x_ref, att_ref, *refs):
        out = refs[-1]
        lefts = []
        at_add = count * (1 + 2 * lane_blocks)
        for c in range(count):
            qkv_ref, *pair = refs[c * (1 + 2 * lane_blocks) : (c + 1) * (1 + 2 * lane_blocks)]
            for k, half in enumerate(halves):
                left_all = dot_tn(x_ref[0, :, half * GROUP : (half + 1) * GROUP], qkv_ref[...])
                for z in range(heads):
                    if whole_cols:
                        lanes = slice((2 * z + half) * GROUP, (2 * z + half + 1) * GROUP)
                        up, down = pair[0][:, lanes], pair[1][:, lanes]
                    else:
                        up, down = pair[2 * k][...], pair[2 * k + 1][...]
                    right = dot_tn(att_ref[0, 0:rows, :], up) + dot_tn(att_ref[0, rows:, :], down)
                    left = left_all[:, z * 384 : (z + 1) * 384]
                    first = at_add + c * n_add + k * per
                    lo = z * 512
                    for add in refs[first : first + per]:
                        left += add[0, 0, :, lo : lo + 384].astype(F32)
                        right += add[0, 0, :, lo + 384 : lo + 512].astype(F32)
                    if finish:
                        lefts.append(left)
                        out[:, half * GROUP : (half + 1) * GROUP] = right
                        continue
                    out[c, k, :, lo : lo + 384] = left.astype(BF)
                    out[c, k, :, lo + 384 : lo + 512] = right.astype(BF)
        if finish:
            mine = spot_ref[1] == 0
            refs[-3][...] = jnp.where(mine, lefts[1], lefts[0]).astype(BF)
            refs[-2][...] = jnp.where(mine, lefts[0], lefts[1])

    specs = [
        pl.BlockSpec((1, tokens, 256), lambda i, s: (blocks[0] + step * i, 0, 0)),
        pl.BlockSpec((1, tokens, GROUP), lambda i, s: (blocks[0] + step * i, 0, 0)),
    ]
    inputs = []
    for place in places:
        specs.append(pl.BlockSpec((tokens, 384 * heads), lambda i, s, c=place: (0, column(s, c))))
        inputs.append(grad_qkv)
        for half in halves[:lane_blocks]:
            if whole_cols:
                index = lambda i, s: (0, 0)
            else:
                index = lambda i, s, c=place, half=half: (0, 2 * column(s, c) + half)
            specs += [pl.BlockSpec((rows, D if whole_cols else GROUP), index)] * 2
            inputs += [own, other]
    for place in places:
        for a, at, k, aligned in adds:
            if aligned:
                index = lambda i, s, at=at, k=k, c=place: (at, k, 0, column(s, c))
            else:
                index = lambda i, s, at=at, k=k: (at, k, 0, 0)
            specs.append(pl.BlockSpec((1, 1, GROUP, 512 * heads), index))
            inputs.append(a)
    out_shape = jax.ShapeDtypeStruct((len(blocks) * count, n_half, GROUP, 512 * heads), BF)
    out_spec = pl.BlockSpec((count, n_half, GROUP, 512 * heads), lambda i, s: (i, 0, 0, 0))
    if finish:
        out_shape = [
            jax.ShapeDtypeStruct((GROUP, 384), BF),
            jax.ShapeDtypeStruct((GROUP, 384), F32),
            jax.ShapeDtypeStruct((GROUP, 2 * GROUP), F32),
        ]
        out_spec = [pl.BlockSpec(a.shape, lambda i, s: (0, 0)) for a in out_shape]
    return pl.pallas_call(
        kernel,
        out_shape=out_shape,
        grid_spec=pltpu.PrefetchScalarGridSpec(
            num_scalar_prefetch=1,
            grid=(len(blocks),),
            in_specs=specs,
            out_specs=out_spec,
        ),
        compiler_params=params(58),
        cost_estimate=cost(micros),
        name=name,
    )(spot, x, att, *inputs)


def tail_pair(x, grad_qkv, att, own, other, jobs, adds, name, micros):
    tokens = x.shape[1]
    rows = tokens // 2

    def kernel(x_ref, qkv_ref, att_ref, own_ref, other_ref, *refs):
        for n, blocks in enumerate(jobs):
            out = refs[len(adds) + n]
            for k, (r, half) in enumerate(blocks):
                left_all = dot_tn(x_ref[r, :, half * GROUP : (half + 1) * GROUP], qkv_ref[...])
                for z in range(4):
                    lanes = slice((2 * z + half) * GROUP, (2 * z + half + 1) * GROUP)
                    right = dot_tn(att_ref[r, 0:rows, :], own_ref[:, lanes])
                    right += dot_tn(att_ref[r, rows:, :], other_ref[:, lanes])
                    left = left_all[:, z * 384 : (z + 1) * 384]
                    lo = z * 512
                    if adds:
                        left += refs[n][0, 0, :, lo : lo + 384].astype(F32)
                        right += refs[n][0, 0, :, lo + 384 : lo + 512].astype(F32)
                    out[k, 0, :, lo : lo + 384] = left.astype(BF)
                    out[k, 0, :, lo + 384 : lo + 512] = right.astype(BF)

    outs = [jax.ShapeDtypeStruct((len(blocks), 1, GROUP, 2048), BF) for blocks in jobs]
    specs = [whole(a) for a in (x, grad_qkv, att, own, other)]
    specs += [pl.BlockSpec((1, 1, GROUP, 2048), lambda i: (1, 0, 0, 0))] * len(adds)
    return pl.pallas_call(
        kernel,
        out_shape=outs,
        grid=(1,),
        in_specs=specs,
        out_specs=[whole(a) for a in outs],
        compiler_params=params(24 if adds else 58),
        cost_estimate=cost(micros),
        name=name,
    )(x, grad_qkv, att, own, other, *adds)


def pack_sums(spot, two, one, up, qkv, scalars, heads, out):
    core, hd = spot[1], spot[2]
    out[...] = jnp.zeros_like(out)
    for i in range(3 * PAIRS):
        out[2 * (i % 4) + core, i // 4 : i // 4 + 1, :] = qkv[0:1, i * GROUP : (i + 1) * GROUP]
    for i in range(4 * QUADS):
        out[2 * (i // 4) + core, 9 + i % 4 : 10 + i % 4, :] = up[
            0:1, i * GROUP : (i + 1) * GROUP
        ]
    once = jnp.where(hd == 0, 1.0, 0.0).astype(F32)
    totals = [jnp.sum(scalars[k : k + 1, :], axis=1, keepdims=True) * once for k in range(2)]
    for t in range(2 * QUADS):
        at = slice(t * GROUP, (t + 1) * GROUP)
        out[t, 3:4, :] = one[2:3, at]
        out[t, 4:5, :] = two[2:3, at]
        out[t, 5:6, :] = one[0:1, at]
        out[t, 6:7, :] = two[0:1, at]
        out[t, 7:8, :] = one[1:2, at]
        out[t, 8:9, :] = two[1:2, at]
        for k in range(2):
            out[t, 13 + k : 14 + k, :] = jnp.broadcast_to(totals[k], (1, GROUP))


def pack_matrices(up, down, heads, out):
    rows = up.shape[0]
    groups = up.shape[1] // 256
    for i in range(groups):
        out[i * rows : (i + 1) * rows, :] = up[:, i * 256 : (i + 1) * 256]
    at = groups * rows
    out[at : at + down.shape[0], :] = down[...]
    at += down.shape[0]
    out[at : at + 64, 0:GROUP] = heads[0:64, :]
    out[at : at + 64, GROUP:] = heads[64:, :]


def make_windows(tiles, windows, wide):
    cols = windows.shape[0] // 4
    for dp in range(2 * QUADS):
        at = slice(dp * GROUP, (dp + 1) * GROUP)
        for z in range(4):
            lo = z * cols
            wide[lo : lo + 64, at] = tiles[dp, z, :, 0:GROUP].astype(F32)
            rest = tiles[dp, z, 0:16, GROUP:].astype(F32)
            wide[lo + 64 : lo + cols, at] = rest[0 : cols - 64, :]
    windows[...] = wide[...].astype(BF)


def on_device(
    layer_entries,
    triple_projection_matrix,
    attention_exit_matrix,
    expand_matrix,
    contract_matrix,
    nested_projector,
    offset_model_width,
    offset_expanded,
    standardize_factor,
    standardize_offset,
    logarithmic_warmth,
    passage_lengths_each,
    question_lengths,
    relevant_passage,
):
    n_dp = lax.axis_size("dp")
    n_hd = lax.axis_size("head")
    n_all = n_dp * n_hd
    dp = lax.axis_index("dp")
    hd = lax.axis_index("head")
    low_span = n_dp // 8
    quad = dp // (2 * low_span)
    core = (dp // low_span) % 2
    pair_mask = low_span
    x_mask = 2 * low_span
    y_mask = 4 * low_span

    def swap(a, dp_mask=0, hd_mask=0):
        pairs = [
            (d * n_hd + h, (d ^ dp_mask) * n_hd + (h ^ hd_mask))
            for d in range(n_dp)
            for h in range(n_hd)
        ]
        return lax.ppermute(a, ("dp", "head"), pairs)

    def after(value, *others):
        return lax.optimization_barrier((value, *others))[0]

    def joined(bit, own, other):
        return jnp.where(
            bit == 0, jnp.concatenate([own, other], 0), jnp.concatenate([other, own], 0)
        )

    def gather_low(a):
        span = 1
        while span < low_span:
            a = joined((dp // span) % 2, a, swap(a, span))
            span *= 2
        return a

    def scatter_low(a):
        span = low_span // 2
        while span >= 1:
            half = a.shape[0] // 2
            bit = (dp // span) % 2
            give = lax.dynamic_slice_in_dim(a, (1 - bit) * half, half, 0)
            keep = lax.dynamic_slice_in_dim(a, bit * half, half, 0)
            a = (keep.astype(F32) + swap(give, span).astype(F32)).astype(BF)
            span //= 2
        return a

    rows = layer_entries.shape[0]
    docs = passage_lengths_each.shape[0]

    wup_low = gather_low(expand_matrix)
    col_blocks = wup_low.shape[1] // 256
    heads_low = gather_low(nested_projector)
    head_cols = heads_low.shape[1]
    heads_low = jnp.pad(heads_low.T, ((0, GROUP - head_cols), (0, 0)))
    wdown_low = gather_low(contract_matrix)
    (packed_mlp,) = call(
        pack_matrices,
        [jax.ShapeDtypeStruct((wup_low.shape[0] * col_blocks + wdown_low.shape[0] + 64, 256), BF)],
        [wup_low, wdown_low, heads_low],
        0, 16, cost(0.1), "pack_matrices",
    )
    if low_span > 1:
        dp_groups = [
            [((q * 2 + k) * low_span + s) for q in range(QUADS) for k in range(2)]
            for s in range(low_span)
        ]
        mlp_all = lax.all_gather(
            lax.all_gather(packed_mlp, "head"), "dp", axis_index_groups=dp_groups
        )
    else:
        mlp_all = lax.all_gather(packed_mlp, ("dp", "head"))
    mlp_all = mlp_all.reshape((8, n_hd) + packed_mlp.shape)

    partner_rows = swap(layer_entries, pair_mask)
    lens_own = jnp.concatenate([passage_lengths_each, question_lengths])
    lens_partner = swap(lens_own, pair_mask)
    both = jnp.concatenate([layer_entries, partner_rows], axis=0)
    order = [quad ^ r for r in range(QUADS)]
    both_rel = jnp.stack(
        [lax.dynamic_slice(both, (0, order[r] * 256), (2 * rows, 256)) for r in range(QUADS)]
    )

    wide = offset_model_width.shape[1]
    mine = (jnp.arange(n_hd) == hd).astype(BF)
    vectors = jnp.concatenate([offset_model_width, standardize_factor, standardize_offset], axis=0)
    n_vec = vectors.shape[0]
    vectors = gather_low(vectors[None]).transpose(1, 0, 2)
    vectors = (vectors[:, :, None, :] * mine[None, None, :, None]).reshape(n_vec, GROUP)
    middle = gather_low(offset_expanded[None])
    middle = (middle[:, None, :] * mine[None, :, None]).reshape(4, GROUP)
    vectors = jnp.concatenate([vectors, middle, jnp.zeros((16 - n_vec - 4, GROUP), BF)], axis=0)

    wqkv_low = gather_low(triple_projection_matrix)
    parts = wqkv_low.reshape(wqkv_low.shape[0], -1, 2, GROUP)
    keep, give = (
        lax.dynamic_index_in_dim(parts, k, 2, False).reshape(wqkv_low.shape[0], -1)
        for k in (core, 1 - core)
    )
    qkv_cols = keep.shape[1]
    k_rows = keep.shape[0]
    other = jnp.pad(vectors, ((0, 0), (0, qkv_cols - GROUP)))
    other = swap(jnp.concatenate([give, other], axis=0), pair_mask)
    wout_low = gather_low(attention_exit_matrix)
    wout_own = jnp.concatenate([wout_low[:, :GROUP], wout_low[:, GROUP:]], axis=0)
    vectors = jnp.where(
        core == 0,
        jnp.concatenate([vectors, other[k_rows:, :GROUP]], axis=1),
        jnp.concatenate([other[k_rows:, :GROUP], vectors], axis=1),
    )
    packed = jnp.concatenate(
        [
            jnp.concatenate([joined(core, keep, other[:k_rows]), wout_own], axis=1),
            jnp.pad(vectors, ((0, 0), (0, qkv_cols + GROUP - 2 * GROUP))),
        ],
        axis=0,
    )[None]

    a0 = jnp.concatenate([packed, swap(packed, 0, 2)], axis=0)
    b0 = swap(a0, 0, 1)
    ax = swap(a0, x_mask)
    by = swap(b0, y_mask)
    ay = swap(jnp.stack([a0, ax]), y_mask)
    bx = swap(jnp.stack([b0, by]), x_mask)
    attn_pieces = (a0, ax, ay, b0, by, bx)
    spot = jnp.stack([quad, core, hd]).astype(jnp.int32)

    row_ids = jnp.arange(rows, dtype=jnp.int32)
    is_query = hd == 0

    def valid_of(lens):
        doc_here = lens[jnp.maximum(hd - 1, 0)]
        return jnp.where(
            is_query, row_ids % QLEN < jnp.repeat(lens[docs:], QLEN), row_ids < doc_here
        )

    valid = jnp.stack([valid_of(lens_own), valid_of(lens_partner)])
    segment = jnp.where(is_query, row_ids // QLEN, 0)
    position = jnp.where(is_query, row_ids % QLEN, row_ids)
    mask = ((segment[:, None] == segment[None, :])[None] & valid[:, None, :]).astype(F32)
    halfway = HEAD_DIM // 2
    powers = jnp.arange(halfway, dtype=F32) * (2.0 / HEAD_DIM)
    angles = position.astype(F32)[:, None] * (ROPE_BASE ** (-powers))[None, :]
    cosine, sine = jnp.cos(angles), jnp.sin(angles)
    none = jnp.zeros_like(sine)
    cos = jnp.concatenate([cosine] * 4, axis=1)
    sin_a = jnp.concatenate([-sine, none] * 2, axis=1)
    sin_b = jnp.concatenate([none, sine] * 2, axis=1)
    place = jnp.concatenate(
        [
            jnp.stack([quad, hd]).astype(jnp.int32),
            passage_lengths_each,
            core.reshape(1).astype(jnp.int32),
        ]
    ).astype(jnp.int32)
    tokens = 2 * rows

    qkv, att, part, vec = call(
        attention_forward,
        [
            jax.ShapeDtypeStruct((tokens, 3 * D // 2), BF),
            jax.ShapeDtypeStruct((PAIRS, tokens, GROUP), BF),
            jax.ShapeDtypeStruct((tokens, D), F32),
            jax.ShapeDtypeStruct((16, D), F32),
        ],
        [place, both_rel, *attn_pieces, cos, sin_a, sin_b, mask],
        1, 58, cost(0.1), "attention_forward",
    )
    recv = swap(part, pair_mask)
    scaled_one, inv_one, low_both, low_rel = call(
        first_norm,
        [
            jax.ShapeDtypeStruct((rows, D), F32),
            jax.ShapeDtypeStruct((rows, 1), F32),
            jax.ShapeDtypeStruct((tokens, D), BF),
            jax.ShapeDtypeStruct((QUADS, tokens, 256), BF),
        ],
        [place, both, part, recv, vec],
        1, 24, cost(1), "first_norm",
    )

    def const2(r, s):
        return (0, 0)

    def hide(r, s):
        return s[0] ^ jnp.minimum(r, QUADS - 1)

    def column(r):
        return jnp.maximum(r - QUADS, 0)

    by_core = mlp_all.reshape((QUADS, 2) + mlp_all.shape[1:])
    up_spec = pl.BlockSpec((8, 1, 256, 256), lambda r, s: (0, s[0] ^ r, s[1], 0))
    down_spec = pl.BlockSpec((1, 4, HIDE, 256), lambda r, s: (2 * (s[0] ^ r) + s[1], 0, 1, 0))
    hidden_spec = pl.BlockSpec(
        (1, tokens, HIDE), lambda r, s: (jnp.minimum(r, QUADS - 1), 0, 0)
    )
    column_spec = pl.BlockSpec((rows, 256), lambda r, s: (0, column(r)))
    hidden, slope, out_own, out_other = pl.pallas_call(
        feed_forward,
        out_shape=[
            jax.ShapeDtypeStruct((QUADS, tokens, HIDE), BF),
            jax.ShapeDtypeStruct((QUADS, tokens, HIDE), BF),
            jax.ShapeDtypeStruct((rows, D), F32),
            jax.ShapeDtypeStruct((rows, D), F32),
        ],
        grid_spec=pltpu.PrefetchScalarGridSpec(
            num_scalar_prefetch=1,
            grid=(2 * QUADS,),
            in_specs=[
                pl.BlockSpec((tokens, D), const2),
                pl.BlockSpec((16, D), const2),
                pl.BlockSpec((8, 1, 256, 256), lambda r, s: (0, hide(r, s), s[1], 0)),
                pl.BlockSpec(
                    (QUADS, 1, 1, HIDE, 256), lambda r, s: (0, s[1], column(r), 1, 0)
                ),
            ],
            out_specs=[hidden_spec, hidden_spec, column_spec, column_spec],
            scratch_shapes=[pltpu.VMEM((QUADS, tokens, HIDE), BF)],
        ),
        compiler_params=params(58),
        cost_estimate=cost(12),
        name="feed_forward",
    )(spot, low_both, vec, mlp_all, by_core)
    all_cols = n_hd * head_cols
    windows = pl.pallas_call(
        make_windows,
        out_shape=jax.ShapeDtypeStruct((all_cols, D), BF),
        grid=(1,),
        in_specs=[pl.BlockSpec((8, 4, 64, 256), lambda i: (0, 0, 16, 0))],
        out_specs=pl.BlockSpec((all_cols, D), lambda i: (0, 0)),
        scratch_shapes=[pltpu.VMEM((all_cols, D), F32)],
        compiler_params=params(58),
        cost_estimate=cost(1),
        name="make_windows",
    )(mlp_all)
    recv = swap(out_other, pair_mask)
    outputs, scaled_two, inv_two, own_proj = call(
        final_norm,
        [
            jax.ShapeDtypeStruct((rows, D), BF),
            jax.ShapeDtypeStruct((rows, D), F32),
            jax.ShapeDtypeStruct((rows, 1), F32),
            jax.ShapeDtypeStruct((all_cols, rows), BF),
        ],
        [scaled_one, out_own, recv, vec, windows],
        0, 16, cost(2.6), "final_norm",
    )
    projs = [own_proj] + [swap(own_proj, 0, k) for k in range(1, n_hd)]
    lanes = jnp.stack(
        [
            jnp.pad(question_lengths.astype(F32), (0, GROUP - question_lengths.shape[0])),
            jnp.pad(relevant_passage.astype(F32), (0, GROUP - relevant_passage.shape[0])),
        ]
    )
    grad_two, low_two, grad_heads, sums_two, scalars = call(
        soft_maxsim,
        [
            jax.ShapeDtypeStruct((rows, D), F32),
            jax.ShapeDtypeStruct((rows, D), BF),
            jax.ShapeDtypeStruct((2 * QUADS, all_cols + 16, GROUP), F32),
            jax.ShapeDtypeStruct((3, D), F32),
            jax.ShapeDtypeStruct((2, GROUP), F32),
        ],
        [place, logarithmic_warmth, lanes, *projs, windows, outputs, scaled_two, inv_two, vec],
        2, 24, cost(4.3), "soft_maxsim", [
            pltpu.VMEM((all_cols, rows), BF),
            pltpu.VMEM((EMB, (docs + 1) * rows), BF),
            pltpu.VMEM((rows, docs * rows), F32),
            pltpu.VMEM((rows, docs * rows), BF),
        ],
    )

    low_two_other = swap(low_two, pair_mask)

    def swap_head(a, mask):
        return swap(a, 0, mask)

    def finish_split(a, group):
        count = a.shape[0] // 2
        give = lax.dynamic_slice_in_dim(a, (1 - core) * count, count, 0)
        keep = lax.dynamic_slice_in_dim(a, core * count, count, 0)
        return joined_columns(keep, swap(give, pair_mask), group)

    def joined_columns(keep, other, group):
        count = keep.shape[0]
        keep = keep.reshape(count, -1, 1, group)
        other = other.reshape(count, -1, 1, group)
        whole = jnp.where(
            core == 0,
            jnp.concatenate([keep, other], axis=2),
            jnp.concatenate([other, keep], axis=2),
        ).reshape(count, -1)
        return scatter_low(whole).astype(F32)

    down_far = weight_grad(
        spot, hidden, (low_two, low_two_other), (1, 3), None, (), "down_far", 0.1
    )
    down_got = swap(down_far, x_mask)
    low_two_next = after(low_two, down_far)
    grad_pre, gn_own, gn_other, bias_up_grad = pl.pallas_call(
        feed_forward_back,
        out_shape=[
            jax.ShapeDtypeStruct((tokens, QUADS * HIDE), BF),
            jax.ShapeDtypeStruct((rows, D), F32),
            jax.ShapeDtypeStruct((rows, D), F32),
            jax.ShapeDtypeStruct((1, QUADS * HIDE), F32),
        ],
        grid_spec=pltpu.PrefetchScalarGridSpec(
            num_scalar_prefetch=1,
            grid=(QUADS,),
            in_specs=[
                pl.BlockSpec((rows, D), const2),
                pl.BlockSpec((rows, D), const2),
                pl.BlockSpec((1, tokens, HIDE), lambda r, s: (r, 0, 0)),
                up_spec,
                down_spec,
            ],
            out_specs=[
                pl.BlockSpec((tokens, HIDE), lambda r, s: (0, s[0] ^ r)),
                pl.BlockSpec((rows, D), const2),
                pl.BlockSpec((rows, D), const2),
                pl.BlockSpec((1, HIDE), lambda r, s: (0, s[0] ^ r)),
            ],
            scratch_shapes=[pltpu.VMEM((tokens, D), BF)],
        ),
        compiler_params=params(58),
        cost_estimate=cost(0.1),
        name="feed_forward_back",
    )(spot, low_two_next, low_two_other, slope, mlp_all, mlp_all)
    up_far = weight_grad(spot, low_rel, (grad_pre,), (2, 3), None, (), "up_far", 0.1)
    up_got = swap(up_far, y_mask)
    recv = swap(gn_other, pair_mask)
    grad_one, low_one, sums_one = call(
        first_norm_back,
        [
            jax.ShapeDtypeStruct((rows, D), F32),
            jax.ShapeDtypeStruct((rows, D), BF),
            jax.ShapeDtypeStruct((3, D), F32),
        ],
        [grad_two, after(gn_own, up_far), recv, scaled_one, inv_one, vec],
        0, 16, cost(0.1), "first_norm_back",
    )
    low_one_other = swap(low_one, pair_mask)
    grad_qkv, gx_own, gx_other, bias_qkv_grad = call(
        attention_backward,
        [
            jax.ShapeDtypeStruct((tokens, 3 * D // 2), BF),
            jax.ShapeDtypeStruct((rows, D), F32),
            jax.ShapeDtypeStruct((rows, D), F32),
            jax.ShapeDtypeStruct((1, 3 * D // 2), F32),
        ],
        [place, low_one, low_one_other, qkv, *attn_pieces, cos, sin_a, sin_b, mask],
        1, 58, cost(0.1), "attention_backward", [pltpu.VMEM((PAIRS, tokens, GROUP), BF)],
    )
    mixed = pl.pallas_call(
        pack_sums,
        out_shape=jax.ShapeDtypeStruct(grad_heads.shape, F32),
        grid=(1,),
        in_specs=[SMEM_SPEC]
        + [whole(a) for a in (sums_two, sums_one, bias_up_grad, bias_qkv_grad, scalars)]
        + [pl.BlockSpec(memory_space=pl.ANY)],
        out_specs=pl.BlockSpec((2 * QUADS, 16, GROUP), lambda i: (0, all_cols // 16, 0)),
        input_output_aliases={6: 0},
        compiler_params=params(24),
        cost_estimate=cost(0.1),
        name="pack_sums",
    )(spot, sums_two, sums_one, bias_up_grad, bias_qkv_grad, scalars, grad_heads)

    def tail(after_this, halves, blocks, places, adds, name, micros, finish=False):
        return tail_grad(
            spot, both_rel, after(grad_qkv, *after_this), att, low_one, low_one_other,
            halves, blocks, places, adds, name, micros, finish,
        )

    def second(value, *others):
        return (after(value, *others), low_two_other)

    tail_args = (both_rel, grad_qkv, att, low_one, low_one_other)
    tail_a, tail_b = tail_pair(
        *tail_args, (((1, 0), (3, 0)), ((2, 1), (3, 1))), (), "tail_far", 0.1
    )
    a_got = swap(tail_a, x_mask)
    b_got = swap(tail_b, y_mask)

    down_z = weight_grad(
        spot, hidden, second(low_two, tail_b), (0, 2), (1, 3),
        ((down_got, 0, 1, 0, True),), "down_head", 6,
    )
    down_z1 = swap_head(down_z, 1)
    up_near = weight_grad(
        spot, low_rel, (after(grad_pre, down_z),), (1,), None,
        ((up_got, 1, 0, 0, True),), "up_near", 8,
    )
    up_last = swap(up_near, x_mask)
    down_zz = weight_grad(
        spot, hidden, second(low_two, up_near), (0, 2), (2,),
        ((down_got, 0, 1, 0, True), (down_z1, 1, 2, 0, False)), "down_head_near", 5,
    )
    down_z2 = swap_head(down_zz, 2)
    a_near, b_near = tail_pair(
        both_rel, after(grad_qkv, down_zz), att, low_one, low_one_other,
        (((2, 0),), ((1, 1),)), (a_got, b_got), "tail_near", 5,
    )
    a_last = swap(a_near, y_mask)
    b_last = swap(b_near, x_mask)
    up_adds = ((up_got, 0, 0, 0, True), (up_last, 0, 0, 0, True))
    up_z = weight_grad(
        spot, low_rel, (after(grad_pre, b_near),), (0,), (1, 3), up_adds, "up_head", 5
    )
    up_z1 = swap_head(up_z, 1)
    down_y = weight_grad(
        spot, hidden, second(low_two, up_z), (2,), (0,),
        ((down_got, 1, 0, 0, True), (down_z1, 2, 0, 0, False), (down_z2, 1, 0, 0, False)),
        "down_near", 0.1,
    )
    down_last = swap(down_y, y_mask)
    a_adds = ((a_got, 0, 0, True), (a_last, 0, 0, True))
    b_adds = ((b_got, 0, 0, True), (b_last, 0, 0, True))
    tail_z = tail((down_y,), (0, 1), (0,), (1, 3), a_adds + b_adds, "tail_head", 5)
    tail_z1 = swap_head(tail_z, 1)
    up_zz = weight_grad(
        spot, low_rel, (after(grad_pre, tail_z),), (0,), (2,),
        up_adds + ((up_z1, 1, 0, 0, False),), "up_head_near", 4,
    )
    up_z2 = swap_head(up_zz, 2)
    tail_zz = tail(
        (up_zz,), (0, 1), (0,), (2,),
        a_adds + ((tail_z1, 1, 0, False),) + b_adds + ((tail_z1, 1, 1, False),),
        "tail_head_near", 4,
    )
    tail_z2 = swap_head(tail_zz, 2)
    exact = BF if low_span > 1 else F32
    grad_w_down = weight_grad(
        spot, hidden, second(low_two, tail_zz), (0,), (0,),
        (
            (down_got, 0, 0, 0, True), (down_z1, 0, 0, 0, False),
            (down_z2, 0, 0, 0, False), (down_last, 0, 0, 0, False),
        ),
        "down_own", 4, exact,
    )[0]
    up_own = weight_grad(
        spot, low_rel, (after(grad_pre, grad_w_down),), (0,), (0,),
        up_adds + ((up_z1, 0, 0, 0, False), (up_z2, 0, 0, 0, False)), "up_own", 4,
    )[0]
    give, keep, grad_w_out = tail(
        (up_own,), (0, 1), (0,), (0,),
        a_adds + ((tail_z1, 0, 0, False), (tail_z2, 0, 0, False))
        + b_adds + ((tail_z1, 0, 1, False), (tail_z2, 0, 1, False)),
        "tail_own", 4, True,
    )
    grad_w_down = scatter_low(grad_w_down).astype(F32)
    grad_w_up = finish_split(up_own, HIDE)
    grad_w_qkv = joined_columns(keep, swap(give, pair_mask), GROUP)
    grad_w_out = scatter_low(grad_w_out).astype(F32)
    mixed = jnp.repeat(mixed, low_span, axis=0) if low_span > 1 else mixed
    mixed = lax.psum_scatter(
        mixed.reshape(n_dp * (all_cols + 16), GROUP), "dp", scatter_dimension=0, tiled=True
    )
    shard = (head_cols + 16 + 31) // 32 * 32
    sums = jnp.pad(mixed[all_cols:], ((0, shard - head_cols - 16), (0, 0)))
    sums = jnp.broadcast_to(sums, (n_hd,) + sums.shape)
    mixed = jnp.concatenate([mixed[:all_cols].reshape(n_hd, head_cols, GROUP), sums], axis=1)
    mixed = lax.psum_scatter(
        mixed.reshape(n_hd * shard, GROUP), "head", scatter_dimension=0, tiled=True
    )
    head_rows = D // n_dp
    grad_w_heads = lax.dynamic_slice(
        mixed, (0, (dp % low_span) * head_rows), (head_cols, head_rows)
    ).T
    sums = mixed[head_cols : head_cols + 16]
    grad_tokens = grad_one + gx_own + swap(gx_other, pair_mask)

    place_in = (dp % low_span) * n_hd + hd
    mat = lax.dynamic_slice(sums[:9], (0, place_in * wide), (9, wide))
    mid = FF // n_all
    up_sum = lax.dynamic_slice(sums[9:13].reshape(-1), (place_in * mid,), (mid,))
    return (
        outputs,
        sums[13, 0:1],
        grad_tokens,
        grad_w_qkv,
        grad_w_out,
        grad_w_up,
        grad_w_down,
        grad_w_heads,
        mat[:5],
        up_sum,
        mat[5:7],
        mat[7:9],
        sums[14, 0:1],
    )


def solution(mesh):
    return jax.shard_map(
        on_device,
        mesh=mesh,
        in_specs=(
            P(("dp", "head"), None),
            P("dp", "head"),
            P("dp", "head"),
            P("dp", "head"),
            P("dp", "head"),
            P("dp", "head"),
            P(None, ("dp", "head")),
            P(("dp", "head")),
            P(None, ("dp", "head")),
            P(None, ("dp", "head")),
            P(),
            P("dp"),
            P("dp"),
            P("dp"),
        ),
        out_specs=(
            P(("dp", "head"), None),
            P(),
            P(("dp", "head"), None),
            P("dp", "head"),
            P("dp", "head"),
            P("dp", "head"),
            P("dp", "head"),
            P("dp", "head"),
            P(None, ("dp", "head")),
            P(("dp", "head")),
            P(None, ("dp", "head")),
            P(None, ("dp", "head")),
            P(),
        ),
        check_vma=False,
    )
```

```python
import jax
import jax.numpy as jnp
from jax import lax
from jax.experimental import pallas as pl
from jax.experimental.pallas import tpu as pltpu
from jax.sharding import PartitionSpec as P

D = 1024
HEADS = 16
HEAD_DIM = 64
FF = 4096
EMB = 128
EMB_MID = 96
EMB_SMALL = 64
QLEN = 32

EPS_NORM = 1e-05
EPS_UNIT = 1e-06
SHARPNESS = 0.05
ROPE_BASE = 10000.0
MASKED = -1000000000.0
SQRT_HALF = 0.7071067811865476
GAUSS_SCALE = 0.3989422804014327

BF = jnp.bfloat16
F32 = jnp.float32
STARTS = (0, EMB, EMB + EMB_MID)
WIDTHS = (EMB, EMB_MID, EMB_SMALL)
SLOTS = 3
QUADS = 4
GROUP = 128
HIDE = FF // 8


PAIRS = 4
VMEM_SPEC = pl.BlockSpec(memory_space=pltpu.VMEM)
SMEM_SPEC = pl.BlockSpec(memory_space=pltpu.SMEM)


def dot_nn(a, b):
    return lax.dot_general(a, b, (((1,), (0,)), ((), ())), preferred_element_type=F32)


def dot_tn(a, b):
    return lax.dot_general(a, b, (((0,), (0,)), ((), ())), preferred_element_type=F32)


def dot_nt(a, b):
    return lax.dot_general(a, b, (((1,), (1,)), ((), ())), preferred_element_type=F32)


def params(mib):
    return pltpu.CompilerParams(vmem_limit_bytes=mib << 20)


TIME_UNIT = 1150000000


def cost(micros):
    return pl.CostEstimate(flops=int(micros * TIME_UNIT), bytes_accessed=1, transcendentals=0)


def whole(a):
    zeros = (0,) * len(a.shape)
    return pl.BlockSpec(a.shape, lambda i: zeros, pipeline_mode=pl.Buffered(1))


def call(kernel, outs, args, n_smem, mib, estimate, name, scratch=()):
    return pl.pallas_call(
        kernel,
        out_shape=outs,
        grid=(1,),
        in_specs=[SMEM_SPEC] * n_smem + [whole(a) for a in args[n_smem:]],
        out_specs=[whole(a) for a in outs],
        scratch_shapes=list(scratch),
        compiler_params=params(mib),
        cost_estimate=estimate,
        name=name,
    )(*args)


def norm_parts(values):
    centred = values - jnp.mean(values, axis=-1, keepdims=True)
    variance = jnp.mean(centred * centred, axis=-1, keepdims=True)
    inverse = lax.rsqrt(variance + EPS_NORM)
    return centred * inverse, inverse


def norm_back(grad_out, scaled, inverse, gain):
    grad_scaled = grad_out * gain
    return inverse * (
        grad_scaled
        - jnp.mean(grad_scaled, axis=-1, keepdims=True)
        - scaled * jnp.mean(grad_scaled * scaled, axis=-1, keepdims=True)
    )


def pieces_of(a0, ax, ay, b0, by, bx):
    def piece(rq, rz):
        at = rz // 2
        if rz % 2 == 0:
            return [a0.at[at], ax.at[at], ay.at[0, at], ay.at[1, at]][rq]
        return [b0.at[at], bx.at[0, at], by.at[at], bx.at[1, at]][rq]

    return piece


def exit_tile(piece, rq, rz):
    return jnp.concatenate(
        [
            jnp.concatenate([piece(q, rz)[0:128, 384:512], piece(q, rz)[128:256, 384:512]], axis=1)
            for q in (rq, rq + 1)
        ],
        axis=0,
    )


def lanes_at(index, width=GROUP):
    return pl.ds(pl.multiple_of(index * width, width), width)


def turn(x, cos, sin_a, sin_b):
    return x * cos + pltpu.roll(x, 96, 1) * sin_a + pltpu.roll(x, 32, 1) * sin_b


def head_mask(h, shape):
    lane = lax.broadcasted_iota(jnp.int32, shape, 1)
    return (lane < HEAD_DIM) if h == 0 else (lane >= HEAD_DIM)


def stacked(a):
    zero = jnp.zeros_like(a)
    return jnp.concatenate(
        [jnp.where(head_mask(0, a.shape), a, zero), jnp.where(head_mask(1, a.shape), a, zero)],
        axis=0,
    )


def unstacked(a):
    half = a.shape[0] // 2
    top = a[:half]
    return jnp.where(head_mask(0, top.shape), top, a[half:])


def softmax_rows(q, k, mask):
    mask = jnp.concatenate([mask, mask], axis=0)
    s = jnp.where(mask > 0, dot_nt(q, k), MASKED)
    raised = jnp.exp(s - jnp.max(s, axis=-1, keepdims=True))
    return raised * (1.0 / jnp.sum(raised, axis=-1, keepdims=True))


def attention_forward(
    place, x, a0, ax, ay, b0, by, bx, cos, sin_a, sin_b, mask, qkv, att, part, vec
):
    quad, hd, core = place[0], place[1], place[5]
    piece = pieces_of(a0, ax, ay, b0, by, bx)
    rows = cos.shape[0]
    for rq in range(4):
        for c in range(2):
            at = slice(c * GROUP, (c + 1) * GROUP)
            total = piece(rq, 0)[256:272, at].astype(F32)
            for rz in range(1, 4):
                total += piece(rq, rz)[256:272, at].astype(F32)
            vec[:, lanes_at(2 * (quad ^ rq) + c)] = total
    for rz in range(4):
        z = hd ^ rz
        acc = dot_nn(x[0], piece(0, rz)[0:256, 0:384])
        for rq in range(1, 4):
            acc += dot_nn(x[rq], piece(rq, rz)[0:256, 0:384])
        for j in range(3):
            i = 3 * z + j
            scale = jnp.where(i < PAIRS, HEAD_DIM**-0.5, 1.0).astype(F32)
            near = vec[0:8, lanes_at(2 * (i % 4) + core)]
            row = lax.broadcasted_iota(jnp.int32, near.shape, 0)
            bias = jnp.sum(jnp.where(row == i // 4, near, 0.0), axis=0, keepdims=True)
            for b in range(2):
                here = acc[b * rows : (b + 1) * rows, j * GROUP : (j + 1) * GROUP]
                here = here + bias
                turned = turn(here, cos[...], sin_a[...], sin_b[...])
                here = jnp.where(i < 2 * PAIRS, turned, here) * scale
                qkv[b * rows : (b + 1) * rows, lanes_at(i)] = here.astype(BF)

    def one(it, carry):
        b, r = it // PAIRS, it % PAIRS
        i = quad ^ r
        row = pl.ds(pl.multiple_of(b * rows, rows), rows)
        q = qkv[row, pl.ds(pl.multiple_of(i * GROUP, GROUP), GROUP)]
        k = qkv[row, pl.ds(pl.multiple_of((PAIRS + i) * GROUP, GROUP), GROUP)]
        v = qkv[row, pl.ds(pl.multiple_of((2 * PAIRS + i) * GROUP, GROUP), GROUP)]
        probs = softmax_rows(stacked(q), k, mask[b])
        both = dot_nn(probs.astype(BF), v)
        att[r, row, :] = unstacked(both).astype(BF)
        return carry

    lax.fori_loop(0, 2 * PAIRS, one, 0)
    pairs = [jnp.concatenate([att[0], att[1]], axis=1), jnp.concatenate([att[2], att[3]], axis=1)]
    for rz in range(4):
        acc = dot_nn(pairs[0], exit_tile(piece, 0, rz)) + dot_nn(pairs[1], exit_tile(piece, 2, rz))
        part[:, lanes_at(hd ^ rz, 256)] = acc


def attention_backward(
    place, own, other, qkv, a0, ax, ay, b0, by, bx, cos, sin_a, sin_b, mask,
    grad_qkv, gx_own, gx_other, sums, ga,
):
    quad, hd = place[0], place[1]
    piece = pieces_of(a0, ax, ay, b0, by, bx)
    rows = cos.shape[0]
    for rq in (0, 2):
        sums_of = [None, None]
        for rz in range(4):
            w = exit_tile(piece, rq, rz)
            for b, grad in ((0, own), (1, other)):
                term = dot_nt(grad[:, lanes_at(hd ^ rz, 256)], w)
                sums_of[b] = term if sums_of[b] is None else sums_of[b] + term
        for b in range(2):
            at = slice(b * rows, (b + 1) * rows)
            ga[rq, at, :] = sums_of[b][:, 0:GROUP].astype(BF)
            ga[rq + 1, at, :] = sums_of[b][:, GROUP:].astype(BF)

    def one(it, carry):
        b, r = it // PAIRS, it % PAIRS
        i = quad ^ r
        row = pl.ds(pl.multiple_of(b * rows, rows), rows)
        at_q = pl.ds(pl.multiple_of(i * GROUP, GROUP), GROUP)
        at_k = pl.ds(pl.multiple_of((PAIRS + i) * GROUP, GROUP), GROUP)
        at_v = pl.ds(pl.multiple_of((2 * PAIRS + i) * GROUP, GROUP), GROUP)
        q, k, v = qkv[row, at_q], qkv[row, at_k], qkv[row, at_v]
        q_pair, grad_pair = stacked(q), stacked(ga[r, row, :])
        probs = softmax_rows(q_pair, k, mask[b])
        gp = dot_nt(grad_pair, v)
        gs = probs * (gp - jnp.sum(probs * gp, axis=-1, keepdims=True))
        gs = gs.astype(BF)
        gq = unstacked(dot_nn(gs, k))
        gk = dot_tn(gs, q_pair)
        gv = dot_tn(probs.astype(BF), grad_pair)
        c, sa, sb = cos[...], -sin_a[...], -sin_b[...]
        grad_qkv[row, at_q] = turn(gq * (HEAD_DIM**-0.5), c, sa, sb).astype(BF)
        grad_qkv[row, at_k] = turn(gk, c, sa, sb).astype(BF)
        grad_qkv[row, at_v] = gv.astype(BF)
        return carry

    lax.fori_loop(0, 2 * PAIRS, one, 0)
    for rq in range(4):
        at = pl.ds(pl.multiple_of((quad ^ rq) * 256, 256), 256)
        acc = None
        for rz in range(4):
            cols = pl.ds(pl.multiple_of((hd ^ rz) * 384, GROUP), 384)
            term = dot_nt(grad_qkv[:, cols], piece(rq, rz)[0:256, 0:384])
            acc = term if acc is None else acc + term
        gx_own[:, at] = acc[:rows]
        gx_other[:, at] = acc[rows:]
    sums[...] = jnp.sum(grad_qkv[...].astype(F32), axis=0, keepdims=True)


def first_norm(place, x, part, recv, vec, scaled_out, inv_out, low, rel_out):
    rows = scaled_out.shape[0]
    for b in range(2):
        sel = slice(b * rows, (b + 1) * rows)
        swapped = slice((1 - b) * rows, (2 - b) * rows)
        h = x[sel, :].astype(F32) + part[sel, :] + recv[swapped, :] + vec[3:4, :]
        scaled, inverse = norm_parts(h)
        low[sel, :] = (scaled * vec[5:6, :] + vec[7:8, :]).astype(BF)
        if b == 0:
            scaled_out[...] = scaled
            inv_out[...] = inverse
    for q in range(QUADS):
        rel_out[q, :, :] = low[:, lanes_at(place[0] ^ q, 256)]


def feed_forward(place, low, vec, wup, wdown, hidden_out, slope_out, own_out, other_out, kept):
    step = pl.program_id(0)
    rows = own_out.shape[0]

    @pl.when(step < QUADS)
    def _():
        for cb in range(2):
            cols = slice(cb * 256, (cb + 1) * 256)
            w = wup[:, 0, cb * 128 : (cb + 1) * 128, :].reshape(D, 256)
            bias = [
                vec[9 + 2 * cb + k : 10 + 2 * cb + k, lanes_at(2 * (place[0] ^ step) + place[1])]
                for k in range(2)
            ]
            pre = dot_nn(low[...], w) + jnp.concatenate(bias, axis=1)
            gate = 0.5 * (1.0 + lax.erf(pre * SQRT_HALF))
            hidden = (pre * gate).astype(BF)
            hidden_out[0, :, cols] = hidden
            kept[step, :, cols] = hidden
            slope_out[0, :, cols] = (
                gate + pre * jnp.exp(-0.5 * pre * pre) * GAUSS_SCALE
            ).astype(BF)

    @pl.when(step >= QUADS)
    def _():
        acc = dot_nn(kept[0], wdown[place[0], 0, 0])
        for r in range(1, QUADS):
            acc += dot_nn(kept[r], wdown[place[0] ^ r, 0, 0])
        own_out[...] = acc[:rows]
        other_out[...] = acc[rows:]


def feed_forward_back(
    place, own, other, slope, wup, wdown, pre_out, own_out, other_out, sums, both
):
    r = pl.program_id(0)
    rows = own.shape[0]

    @pl.when(r == 0)
    def _():
        both[0:rows, :] = own[...]
        both[rows:, :] = other[...]
        own_out[...] = jnp.zeros_like(own_out)
        other_out[...] = jnp.zeros_like(other_out)

    acc = dot_nt(both[:, 0:256], wdown[0, 0])
    for z in range(1, 4):
        acc += dot_nt(both[:, z * 256 : (z + 1) * 256], wdown[0, z])
    grad = (acc * slope[0].astype(F32)).astype(BF)
    pre_out[...] = grad
    sums[...] = jnp.sum(grad.astype(F32), axis=0, keepdims=True)
    total = None
    for cb in range(2):
        w = wup[:, 0, cb * 128 : (cb + 1) * 128, :].reshape(D, 256)
        term = dot_nt(pre_out[:, cb * 256 : (cb + 1) * 256], w)
        total = term if total is None else total + term
    own_out[...] += total[:rows]
    other_out[...] += total[rows:]


def final_norm(scaled_one, part, recv, vec, windows, out, scaled_out, inv_out, proj):
    h = scaled_one[...] * vec[5:6, :] + vec[7:8, :] + part[...] + recv[...] + vec[4:5, :]
    scaled, inverse = norm_parts(h)
    scaled_out[...] = scaled
    inv_out[...] = inverse
    low = (scaled * vec[6:7, :] + vec[8:9, :]).astype(BF)
    out[...] = low
    proj[...] = dot_nt(windows[...], low).astype(BF)


def soft_maxsim(
    place, temp, lanes, proj_0, proj_1, proj_2, proj_3, windows, out, scaled, inverse_two, vec,
    grad_two, low_two, grad_heads, sums, scalars, gproj, units, shares, similar_low,
):
    hd = place[1]
    rows = out.shape[0]
    projs = (proj_0, proj_1, proj_2, proj_3)
    docs = len(projs) - 1
    row = lax.broadcasted_iota(jnp.int32, (rows, GROUP), 0)
    lane = lax.broadcasted_iota(jnp.int32, (rows, GROUP), 1)
    member = (row // QLEN == lane).astype(F32)
    lens = lanes[0:1, :]
    len_row = jnp.sum(member * lens, axis=1, keepdims=True)
    valid = (row % QLEN).astype(F32) < len_row
    queries = rows // QLEN
    used = lax.broadcasted_iota(jnp.int32, (1, GROUP), 1) < queries
    weight = jnp.where(valid, member, 0.0) / jnp.where(used, lens, 1.0)
    warmth = jnp.exp(jnp.full((1, GROUP), temp[0], F32))
    key = lax.broadcasted_iota(jnp.int32, (rows, rows), 1)
    loss = jnp.zeros((1, GROUP), F32)
    grad_temp = jnp.zeros((1, GROUP), F32)
    for slot in range(SLOTS):
        width = WIDTHS[slot]
        cols = slice(STARTS[slot], STARTS[slot] + width)

        def unit_of(away):
            mapped = projs[away][cols, :].astype(F32)
            inverse = lax.rsqrt(jnp.sum(mapped * mapped, axis=0, keepdims=True) + EPS_UNIT)
            return mapped * inverse, inverse

        for away in range(docs + 1):
            units[0:width, lanes_at(hd ^ away, rows)] = unit_of(away)[0].astype(BF)
        logits = []
        for d in range(docs):
            doc = slice((d + 1) * rows, (d + 2) * rows)
            similar = dot_tn(units[0:width, 0:rows], units[0:width, doc]) * (1.0 / SHARPNESS)
            similar = jnp.where(key < place[2 + d], similar, MASKED)
            top = jnp.max(similar, axis=-1, keepdims=True)
            raised = jnp.exp(similar - top)
            total = jnp.sum(raised, axis=-1, keepdims=True)
            soft = SHARPNESS * (top + jnp.log(total))
            shares[:, d * rows : (d + 1) * rows] = raised * (1.0 / total)
            logits.append(jnp.sum(soft * weight, axis=0, keepdims=True) / warmth)
        top_logit = jnp.maximum(jnp.maximum(logits[0], logits[1]), logits[2])
        exps = [jnp.exp(x - top_logit) for x in logits]
        total = exps[0] + exps[1] + exps[2]
        hits = [(lanes[1:2, :] == float(d)).astype(F32) for d in range(docs)]
        picked = logits[0] * hits[0] + logits[1] * hits[1] + logits[2] * hits[2]
        loss += jnp.where(used, top_logit + jnp.log(total) - picked, 0.0) / queries
        for d in range(docs):
            grad = jnp.where(used, exps[d] / total - hits[d], 0.0) / queries
            grad_temp -= grad * logits[d]
            grad_soft = jnp.sum(weight * (grad / warmth), axis=1, keepdims=True)
            at = slice(d * rows, (d + 1) * rows)
            similar_low[:, at] = (grad_soft * shares[:, at]).astype(BF)

        own = jnp.maximum(hd - 1, 0)
        at = pl.ds(pl.multiple_of(own * rows, rows), rows)
        from_docs = dot_nt(units[0:width, rows:], similar_low[...])
        from_queries = dot_nn(units[0:width, 0:rows], similar_low[:, at])
        grad = jnp.where(hd == 0, from_docs, from_queries)
        unit, inverse = unit_of(0)
        gproj[cols, :] = (
            inverse * (grad - unit * jnp.sum(grad * unit, axis=0, keepdims=True))
        ).astype(BF)

    scalars[0:1, :] = loss
    scalars[1:2, :] = grad_temp
    grad_final = dot_tn(gproj[...], windows[...])
    xhat = scaled[...]
    grad = norm_back(grad_final, xhat, inverse_two[...], vec[6:7, :])
    grad_two[...] = grad
    low_two[...] = grad.astype(BF)
    sums[0:1, :] = jnp.sum(grad_final * xhat, axis=0, keepdims=True)
    sums[1:2, :] = jnp.sum(grad_final, axis=0, keepdims=True)
    sums[2:3, :] = jnp.sum(low_two[...].astype(F32), axis=0, keepdims=True)
    heads = dot_nn(gproj[...], out[...])
    for t in range(2 * QUADS):
        grad_heads[t, 0 : heads.shape[0], :] = heads[:, t * GROUP : (t + 1) * GROUP]


def first_norm_back(grad_two, own, recv, scaled, inverse, vec, grad_one, low_one, sums):
    grad_out = grad_two[...] + own[...] + recv[...]
    xhat = scaled[...]
    grad = norm_back(grad_out, xhat, inverse[...], vec[5:6, :])
    grad_one[...] = grad
    low_one[...] = grad.astype(BF)
    sums[0:1, :] = jnp.sum(grad_out * xhat, axis=0, keepdims=True)
    sums[1:2, :] = jnp.sum(grad_out, axis=0, keepdims=True)
    sums[2:3, :] = jnp.sum(low_one[...].astype(F32), axis=0, keepdims=True)


def weight_grad(spot, lhs, rhs, blocks, places, adds, name, micros, kind=BF):
    tokens, width = lhs.shape[1:]
    whole_cols = places is None
    places = (None,) if whole_cols else places
    count = len(places)
    tile = rhs[0].shape[1] // (1 if whole_cols else 4)
    step = (blocks[1] - blocks[0]) if len(blocks) > 1 else 0
    parts = len(rhs)
    span = tokens // parts
    n_add = len(adds)

    def column(s, place):
        return 0 if place is None else s[2] ^ place

    def kernel(spot_ref, lhs_ref, *refs):
        out = refs[-1]
        for k in range(count):
            total = None
            for p in range(parts):
                term = dot_tn(lhs_ref[0, p * span : (p + 1) * span, :], refs[k * parts + p][...])
                total = term if total is None else total + term
            for add in refs[count * parts + k * n_add : count * parts + (k + 1) * n_add]:
                total += add[0].astype(F32)
            out[k] = total.astype(kind)

    specs = [pl.BlockSpec((1, tokens, width), lambda i, s: (blocks[0] + step * i, 0, 0))]
    for place in places:
        specs += [pl.BlockSpec((span, tile), lambda i, s, c=place: (0, column(s, c)))] * parts
    for k, place in enumerate(places):
        for _, at, per_block, per_place, aligned in adds:
            at += per_place * k
            if aligned:
                index = lambda i, s, at=at, n=per_block, c=place: (at + n * i, 0, column(s, c))
            else:
                index = lambda i, s, at=at, n=per_block: (at + n * i, 0, 0)
            specs.append(pl.BlockSpec((1, width, tile), index))
    return pl.pallas_call(
        kernel,
        out_shape=jax.ShapeDtypeStruct((len(blocks) * count, width, tile), kind),
        grid_spec=pltpu.PrefetchScalarGridSpec(
            num_scalar_prefetch=1,
            grid=(len(blocks),),
            in_specs=specs,
            out_specs=pl.BlockSpec((count, width, tile), lambda i, s: (i, 0, 0)),
        ),
        compiler_params=params(24),
        cost_estimate=cost(micros),
        name=name,
    )(spot, lhs, *(list(rhs) * count), *([add[0] for add in adds] * count))


def tail_grad(spot, x, grad_qkv, att, own, other, halves, blocks, places, adds, name, micros, finish=False):
    tokens = x.shape[1]
    whole_cols = places is None
    places = (None,) if whole_cols else places
    count = len(places)
    heads = 4 if whole_cols else 1
    step = (blocks[1] - blocks[0]) if len(blocks) > 1 else 0
    n_half = len(halves)
    rows = tokens // 2
    n_add = len(adds)
    per = n_add // n_half
    lane_blocks = 1 if whole_cols else n_half

    def column(s, place):
        return 0 if place is None else s[2] ^ place

    def kernel(spot_ref, x_ref, att_ref, *refs):
        out = refs[-1]
        lefts = []
        at_add = count * (1 + 2 * lane_blocks)
        for c in range(count):
            qkv_ref, *pair = refs[c * (1 + 2 * lane_blocks) : (c + 1) * (1 + 2 * lane_blocks)]
            for k, half in enumerate(halves):
                left_all = dot_tn(x_ref[0, :, half * GROUP : (half + 1) * GROUP], qkv_ref[...])
                for z in range(heads):
                    if whole_cols:
                        lanes = slice((2 * z + half) * GROUP, (2 * z + half + 1) * GROUP)
                        up, down = pair[0][:, lanes], pair[1][:, lanes]
                    else:
                        up, down = pair[2 * k][...], pair[2 * k + 1][...]
                    right = dot_tn(att_ref[0, 0:rows, :], up) + dot_tn(att_ref[0, rows:, :], down)
                    left = left_all[:, z * 384 : (z + 1) * 384]
                    first = at_add + c * n_add + k * per
                    lo = z * 512
                    for add in refs[first : first + per]:
                        left += add[0, 0, :, lo : lo + 384].astype(F32)
                        right += add[0, 0, :, lo + 384 : lo + 512].astype(F32)
                    if finish:
                        lefts.append(left)
                        out[:, half * GROUP : (half + 1) * GROUP] = right
                        continue
                    out[c, k, :, lo : lo + 384] = left.astype(BF)
                    out[c, k, :, lo + 384 : lo + 512] = right.astype(BF)
        if finish:
            mine = spot_ref[1] == 0
            refs[-3][...] = jnp.where(mine, lefts[1], lefts[0]).astype(BF)
            refs[-2][...] = jnp.where(mine, lefts[0], lefts[1])

    specs = [
        pl.BlockSpec((1, tokens, 256), lambda i, s: (blocks[0] + step * i, 0, 0)),
        pl.BlockSpec((1, tokens, GROUP), lambda i, s: (blocks[0] + step * i, 0, 0)),
    ]
    inputs = []
    for place in places:
        specs.append(pl.BlockSpec((tokens, 384 * heads), lambda i, s, c=place: (0, column(s, c))))
        inputs.append(grad_qkv)
        for half in halves[:lane_blocks]:
            if whole_cols:
                index = lambda i, s: (0, 0)
            else:
                index = lambda i, s, c=place, half=half: (0, 2 * column(s, c) + half)
            specs += [pl.BlockSpec((rows, D if whole_cols else GROUP), index)] * 2
            inputs += [own, other]
    for place in places:
        for a, at, k, aligned in adds:
            if aligned:
                index = lambda i, s, at=at, k=k, c=place: (at, k, 0, column(s, c))
            else:
                index = lambda i, s, at=at, k=k: (at, k, 0, 0)
            specs.append(pl.BlockSpec((1, 1, GROUP, 512 * heads), index))
            inputs.append(a)
    out_shape = jax.ShapeDtypeStruct((len(blocks) * count, n_half, GROUP, 512 * heads), BF)
    out_spec = pl.BlockSpec((count, n_half, GROUP, 512 * heads), lambda i, s: (i, 0, 0, 0))
    if finish:
        out_shape = [
            jax.ShapeDtypeStruct((GROUP, 384), BF),
            jax.ShapeDtypeStruct((GROUP, 384), F32),
            jax.ShapeDtypeStruct((GROUP, 2 * GROUP), F32),
        ]
        out_spec = [pl.BlockSpec(a.shape, lambda i, s: (0, 0)) for a in out_shape]
    return pl.pallas_call(
        kernel,
        out_shape=out_shape,
        grid_spec=pltpu.PrefetchScalarGridSpec(
            num_scalar_prefetch=1,
            grid=(len(blocks),),
            in_specs=specs,
            out_specs=out_spec,
        ),
        compiler_params=params(24 if whole_cols or finish else 58),
        cost_estimate=cost(micros),
        name=name,
    )(spot, x, att, *inputs)


def tail_pair(x, grad_qkv, att, own, other, jobs, adds, name, micros):
    tokens = x.shape[1]
    rows = tokens // 2

    def kernel(x_ref, qkv_ref, att_ref, own_ref, other_ref, *refs):
        for n, blocks in enumerate(jobs):
            out = refs[len(adds) + n]
            for k, (r, half) in enumerate(blocks):
                left_all = dot_tn(x_ref[r, :, half * GROUP : (half + 1) * GROUP], qkv_ref[...])
                for z in range(4):
                    lanes = slice((2 * z + half) * GROUP, (2 * z + half + 1) * GROUP)
                    right = dot_tn(att_ref[r, 0:rows, :], own_ref[:, lanes])
                    right += dot_tn(att_ref[r, rows:, :], other_ref[:, lanes])
                    left = left_all[:, z * 384 : (z + 1) * 384]
                    lo = z * 512
                    if adds:
                        left += refs[n][0, 0, :, lo : lo + 384].astype(F32)
                        right += refs[n][0, 0, :, lo + 384 : lo + 512].astype(F32)
                    out[k, 0, :, lo : lo + 384] = left.astype(BF)
                    out[k, 0, :, lo + 384 : lo + 512] = right.astype(BF)

    outs = [jax.ShapeDtypeStruct((len(blocks), 1, GROUP, 2048), BF) for blocks in jobs]
    specs = [whole(a) for a in (x, grad_qkv, att, own, other)]
    specs += [pl.BlockSpec((1, 1, GROUP, 2048), lambda i: (1, 0, 0, 0))] * len(adds)
    return pl.pallas_call(
        kernel,
        out_shape=outs,
        grid=(1,),
        in_specs=specs,
        out_specs=[whole(a) for a in outs],
        compiler_params=params(24 if adds else 58),
        cost_estimate=cost(micros),
        name=name,
    )(x, grad_qkv, att, own, other, *adds)


def pack_sums(spot, two, one, up, qkv, scalars, heads, out):
    core, hd = spot[1], spot[2]
    out[...] = jnp.zeros_like(out)
    for i in range(3 * PAIRS):
        out[2 * (i % 4) + core, i // 4 : i // 4 + 1, :] = qkv[0:1, i * GROUP : (i + 1) * GROUP]
    for i in range(4 * QUADS):
        out[2 * (i // 4) + core, 9 + i % 4 : 10 + i % 4, :] = up[
            0:1, i * GROUP : (i + 1) * GROUP
        ]
    once = jnp.where(hd == 0, 1.0, 0.0).astype(F32)
    totals = [jnp.sum(scalars[k : k + 1, :], axis=1, keepdims=True) * once for k in range(2)]
    for t in range(2 * QUADS):
        at = slice(t * GROUP, (t + 1) * GROUP)
        out[t, 3:4, :] = one[2:3, at]
        out[t, 4:5, :] = two[2:3, at]
        out[t, 5:6, :] = one[0:1, at]
        out[t, 6:7, :] = two[0:1, at]
        out[t, 7:8, :] = one[1:2, at]
        out[t, 8:9, :] = two[1:2, at]
        for k in range(2):
            out[t, 13 + k : 14 + k, :] = jnp.broadcast_to(totals[k], (1, GROUP))


def pack_matrices(up, down, heads, out):
    rows = up.shape[0]
    groups = up.shape[1] // 256
    for i in range(groups):
        out[i * rows : (i + 1) * rows, :] = up[:, i * 256 : (i + 1) * 256]
    at = groups * rows
    out[at : at + down.shape[0], :] = down[...]
    at += down.shape[0]
    out[at : at + 64, 0:GROUP] = heads[0:64, :]
    out[at : at + 64, GROUP:] = heads[64:, :]


def make_windows(tiles, windows, wide):
    cols = windows.shape[0] // 4
    for dp in range(2 * QUADS):
        at = slice(dp * GROUP, (dp + 1) * GROUP)
        for z in range(4):
            lo = z * cols
            wide[lo : lo + 64, at] = tiles[dp, z, :, 0:GROUP].astype(F32)
            rest = tiles[dp, z, 0:16, GROUP:].astype(F32)
            wide[lo + 64 : lo + cols, at] = rest[0 : cols - 64, :]
    windows[...] = wide[...].astype(BF)


def on_device(
    layer_entries,
    triple_projection_matrix,
    attention_exit_matrix,
    expand_matrix,
    contract_matrix,
    nested_projector,
    offset_model_width,
    offset_expanded,
    standardize_factor,
    standardize_offset,
    logarithmic_warmth,
    passage_lengths_each,
    question_lengths,
    relevant_passage,
):
    n_dp = lax.axis_size("dp")
    n_hd = lax.axis_size("head")
    n_all = n_dp * n_hd
    dp = lax.axis_index("dp")
    hd = lax.axis_index("head")
    low_span = n_dp // 8
    quad = dp // (2 * low_span)
    core = (dp // low_span) % 2
    pair_mask = low_span
    x_mask = 2 * low_span
    y_mask = 4 * low_span

    def swap(a, dp_mask=0, hd_mask=0):
        pairs = [
            (d * n_hd + h, (d ^ dp_mask) * n_hd + (h ^ hd_mask))
            for d in range(n_dp)
            for h in range(n_hd)
        ]
        return lax.ppermute(a, ("dp", "head"), pairs)

    def after(value, *others):
        return lax.optimization_barrier((value, *others))[0]

    def joined(bit, own, other):
        return jnp.where(
            bit == 0, jnp.concatenate([own, other], 0), jnp.concatenate([other, own], 0)
        )

    def gather_low(a):
        span = 1
        while span < low_span:
            a = joined((dp // span) % 2, a, swap(a, span))
            span *= 2
        return a

    def scatter_low(a):
        span = low_span // 2
        while span >= 1:
            half = a.shape[0] // 2
            bit = (dp // span) % 2
            give = lax.dynamic_slice_in_dim(a, (1 - bit) * half, half, 0)
            keep = lax.dynamic_slice_in_dim(a, bit * half, half, 0)
            a = (keep.astype(F32) + swap(give, span).astype(F32)).astype(BF)
            span //= 2
        return a

    rows = layer_entries.shape[0]
    docs = passage_lengths_each.shape[0]

    wup_low = gather_low(expand_matrix)
    col_blocks = wup_low.shape[1] // 256
    heads_low = gather_low(nested_projector)
    head_cols = heads_low.shape[1]
    heads_low = jnp.pad(heads_low.T, ((0, GROUP - head_cols), (0, 0)))
    wdown_low = gather_low(contract_matrix)
    (packed_mlp,) = call(
        pack_matrices,
        [jax.ShapeDtypeStruct((wup_low.shape[0] * col_blocks + wdown_low.shape[0] + 64, 256), BF)],
        [wup_low, wdown_low, heads_low],
        0, 16, cost(0.1), "pack_matrices",
    )
    if low_span > 1:
        dp_groups = [
            [((q * 2 + k) * low_span + s) for q in range(QUADS) for k in range(2)]
            for s in range(low_span)
        ]
        mlp_all = lax.all_gather(
            lax.all_gather(packed_mlp, "head"), "dp", axis_index_groups=dp_groups
        )
    else:
        mlp_all = lax.all_gather(packed_mlp, ("dp", "head"))
    mlp_all = mlp_all.reshape((8, n_hd) + packed_mlp.shape)

    partner_rows = swap(layer_entries, pair_mask)
    lens_own = jnp.concatenate([passage_lengths_each, question_lengths])
    lens_partner = swap(lens_own, pair_mask)
    both = jnp.concatenate([layer_entries, partner_rows], axis=0)
    order = [quad ^ r for r in range(QUADS)]
    both_rel = jnp.stack(
        [lax.dynamic_slice(both, (0, order[r] * 256), (2 * rows, 256)) for r in range(QUADS)]
    )

    wide = offset_model_width.shape[1]
    mine = (jnp.arange(n_hd) == hd).astype(BF)
    vectors = jnp.concatenate([offset_model_width, standardize_factor, standardize_offset], axis=0)
    n_vec = vectors.shape[0]
    vectors = gather_low(vectors[None]).transpose(1, 0, 2)
    vectors = (vectors[:, :, None, :] * mine[None, None, :, None]).reshape(n_vec, GROUP)
    middle = gather_low(offset_expanded[None])
    middle = (middle[:, None, :] * mine[None, :, None]).reshape(4, GROUP)
    vectors = jnp.concatenate([vectors, middle, jnp.zeros((16 - n_vec - 4, GROUP), BF)], axis=0)

    wqkv_low = gather_low(triple_projection_matrix)
    parts = wqkv_low.reshape(wqkv_low.shape[0], -1, 2, GROUP)
    keep, give = (
        lax.dynamic_index_in_dim(parts, k, 2, False).reshape(wqkv_low.shape[0], -1)
        for k in (core, 1 - core)
    )
    qkv_cols = keep.shape[1]
    k_rows = keep.shape[0]
    other = jnp.pad(vectors, ((0, 0), (0, qkv_cols - GROUP)))
    other = swap(jnp.concatenate([give, other], axis=0), pair_mask)
    wout_low = gather_low(attention_exit_matrix)
    wout_own = jnp.concatenate([wout_low[:, :GROUP], wout_low[:, GROUP:]], axis=0)
    vectors = jnp.where(
        core == 0,
        jnp.concatenate([vectors, other[k_rows:, :GROUP]], axis=1),
        jnp.concatenate([other[k_rows:, :GROUP], vectors], axis=1),
    )
    packed = jnp.concatenate(
        [
            jnp.concatenate([joined(core, keep, other[:k_rows]), wout_own], axis=1),
            jnp.pad(vectors, ((0, 0), (0, qkv_cols + GROUP - 2 * GROUP))),
        ],
        axis=0,
    )[None]

    a0 = jnp.concatenate([packed, swap(packed, 0, 2)], axis=0)
    b0 = swap(a0, 0, 1)
    ax = swap(a0, x_mask)
    by = swap(b0, y_mask)
    ay = swap(jnp.stack([a0, ax]), y_mask)
    bx = swap(jnp.stack([b0, by]), x_mask)
    attn_pieces = (a0, ax, ay, b0, by, bx)
    spot = jnp.stack([quad, core, hd]).astype(jnp.int32)

    row_ids = jnp.arange(rows, dtype=jnp.int32)
    is_query = hd == 0

    def valid_of(lens):
        doc_here = lens[jnp.maximum(hd - 1, 0)]
        return jnp.where(
            is_query, row_ids % QLEN < jnp.repeat(lens[docs:], QLEN), row_ids < doc_here
        )

    valid = jnp.stack([valid_of(lens_own), valid_of(lens_partner)])
    segment = jnp.where(is_query, row_ids // QLEN, 0)
    position = jnp.where(is_query, row_ids % QLEN, row_ids)
    mask = ((segment[:, None] == segment[None, :])[None] & valid[:, None, :]).astype(F32)
    halfway = HEAD_DIM // 2
    powers = jnp.arange(halfway, dtype=F32) * (2.0 / HEAD_DIM)
    angles = position.astype(F32)[:, None] * (ROPE_BASE ** (-powers))[None, :]
    cosine, sine = jnp.cos(angles), jnp.sin(angles)
    none = jnp.zeros_like(sine)
    cos = jnp.concatenate([cosine] * 4, axis=1)
    sin_a = jnp.concatenate([-sine, none] * 2, axis=1)
    sin_b = jnp.concatenate([none, sine] * 2, axis=1)
    place = jnp.concatenate(
        [
            jnp.stack([quad, hd]).astype(jnp.int32),
            passage_lengths_each,
            core.reshape(1).astype(jnp.int32),
        ]
    ).astype(jnp.int32)
    tokens = 2 * rows

    qkv, att, part, vec = call(
        attention_forward,
        [
            jax.ShapeDtypeStruct((tokens, 3 * D // 2), BF),
            jax.ShapeDtypeStruct((PAIRS, tokens, GROUP), BF),
            jax.ShapeDtypeStruct((tokens, D), F32),
            jax.ShapeDtypeStruct((16, D), F32),
        ],
        [place, both_rel, *attn_pieces, cos, sin_a, sin_b, mask],
        1, 58, cost(0.1), "attention_forward",
    )
    recv = swap(part, pair_mask)
    scaled_one, inv_one, low_both, low_rel = call(
        first_norm,
        [
            jax.ShapeDtypeStruct((rows, D), F32),
            jax.ShapeDtypeStruct((rows, 1), F32),
            jax.ShapeDtypeStruct((tokens, D), BF),
            jax.ShapeDtypeStruct((QUADS, tokens, 256), BF),
        ],
        [place, both, part, recv, vec],
        1, 24, cost(1), "first_norm",
    )

    def const2(r, s):
        return (0, 0)

    def hide(r, s):
        return s[0] ^ jnp.minimum(r, QUADS - 1)

    def column(r):
        return jnp.maximum(r - QUADS, 0)

    by_core = mlp_all.reshape((QUADS, 2) + mlp_all.shape[1:])
    up_spec = pl.BlockSpec((8, 1, 256, 256), lambda r, s: (0, s[0] ^ r, s[1], 0))
    down_spec = pl.BlockSpec((1, 4, HIDE, 256), lambda r, s: (2 * (s[0] ^ r) + s[1], 0, 1, 0))
    hidden_spec = pl.BlockSpec(
        (1, tokens, HIDE), lambda r, s: (jnp.minimum(r, QUADS - 1), 0, 0)
    )
    column_spec = pl.BlockSpec((rows, 256), lambda r, s: (0, column(r)))
    hidden, slope, out_own, out_other = pl.pallas_call(
        feed_forward,
        out_shape=[
            jax.ShapeDtypeStruct((QUADS, tokens, HIDE), BF),
            jax.ShapeDtypeStruct((QUADS, tokens, HIDE), BF),
            jax.ShapeDtypeStruct((rows, D), F32),
            jax.ShapeDtypeStruct((rows, D), F32),
        ],
        grid_spec=pltpu.PrefetchScalarGridSpec(
            num_scalar_prefetch=1,
            grid=(2 * QUADS,),
            in_specs=[
                pl.BlockSpec((tokens, D), const2),
                pl.BlockSpec((16, D), const2),
                pl.BlockSpec((8, 1, 256, 256), lambda r, s: (0, hide(r, s), s[1], 0)),
                pl.BlockSpec(
                    (QUADS, 1, 1, HIDE, 256), lambda r, s: (0, s[1], column(r), 1, 0)
                ),
            ],
            out_specs=[hidden_spec, hidden_spec, column_spec, column_spec],
            scratch_shapes=[pltpu.VMEM((QUADS, tokens, HIDE), BF)],
        ),
        compiler_params=params(58),
        cost_estimate=cost(12),
        name="feed_forward",
    )(spot, low_both, vec, mlp_all, by_core)
    all_cols = n_hd * head_cols
    windows = pl.pallas_call(
        make_windows,
        out_shape=jax.ShapeDtypeStruct((all_cols, D), BF),
        grid=(1,),
        in_specs=[pl.BlockSpec((8, 4, 64, 256), lambda i: (0, 0, 16, 0))],
        out_specs=pl.BlockSpec((all_cols, D), lambda i: (0, 0)),
        scratch_shapes=[pltpu.VMEM((all_cols, D), F32)],
        compiler_params=params(58),
        cost_estimate=cost(1),
        name="make_windows",
    )(mlp_all)
    recv = swap(out_other, pair_mask)
    outputs, scaled_two, inv_two, own_proj = call(
        final_norm,
        [
            jax.ShapeDtypeStruct((rows, D), BF),
            jax.ShapeDtypeStruct((rows, D), F32),
            jax.ShapeDtypeStruct((rows, 1), F32),
            jax.ShapeDtypeStruct((all_cols, rows), BF),
        ],
        [scaled_one, out_own, recv, vec, windows],
        0, 16, cost(2.6), "final_norm",
    )
    projs = [own_proj] + [swap(own_proj, 0, k) for k in range(1, n_hd)]
    lanes = jnp.stack(
        [
            jnp.pad(question_lengths.astype(F32), (0, GROUP - question_lengths.shape[0])),
            jnp.pad(relevant_passage.astype(F32), (0, GROUP - relevant_passage.shape[0])),
        ]
    )
    grad_two, low_two, grad_heads, sums_two, scalars = call(
        soft_maxsim,
        [
            jax.ShapeDtypeStruct((rows, D), F32),
            jax.ShapeDtypeStruct((rows, D), BF),
            jax.ShapeDtypeStruct((2 * QUADS, all_cols + 16, GROUP), F32),
            jax.ShapeDtypeStruct((3, D), F32),
            jax.ShapeDtypeStruct((2, GROUP), F32),
        ],
        [place, logarithmic_warmth, lanes, *projs, windows, outputs, scaled_two, inv_two, vec],
        2, 24, cost(4.3), "soft_maxsim", [
            pltpu.VMEM((all_cols, rows), BF),
            pltpu.VMEM((EMB, (docs + 1) * rows), BF),
            pltpu.VMEM((rows, docs * rows), F32),
            pltpu.VMEM((rows, docs * rows), BF),
        ],
    )

    low_two_other = swap(low_two, pair_mask)

    def swap_head(a, mask):
        return swap(a, 0, mask)

    def finish_split(a, group):
        count = a.shape[0] // 2
        give = lax.dynamic_slice_in_dim(a, (1 - core) * count, count, 0)
        keep = lax.dynamic_slice_in_dim(a, core * count, count, 0)
        return joined_columns(keep, swap(give, pair_mask), group)

    def joined_columns(keep, other, group):
        count = keep.shape[0]
        keep = keep.reshape(count, -1, 1, group)
        other = other.reshape(count, -1, 1, group)
        whole = jnp.where(
            core == 0,
            jnp.concatenate([keep, other], axis=2),
            jnp.concatenate([other, keep], axis=2),
        ).reshape(count, -1)
        return scatter_low(whole).astype(F32)

    down_far = weight_grad(
        spot, hidden, (low_two, low_two_other), (1, 3), None, (), "down_far", 0.1
    )
    down_got = swap(down_far, x_mask)
    low_two_next = after(low_two, down_far)
    grad_pre, gn_own, gn_other, bias_up_grad = pl.pallas_call(
        feed_forward_back,
        out_shape=[
            jax.ShapeDtypeStruct((tokens, QUADS * HIDE), BF),
            jax.ShapeDtypeStruct((rows, D), F32),
            jax.ShapeDtypeStruct((rows, D), F32),
            jax.ShapeDtypeStruct((1, QUADS * HIDE), F32),
        ],
        grid_spec=pltpu.PrefetchScalarGridSpec(
            num_scalar_prefetch=1,
            grid=(QUADS,),
            in_specs=[
                pl.BlockSpec((rows, D), const2),
                pl.BlockSpec((rows, D), const2),
                pl.BlockSpec((1, tokens, HIDE), lambda r, s: (r, 0, 0)),
                up_spec,
                down_spec,
            ],
            out_specs=[
                pl.BlockSpec((tokens, HIDE), lambda r, s: (0, s[0] ^ r)),
                pl.BlockSpec((rows, D), const2),
                pl.BlockSpec((rows, D), const2),
                pl.BlockSpec((1, HIDE), lambda r, s: (0, s[0] ^ r)),
            ],
            scratch_shapes=[pltpu.VMEM((tokens, D), BF)],
        ),
        compiler_params=params(58),
        cost_estimate=cost(0.1),
        name="feed_forward_back",
    )(spot, low_two_next, low_two_other, slope, mlp_all, mlp_all)
    up_far = weight_grad(spot, low_rel, (grad_pre,), (2, 3), None, (), "up_far", 0.1)
    up_got = swap(up_far, y_mask)
    recv = swap(gn_other, pair_mask)
    grad_one, low_one, sums_one = call(
        first_norm_back,
        [
            jax.ShapeDtypeStruct((rows, D), F32),
            jax.ShapeDtypeStruct((rows, D), BF),
            jax.ShapeDtypeStruct((3, D), F32),
        ],
        [grad_two, after(gn_own, up_far), recv, scaled_one, inv_one, vec],
        0, 16, cost(0.1), "first_norm_back",
    )
    low_one_other = swap(low_one, pair_mask)
    grad_qkv, gx_own, gx_other, bias_qkv_grad = call(
        attention_backward,
        [
            jax.ShapeDtypeStruct((tokens, 3 * D // 2), BF),
            jax.ShapeDtypeStruct((rows, D), F32),
            jax.ShapeDtypeStruct((rows, D), F32),
            jax.ShapeDtypeStruct((1, 3 * D // 2), F32),
        ],
        [place, low_one, low_one_other, qkv, *attn_pieces, cos, sin_a, sin_b, mask],
        1, 58, cost(0.1), "attention_backward", [pltpu.VMEM((PAIRS, tokens, GROUP), BF)],
    )
    mixed = pl.pallas_call(
        pack_sums,
        out_shape=jax.ShapeDtypeStruct(grad_heads.shape, F32),
        grid=(1,),
        in_specs=[SMEM_SPEC]
        + [whole(a) for a in (sums_two, sums_one, bias_up_grad, bias_qkv_grad, scalars)]
        + [pl.BlockSpec(memory_space=pl.ANY)],
        out_specs=pl.BlockSpec((2 * QUADS, 16, GROUP), lambda i: (0, all_cols // 16, 0)),
        input_output_aliases={6: 0},
        compiler_params=params(24),
        cost_estimate=cost(0.1),
        name="pack_sums",
    )(spot, sums_two, sums_one, bias_up_grad, bias_qkv_grad, scalars, grad_heads)

    def tail(after_this, halves, blocks, places, adds, name, micros, finish=False):
        return tail_grad(
            spot, both_rel, after(grad_qkv, *after_this), att, low_one, low_one_other,
            halves, blocks, places, adds, name, micros, finish,
        )

    def second(value, *others):
        return (after(value, *others), low_two_other)

    tail_args = (both_rel, grad_qkv, att, low_one, low_one_other)
    tail_a, tail_b = tail_pair(
        *tail_args, (((1, 0), (3, 0)), ((2, 1), (3, 1))), (), "tail_far", 0.1
    )
    a_got = swap(tail_a, x_mask)
    b_got = swap(tail_b, y_mask)

    down_z = weight_grad(
        spot, hidden, second(low_two, tail_b), (0, 2), (1, 3),
        ((down_got, 0, 1, 0, True),), "down_head", 6,
    )
    down_z1 = swap_head(down_z, 1)
    up_near = weight_grad(
        spot, low_rel, (after(grad_pre, down_z),), (1,), None,
        ((up_got, 1, 0, 0, True),), "up_near", 8,
    )
    up_last = swap(up_near, x_mask)
    down_zz = weight_grad(
        spot, hidden, second(low_two, up_near), (0, 2), (2,),
        ((down_got, 0, 1, 0, True), (down_z1, 1, 2, 0, False)), "down_head_near", 5,
    )
    down_z2 = swap_head(down_zz, 2)
    a_near, b_near = tail_pair(
        both_rel, after(grad_qkv, down_zz), att, low_one, low_one_other,
        (((2, 0),), ((1, 1),)), (a_got, b_got), "tail_near", 5,
    )
    a_last = swap(a_near, y_mask)
    b_last = swap(b_near, x_mask)
    up_adds = ((up_got, 0, 0, 0, True), (up_last, 0, 0, 0, True))
    up_z = weight_grad(
        spot, low_rel, (after(grad_pre, b_near),), (0,), (1, 3), up_adds, "up_head", 5
    )
    up_z1 = swap_head(up_z, 1)
    down_y = weight_grad(
        spot, hidden, second(low_two, up_z), (2,), (0,),
        ((down_got, 1, 0, 0, True), (down_z1, 2, 0, 0, False), (down_z2, 1, 0, 0, False)),
        "down_near", 0.1,
    )
    down_last = swap(down_y, y_mask)
    a_adds = ((a_got, 0, 0, True), (a_last, 0, 0, True))
    b_adds = ((b_got, 0, 0, True), (b_last, 0, 0, True))
    tail_z = tail((down_y,), (0, 1), (0,), (1, 3), a_adds + b_adds, "tail_head", 5)
    tail_z1 = swap_head(tail_z, 1)
    up_zz = weight_grad(
        spot, low_rel, (after(grad_pre, tail_z),), (0,), (2,),
        up_adds + ((up_z1, 1, 0, 0, False),), "up_head_near", 4,
    )
    up_z2 = swap_head(up_zz, 2)
    tail_zz = tail(
        (up_zz,), (0, 1), (0,), (2,),
        a_adds + ((tail_z1, 1, 0, False),) + b_adds + ((tail_z1, 1, 1, False),),
        "tail_head_near", 4,
    )
    tail_z2 = swap_head(tail_zz, 2)
    exact = BF if low_span > 1 else F32
    grad_w_down = weight_grad(
        spot, hidden, second(low_two, tail_zz), (0,), (0,),
        (
            (down_got, 0, 0, 0, True), (down_z1, 0, 0, 0, False),
            (down_z2, 0, 0, 0, False), (down_last, 0, 0, 0, False),
        ),
        "down_own", 4, exact,
    )[0]
    up_own = weight_grad(
        spot, low_rel, (after(grad_pre, grad_w_down),), (0,), (0,),
        up_adds + ((up_z1, 0, 0, 0, False), (up_z2, 0, 0, 0, False)), "up_own", 4,
    )[0]
    give, keep, grad_w_out = tail(
        (up_own,), (0, 1), (0,), (0,),
        a_adds + ((tail_z1, 0, 0, False), (tail_z2, 0, 0, False))
        + b_adds + ((tail_z1, 0, 1, False), (tail_z2, 0, 1, False)),
        "tail_own", 4, True,
    )
    grad_w_down = scatter_low(grad_w_down).astype(F32)
    grad_w_up = finish_split(up_own, HIDE)
    grad_w_qkv = joined_columns(keep, swap(give, pair_mask), GROUP)
    grad_w_out = scatter_low(grad_w_out).astype(F32)
    mixed = jnp.repeat(mixed, low_span, axis=0) if low_span > 1 else mixed
    mixed = lax.psum_scatter(
        mixed.reshape(n_dp * (all_cols + 16), GROUP), "dp", scatter_dimension=0, tiled=True
    )
    shard = (head_cols + 16 + 31) // 32 * 32
    sums = jnp.pad(mixed[all_cols:], ((0, shard - head_cols - 16), (0, 0)))
    sums = jnp.broadcast_to(sums, (n_hd,) + sums.shape)
    mixed = jnp.concatenate([mixed[:all_cols].reshape(n_hd, head_cols, GROUP), sums], axis=1)
    mixed = lax.psum_scatter(
        mixed.reshape(n_hd * shard, GROUP), "head", scatter_dimension=0, tiled=True
    )
    head_rows = D // n_dp
    grad_w_heads = lax.dynamic_slice(
        mixed, (0, (dp % low_span) * head_rows), (head_cols, head_rows)
    ).T
    sums = mixed[head_cols : head_cols + 16]
    grad_tokens = grad_one + gx_own + swap(gx_other, pair_mask)

    place_in = (dp % low_span) * n_hd + hd
    mat = lax.dynamic_slice(sums[:9], (0, place_in * wide), (9, wide))
    mid = FF // n_all
    up_sum = lax.dynamic_slice(sums[9:13].reshape(-1), (place_in * mid,), (mid,))
    return (
        outputs,
        sums[13, 0:1],
        grad_tokens,
        grad_w_qkv,
        grad_w_out,
        grad_w_up,
        grad_w_down,
        grad_w_heads,
        mat[:5],
        up_sum,
        mat[5:7],
        mat[7:9],
        sums[14, 0:1],
    )


def solution(mesh):
    return jax.shard_map(
        on_device,
        mesh=mesh,
        in_specs=(
            P(("dp", "head"), None),
            P("dp", "head"),
            P("dp", "head"),
            P("dp", "head"),
            P("dp", "head"),
            P("dp", "head"),
            P(None, ("dp", "head")),
            P(("dp", "head")),
            P(None, ("dp", "head")),
            P(None, ("dp", "head")),
            P(),
            P("dp"),
            P("dp"),
            P("dp"),
        ),
        out_specs=(
            P(("dp", "head"), None),
            P(),
            P(("dp", "head"), None),
            P("dp", "head"),
            P("dp", "head"),
            P("dp", "head"),
            P("dp", "head"),
            P("dp", "head"),
            P(None, ("dp", "head")),
            P(("dp", "head")),
            P(None, ("dp", "head")),
            P(None, ("dp", "head")),
            P(),
        ),
        check_vma=False,
    )
```
